32 devices in a mesh: dp: 4 (over x, core), seq: 8 (over z, y).
Axes of the slice: x: 2, y: 2, z: 4, core: 2. Of those that a mesh axis runs over, the one named last changes fastest.
Arguments:
- tokens: bfloat16 [4, 4096, 1024], P('dp', 'seq'), may hold values from -6 to 6
- cotangent: bfloat16 [4, 4096, 1024], P('dp', 'seq'), may hold values from -6 to 6
- norm1_gain: float32 [1024], replicated, may hold values from 0.5 to 1.5
- norm1_bias: float32 [1024], replicated, may hold values from -1.25 to 1.25
- in_weight: bfloat16 [1024, 3072], replicated, may hold values from -0.1875 to 0.1875
- in_bias: float32 [3072], replicated, may hold values from -1.25 to 1.25
- short_weight: float32 [3, 3, 1024], P(None, None, 'seq'), may hold values from -3.5 to 3.5
- short_bias: float32 [3, 1024], P(None, 'seq'), may hold values from -1.25 to 1.25
- filter_in: float32 [33, 64], replicated, may hold values from -2 to 2
- filter_in_bias: float32 [64], replicated, may hold values from -3 to 3
- sine_freq: float32 [64], replicated, may hold values from 0.5 to 2
- filter_out: float32 [64, 1024], P(None, 'seq'), may hold values from -0.03125 to 0.03125
- decay_rates: float32 [1024], P('seq'), may hold values from 2 to 64
- filter_bias: float32 [1024], P('seq'), may hold values from -6 to 6
- out_weight: bfloat16 [1024, 1024], replicated, may hold values from -0.1875 to 0.1875
- out_bias: float32 [1024], replicated, may hold values from -1.25 to 1.25
- norm2_gain: float32 [1024], replicated, may hold values from 0.5 to 1.5
- norm2_bias: float32 [1024], replicated, may hold values from -1.25 to 1.25
- up_weight: bfloat16 [1024, 4096], replicated, may hold values from -0.1875 to 0.1875
- up_bias: float32 [4096], replicated, may hold values from -1.25 to 1.25
- down_weight: bfloat16 [4096, 1024], replicated, may hold values from -0.125 to 0.125
- down_bias: float32 [1024], replicated, may hold values from -1.25 to 1.25
Outputs:
- block_output: bfloat16 [4, 4096, 1024], P('dp', 'seq')
- grad_tokens: float32 [4, 4096, 1024], P('dp', 'seq')
- grad_norm1_gain: float32 [1024], replicated
- grad_norm1_bias: float32 [1024], replicated
- grad_in_weight: float32 [1024, 3072], P('seq', 'dp')
- grad_in_bias: float32 [3072], replicated
- grad_short_weight: float32 [3, 3, 1024], P(None, None, 'seq')
- grad_short_bias: float32 [3, 1024], P(None, 'seq')
- grad_filter_in: float32 [33, 64], replicated
- grad_filter_in_bias: float32 [64], replicated
- grad_sine_freq: float32 [64], replicated
- grad_filter_out: float32 [64, 1024], P(None, 'seq')
- grad_filter_bias: float32 [1024], P('seq')
- grad_out_weight: float32 [1024, 1024], P('seq', 'dp')
- grad_out_bias: float32 [1024], replicated
- grad_norm2_gain: float32 [1024], replicated
- grad_norm2_bias: float32 [1024], replicated
- grad_up_weight: float32 [1024, 4096], P('seq', 'dp')
- grad_up_bias: float32 [4096], replicated
- grad_down_weight: float32 [4096, 1024], P('seq', 'dp')
- grad_down_bias: float32 [1024], replicated
The draws below stay inside these ranges and needn't reach their ends.
All inputs are finite; a program needn't handle non-finite values.
Results may differ from the reference program's by a relative error of at most 0.014.
Values may be sent and summed in bfloat16 or wider, within the bound.
No kernel may reach another device: no remote copies, remote signals or barrier semaphores. Data moves between devices by JAX's collectives and lax.ppermute only.
A program may use at most 320 MiB of HBM per device.

```python
import math
import jax
import jax.numpy as jnp
from jax import lax

D = 1024
FF = 4096
FH = 64
EMB = 33
SEQLEN = 4096
SEQS = 4


def steps_of(rng, extent, split, least, top_value):
    gain, own = 1.0, jax.random.fold_in(rng, 6)
    for position, blocks in split:
        steps = jnp.exp(jax.random.uniform(jax.random.fold_in(own, position), (blocks,), jnp.float32, least / len(split), top_value / len(split)))
        gain = gain * jnp.repeat(steps, extent[position] // blocks).reshape([-1 if axis == position else 1 for axis in range(len(extent))])
    return gain


def normal_values(stream_key, extent, scale, bound, pieces=(), kind=jnp.bfloat16):
    values = scale * jax.random.normal(stream_key, extent, jnp.float32)
    if pieces:
        values = values * steps_of(stream_key, extent, pieces, -0.22, 0.18)
    return jnp.clip(values, -bound, bound).astype(kind)


def setup_inputs(seed: int = 0) -> dict:
    arg_keys = jax.random.split(jax.random.key(seed), 23)
    return {
        "tokens": normal_values(arg_keys[0], (SEQS, SEQLEN, D), 1.0, 6.0, ((0, 4), (1, 8))),
        "cotangent": normal_values(arg_keys[1], (SEQS, SEQLEN, D), 1.0, 6.0, ((0, 4), (1, 8))),
        "norm1_gain": jnp.clip(1.0 + 0.1 * jax.random.normal(arg_keys[2], (D,), jnp.float32), 0.5, 1.5),
        "norm1_bias": normal_values(arg_keys[3], (D,), 0.2, 1.25, (), jnp.float32),
        "in_weight": normal_values(arg_keys[4], (D, 3 * D), D ** -0.5, 0.1875),
        "in_bias": normal_values(arg_keys[5], (3 * D,), 0.2, 1.25, (), jnp.float32),
        "short_weight": normal_values(arg_keys[6], (3, 3, D), 3 ** -0.5, 3.5, ((2, 8),), jnp.float32),
        "short_bias": normal_values(arg_keys[7], (3, D), 0.2, 1.25, ((1, 8),), jnp.float32),
        "filter_in": normal_values(arg_keys[8], (EMB, FH), (EMB // 4) ** -0.5, 2.0, (), jnp.float32),
        "filter_in_bias": normal_values(arg_keys[9], (FH,), 0.5, 3.0, (), jnp.float32),
        "sine_freq": jnp.clip(jax.random.uniform(arg_keys[10], (FH,), jnp.float32, 0.5, 2.0), 0.5, 2.0),
        "filter_out": normal_values(arg_keys[11], (FH, D), (FH * SEQLEN // 8) ** -0.5, 0.03125, ((1, 8),), jnp.float32),
        "decay_rates": jnp.clip(jnp.exp(math.log(64.0) - 3.465736 * jax.random.uniform(arg_keys[12], (D,), jnp.float32) ** steps_of(arg_keys[12], (D,), ((0, 8),), -0.2, 0.2)), 2.0, 64.0),
        "filter_bias": normal_values(arg_keys[13], (D,), 1.0, 6.0, ((0, 8),), jnp.float32),
        "out_weight": normal_values(arg_keys[14], (D, D), D ** -0.5, 0.1875),
        "out_bias": normal_values(arg_keys[15], (D,), 0.2, 1.25, (), jnp.float32),
        "norm2_gain": jnp.clip(1.0 + 0.1 * jax.random.normal(arg_keys[16], (D,), jnp.float32), 0.5, 1.5),
        "norm2_bias": normal_values(arg_keys[17], (D,), 0.2, 1.25, (), jnp.float32),
        "up_weight": normal_values(arg_keys[18], (D, FF), D ** -0.5, 0.1875),
        "up_bias": normal_values(arg_keys[19], (FF,), 0.2, 1.25, (), jnp.float32),
        "down_weight": normal_values(arg_keys[20], (FF, D), (FF // 2) ** -0.5, 0.125),
        "down_bias": normal_values(arg_keys[21], (D,), 0.2, 1.25, (), jnp.float32),
    }


HIGH = lax.Precision.HIGHEST
EPSILON = 1e-05

@jax.custom_vjp
def low(v):
    return lax.optimization_barrier(v.astype(jnp.bfloat16)).astype(jnp.float32)

@jax.custom_vjp
def low_back(v):
    return v

def low_keep(v):
    return (low(v), None)

def low_pass(kept, grad):
    return (grad,)

def back_keep(v):
    return (v, None)

def back_low(kept, grad):
    return (low(grad),)
low.defvjp(low_keep, low_pass)
low_back.defvjp(back_keep, back_low)

def layer_norm(values, scale_vec, shift_vec):
    average = lax.optimization_barrier(jnp.mean(values, axis=-1, keepdims=True))
    centred = values - average
    variance = lax.optimization_barrier(jnp.mean(centred * centred, axis=-1, keepdims=True))
    return centred * lax.rsqrt(variance + EPSILON) * scale_vec + shift_vec

def position_features(length):
    steps = jnp.arange(length, dtype=jnp.float32)
    scaled = steps / (length - 1)
    angles = 2.0 * math.pi * steps / length
    bands = (EMB - 1) // 2
    freqs = 0.0001 + jnp.arange(bands, dtype=jnp.float32) * (bands - 1 - 0.0001) / (bands - 1)
    phase = freqs[:, None] * angles[None, :]
    return jnp.concatenate([scaled[None, :], jnp.cos(phase), -jnp.sin(phase)], axis=0)

def make_filter(filter_in, in_shift, sine_freq, filter_out, decay_rates, features):
    hidden_pre = jnp.dot(filter_in.T, features, precision=HIGH) + in_shift[:, None]
    hidden = jnp.sin(sine_freq[:, None] * hidden_pre)
    raw_kernel = jnp.dot(filter_out.T, hidden, precision=HIGH)
    return raw_kernel * jnp.exp(-decay_rates[:, None] * features[0][None, :])

def mixer_reference(received, short_taps, tap_shift, filter_in, in_shift, sine_freq, filter_out, filter_shift, decay_rates, features):
    length = received.shape[2]
    shifted_one = jnp.pad(received, ((0, 0), (0, 0), (1, 0)))[:, :, :length]
    shifted_two = jnp.pad(received, ((0, 0), (0, 0), (2, 0)))[:, :, :length]
    short = tap_shift[:, :, None] + short_taps[0][:, :, None] * shifted_two + short_taps[1][:, :, None] * shifted_one + short_taps[2][:, :, None] * received
    gate_out, gate_in, values = (short[0], short[1], short[2])
    kernel = make_filter(filter_in, in_shift, sine_freq, filter_out, decay_rates, features)
    inner = values * gate_in
    spectrum = jnp.fft.rfft(inner, n=2 * length, axis=-1) * jnp.fft.rfft(kernel, n=2 * length, axis=-1)
    conv = jnp.fft.irfft(spectrum, n=2 * length, axis=-1)[:, :length] + inner * filter_shift[:, None]
    return conv * gate_out

def block_forward(seq_tokens, weights, decay_rates, features):
    norm1_gain, norm1_bias, in_weight, in_bias, short_weight, short_bias, filter_in, filter_in_bias, sine_freq, filter_out, filter_bias, out_weight, out_bias, norm2_gain, norm2_bias, up_weight, up_bias, down_weight, down_bias = weights
    length = seq_tokens.shape[0]
    normed = low(layer_norm(seq_tokens, norm1_gain, norm1_bias))
    projected = low(low_back(jnp.dot(normed, in_weight, precision=HIGH) + in_bias))
    received = projected.T.reshape(3, D, length)
    mixed = low(low_back(mixer_reference(received, short_weight, short_bias, filter_in, filter_in_bias, sine_freq, filter_out, filter_bias, decay_rates, features)))
    attended = low_back(jnp.dot(mixed.T, out_weight, precision=HIGH) + out_bias)
    resid = seq_tokens + attended
    normed2 = low(layer_norm(resid, norm2_gain, norm2_bias))
    up_pre = low_back(jnp.dot(normed2, up_weight, precision=HIGH) + up_bias)
    activated = low(jax.nn.gelu(up_pre))
    return resid + jnp.dot(activated, down_weight, precision=HIGH) + down_bias

def reference(tokens, cotangent, norm1_gain, norm1_bias, in_weight, in_bias, short_weight, short_bias, filter_in, filter_in_bias, sine_freq, filter_out, decay_rates, filter_bias, out_weight, out_bias, norm2_gain, norm2_bias, up_weight, up_bias, down_weight, down_bias):
    features = position_features(SEQLEN)
    weights = tuple((item.astype(jnp.float32) for item in (norm1_gain, norm1_bias, in_weight, in_bias, short_weight, short_bias, filter_in, filter_in_bias, sine_freq, filter_out, filter_bias, out_weight, out_bias, norm2_gain, norm2_bias, up_weight, up_bias, down_weight, down_bias)))
    decay = decay_rates.astype(jnp.float32)

    def forward(seq_tokens, params):
        return block_forward(seq_tokens, params, decay, features)

    def one_sequence(totals, pair):
        seq_tokens, seq_cotangent = pair
        result, pull = jax.vjp(forward, seq_tokens, weights)
        grad_seq, grad_params = pull(seq_cotangent)
        totals = jax.tree.map(lambda left, right: left + right, totals, grad_params)
        return (totals, (result, grad_seq))
    zeros = jax.tree.map(jnp.zeros_like, weights)
    totals, outputs = lax.scan(one_sequence, zeros, (tokens.astype(jnp.float32), cotangent.astype(jnp.float32)))
    results, grads = outputs
    return (results.astype(jnp.bfloat16), grads, totals[0], totals[1], totals[2], totals[3], totals[4], totals[5], totals[6], totals[7], totals[8], totals[9], totals[10], totals[11], totals[12], totals[13], totals[14], totals[15], totals[16], totals[17], totals[18])
```

```python
import functools
import math

import jax
import jax.numpy as jnp
import numpy as np
from jax import lax
from jax.experimental import pallas as pl
from jax.experimental.pallas import tpu as pltpu
from jax.sharding import PartitionSpec as P

EMB = 33
HIGH = lax.Precision.HIGHEST
EPSILON = 1e-05
BLOCK = 128
ROWS = 16
F32 = jnp.float32
BF16 = jnp.bfloat16


def times_root(re, im, num, den):
    num = num % den
    if num == 0:
        return re, im
    if 4 * num == den:
        return -im, re
    if 2 * num == den:
        return -re, -im
    if 4 * num == 3 * den:
        return im, -re
    angle = 2.0 * math.pi * num / den
    cos, sin = math.cos(angle), math.sin(angle)
    if abs(abs(cos) - abs(sin)) < 1e-12:
        sc, ss = (1.0 if cos > 0 else -1.0), (1.0 if sin > 0 else -1.0)
        root = abs(cos)
        return root * (sc * re - ss * im), root * (sc * im + ss * re)
    return re * cos - im * sin, im * cos + re * sin


def small_fft(re, im, sign):
    count = len(re)
    if count == 1:
        return re, im
    if count == 2:
        return [re[0] + re[1], re[0] - re[1]], [im[0] + im[1], im[0] - im[1]]
    even_re, even_im = small_fft(re[0::2], im[0::2], sign)
    odd_re, odd_im = small_fft(re[1::2], im[1::2], sign)
    low_re, low_im, top_re, top_im = [], [], [], []
    for k in range(count // 2):
        tr, ti = times_root(odd_re[k], odd_im[k], sign * k, count)
        low_re.append(even_re[k] + tr)
        low_im.append(even_im[k] + ti)
        top_re.append(even_re[k] - tr)
        top_im.append(even_im[k] - ti)
    return low_re + top_re, low_im + top_im


def blocks_forward(source, target, count):
    def body(step, carry):
        row = pl.multiple_of(step * ROWS, ROWS)
        re, im = [], []
        for a in range(count):
            value = source[a, pl.ds(row, ROWS), :].astype(F32)
            angle = 2.0 * math.pi * a / (4 * count)
            re.append(value * math.cos(angle))
            im.append(value * math.sin(angle))
        re, im = small_fft(re, im, -1)
        for k in range(count):
            target[k, pl.ds(row, ROWS), :] = re[k].astype(BF16)
            target[k, pl.ds(BLOCK + row, ROWS), :] = im[k].astype(BF16)
        return carry

    lax.fori_loop(0, BLOCK // ROWS, body, 0)


def blocks_inverse(source, emit, count):
    def body(step, carry):
        row = pl.multiple_of(step * ROWS, ROWS)
        re = [source[k, pl.ds(row, ROWS), :] for k in range(count)]
        im = [source[k, pl.ds(BLOCK + row, ROWS), :] for k in range(count)]
        re, im = small_fft(re, im, 1)
        for a in range(count):
            angle = 2.0 * math.pi * a / (4 * count)
            emit(a, row, re[a] * math.cos(angle) + im[a] * math.sin(angle))
        return carry

    lax.fori_loop(0, BLOCK // ROWS, body, 0)


def mxu(left, right):
    return jnp.dot(left, right, preferred_element_type=F32)


def table_kernel(alpha_cos, alpha_sin, beta_cos, beta_sin, forward, inverse, *, scale):
    ca, sa = alpha_cos[0], alpha_sin[0]
    cb, sb = beta_cos[...], beta_sin[...]
    cos = ca * cb - sa * sb
    sin = sa * cb + ca * sb
    forward[0, :BLOCK, :BLOCK] = cos.astype(BF16)
    forward[0, :BLOCK, BLOCK:] = sin.astype(BF16)
    forward[0, BLOCK:, :BLOCK] = (-sin).astype(BF16)
    forward[0, BLOCK:, BLOCK:] = cos.astype(BF16)
    cos, sin = cos.T * scale, sin.T * scale
    inverse[0, :BLOCK, :BLOCK] = cos.astype(BF16)
    inverse[0, :BLOCK, BLOCK:] = (-sin).astype(BF16)
    inverse[0, BLOCK:, :BLOCK] = sin.astype(BF16)
    inverse[0, BLOCK:, BLOCK:] = cos.astype(BF16)


def make_tables(length):
    count = length // BLOCK
    alpha = 2.0 * np.pi * np.arange(BLOCK)[None, :] * (np.arange(count)[:, None] - 0.25) / length
    beta = 2.0 * np.pi * ((np.arange(BLOCK)[:, None] * np.arange(BLOCK)[None, :]) % BLOCK) / BLOCK
    alpha = alpha[:, None, :]
    const = lambda v: jnp.asarray(v, F32)
    row = pl.BlockSpec((1, 1, BLOCK), lambda i: (i, 0, 0))
    flat = pl.BlockSpec((BLOCK, BLOCK), lambda i: (0, 0))
    out = pl.BlockSpec((1, 2 * BLOCK, 2 * BLOCK), lambda i: (i, 0, 0))
    shape = jax.ShapeDtypeStruct((count, 2 * BLOCK, 2 * BLOCK), BF16)
    return pl.pallas_call(
        functools.partial(table_kernel, scale=1.0 / length),
        grid=(count,),
        in_specs=[row, row, flat, flat],
        out_specs=[out, out],
        out_shape=[shape, shape],
        name="tables",
    )(const(np.cos(alpha)), const(np.sin(alpha)), const(np.cos(beta)), const(np.sin(beta)))


def split_spec(value):
    return value[:BLOCK], value[BLOCK:]


def spectrum_kernel(signal, forward, spectrum, mid):
    count = signal.shape[0]
    blocks_forward(signal, mid, count)

    def body(k, carry):
        spectrum[k] = mxu(forward[k], mid[k]).astype(BF16)
        return carry

    lax.fori_loop(0, count, body, 0, unroll=4)


def conv_kernel(signal, kernel_spec, bias, forward, inverse, result, spectrum, mid, back, *, conjugate):
    count = signal.shape[0]
    blocks_forward(signal, mid, count)

    def body(k, carry):
        spec = mxu(forward[k], mid[k])
        spectrum[k] = spec.astype(BF16)
        a_re, a_im = split_spec(spec)
        b_re, b_im = split_spec(kernel_spec[k].astype(F32))
        if conjugate:
            b_im = -b_im
        product = jnp.concatenate([a_re * b_re - a_im * b_im, a_re * b_im + a_im * b_re], axis=0)
        back[k] = mxu(inverse[k], product.astype(BF16))
        return carry

    lax.fori_loop(0, count, body, 0, unroll=4)
    gain = bias[...]

    def emit(a, row, value):
        direct = signal[a, pl.ds(row, ROWS), :].astype(F32) * gain
        result[a, pl.ds(row, ROWS), :] = (value + direct).astype(result.dtype)

    blocks_inverse(back, emit, count)


def kernel_grad_kernel(grad_spec, signal_spec, grad, signal, inverse, result, bias_grad, back):
    count = grad_spec.shape[0]

    def body(k, carry):
        a_re, a_im = split_spec(grad_spec[k].astype(F32))
        b_re, b_im = split_spec(signal_spec[k].astype(F32))
        product = jnp.concatenate([a_re * b_re + a_im * b_im, a_im * b_re - a_re * b_im], axis=0)
        back[k] = mxu(inverse[k], product.astype(BF16))
        return carry

    lax.fori_loop(0, count, body, 0, unroll=4)

    def emit(a, row, value):
        result[a, pl.ds(row, ROWS), :] = value

    blocks_inverse(back, emit, count)

    def total(a, acc):
        prod = grad[a].astype(F32) * signal[a].astype(F32)
        return acc + jnp.sum(prod.reshape(BLOCK // 8, 8, prod.shape[-1]), axis=0)

    acc = lax.fori_loop(0, count, total, jnp.zeros((8, grad.shape[-1]), F32))
    bias_grad[...] = jnp.sum(acc, axis=0, keepdims=True)


VMEM_SPEC = pl.BlockSpec(memory_space=pltpu.VMEM)
BIG = pltpu.CompilerParams(vmem_limit_bytes=48 << 20)


def vmem_call(kernel, outs, scratch, args, name):
    return pl.pallas_call(
        kernel,
        in_specs=[VMEM_SPEC] * len(args),
        out_specs=[VMEM_SPEC] * len(outs),
        out_shape=outs,
        scratch_shapes=scratch,
        compiler_params=BIG,
        name=name,
    )(*args)


class FastMixer:
    def __init__(self, length, channels):
        self.count = length // BLOCK
        self.channels = channels
        self.forward, self.inverse = make_tables(length)
        self.mid = pltpu.VMEM((self.count, 2 * BLOCK, channels), BF16)
        self.back = pltpu.VMEM((self.count, 2 * BLOCK, channels), F32)
        self.spec = jax.ShapeDtypeStruct((self.count, 2 * BLOCK, channels), BF16)

    def blocked(self, value):
        return value.reshape(self.count, BLOCK, self.channels)

    def spectrum(self, signal):
        return vmem_call(
            spectrum_kernel, [self.spec], [self.mid], (self.blocked(signal), self.forward), "spectrum"
        )[0]

    def convolve(self, signal, kernel_spec, bias, conjugate):
        out = jax.ShapeDtypeStruct((self.count, BLOCK, self.channels), BF16)
        result, spectrum = vmem_call(
            functools.partial(conv_kernel, conjugate=conjugate),
            [out, self.spec],
            [self.mid, self.back],
            (self.blocked(signal), kernel_spec, bias[None, :], self.forward, self.inverse),
            "correlate" if conjugate else "convolve",
        )
        return result.reshape(signal.shape), spectrum

    def kernel_grad(self, grad_spec, signal_spec, grad, signal):
        outs = [
            jax.ShapeDtypeStruct((self.count, BLOCK, self.channels), F32),
            jax.ShapeDtypeStruct((1, self.channels), F32),
        ]
        result, bias_grad = vmem_call(
            kernel_grad_kernel,
            outs,
            [self.back],
            (grad_spec, signal_spec, self.blocked(grad), self.blocked(signal), self.inverse),
            "kernel_grad",
        )
        return result.reshape(grad.shape), bias_grad[0]


class PlainMixer:
    def __init__(self, length, channels):
        self.length = length
        self.channels = channels
        full = 2 * length
        p = 2
        while p * p * 2 <= full and full % (p * 2) == 0:
            p = p * 2
        q = full // p
        self.p, self.q = p, q
        ip, iq = jnp.arange(p, dtype=jnp.int32), jnp.arange(q, dtype=jnp.int32)
        tp = 2.0 * math.pi * (ip[:, None] * ip[None, :] % p).astype(F32) / p
        tq = 2.0 * math.pi * (iq[:, None] * iq[None, :] % q).astype(F32) / q
        tt = 2.0 * math.pi * (ip[:, None] * iq[None, :] % full).astype(F32) / full
        self.cp, self.sp, self.cq, self.sq = jnp.cos(tp), jnp.sin(tp), jnp.cos(tq), jnp.sin(tq)
        self.ct, self.st = jnp.cos(tt), jnp.sin(tt)

    def spectrum(self, signal):
        half = self.p // 2
        x = signal.astype(F32).T.reshape(self.channels, half, self.q)
        ein = functools.partial(jnp.einsum, precision=HIGH)
        re = ein("kn,cnq->ckq", self.cp[:, :half], x)
        im = -ein("kn,cnq->ckq", self.sp[:, :half], x)
        re, im = re * self.ct + im * self.st, im * self.ct - re * self.st
        return (
            ein("ckn,nm->ckm", re, self.cq) + ein("ckn,nm->ckm", im, self.sq),
            ein("ckn,nm->ckm", im, self.cq) - ein("ckn,nm->ckm", re, self.sq),
        )

    def back(self, re, im):
        half = self.p // 2
        ein = functools.partial(jnp.einsum, precision=HIGH)
        br = ein("ckm,nm->ckn", re, self.cq) - ein("ckm,nm->ckn", im, self.sq)
        bi = ein("ckm,nm->ckn", im, self.cq) + ein("ckm,nm->ckn", re, self.sq)
        br, bi = br * self.ct - bi * self.st, bi * self.ct + br * self.st
        out = ein("nk,ckq->cnq", self.cp[:half], br) - ein("nk,ckq->cnq", self.sp[:half], bi)
        return (out.reshape(self.channels, self.length) / (2 * self.length)).T

    def convolve(self, signal, kernel_spec, bias, conjugate):
        a_re, a_im = self.spectrum(signal)
        b_re, b_im = kernel_spec
        if conjugate:
            b_im = -b_im
        out = self.back(a_re * b_re - a_im * b_im, a_re * b_im + a_im * b_re)
        out = out + signal.astype(F32) * bias[None, :]
        return out.astype(BF16), (a_re, a_im)

    def kernel_grad(self, grad_spec, signal_spec, grad, signal):
        a_re, a_im = grad_spec
        b_re, b_im = signal_spec
        out = self.back(a_re * b_re + a_im * b_im, a_im * b_re - a_re * b_im)
        return out, jnp.sum(grad.astype(F32) * signal.astype(F32), axis=0)


def position_features(length):
    steps = jnp.arange(length, dtype=F32)
    scaled = steps / (length - 1)
    angles = 2.0 * math.pi * steps / length
    bands = (EMB - 1) // 2
    freqs = 0.0001 + jnp.arange(bands, dtype=F32) * (bands - 1 - 0.0001) / (bands - 1)
    phase = freqs[:, None] * angles[None, :]
    return jnp.concatenate([scaled[None, :], jnp.cos(phase), -jnp.sin(phase)], axis=0)


def swap(value, axis, bit):
    size = lax.axis_size(axis)
    return lax.ppermute(value, axis, [(i, i ^ bit) for i in range(size)])


def pick(value, index, axis):
    return lax.dynamic_index_in_dim(value, index, axis, keepdims=False)


def add(left, right):
    return left.astype(F32) + right.astype(F32)


def seq_stages(block, first_bit):
    seq = lax.axis_size("seq")
    me = lax.axis_index("seq")
    bit = first_bit
    while bit < seq:
        count, rows, cols = block.shape
        pairs = block.reshape(count // 2, 2, rows, cols)
        mine = (me // bit) % 2
        got = swap(pick(pairs, 1 - mine, 1).astype(BF16), "seq", bit)
        block = add(pick(pairs, mine, 1), got)
        bit *= 2
    return block[0]


def scatter_start(left, right, start, width, stride, y_first):
    seq = lax.axis_size("seq")
    dp_me = lax.axis_index("dp")
    mine = lax.axis_index("seq") % 2
    height = left.shape[1] // seq

    def columns(which):
        offset = start + jnp.bitwise_xor(dp_me, which) * stride
        return lax.dynamic_slice_in_dim(right, offset, width, 1)

    def partial(which):
        part = jnp.concatenate([columns(w) for w in which], axis=1)
        return matmul("ta,tb->ab", left, part)

    got = swap(partial((3, 1)).astype(BF16), "dp", 1)
    if y_first:
        both = (partial((2, 0)) + got.astype(F32)).astype(BF16)
        pairs = both.reshape(seq // 2, 2, height, 2 * width)
        return pick(pairs, 1 - mine, 1), pick(pairs, mine, 1)
    send = (partial((2,)) + got[:, :width].astype(F32)).astype(BF16)
    own = (partial((0,)) + got[:, width:].astype(F32)).astype(BF16)
    return send.reshape(seq, height, width), own.reshape(seq, height, width)


def scatter_middle(send, kept, y_first):
    if y_first:
        width = kept.shape[-1] // 2
        got = swap(send, "seq", 1)
        far = add(kept[..., :width], got[..., :width]).astype(BF16)
        return far, add(kept[..., width:], got[..., width:]).astype(BF16)
    got = swap(send, "dp", 2)
    count, height, width = kept.shape
    mine = lax.axis_index("seq") % 2
    kept, got = (v.reshape(count // 2, 2, height, width) for v in (kept, got))
    out = add(pick(kept, 1 - mine, 1), pick(got, 1 - mine, 1)).astype(BF16)
    return out, add(pick(kept, mine, 1), pick(got, mine, 1)).astype(BF16)


def scatter_finish(send, kept, y_first):
    got = swap(send, "dp", 2) if y_first else swap(send, "seq", 1)
    return seq_stages(add(kept, got), 2)


def pack(parts):
    flat = jnp.concatenate([p.reshape(-1) for p in parts])
    short = -flat.shape[0] % 1024
    return jnp.pad(flat, (0, short)).reshape(-1, 128)


def unpack(packed, like):
    flat = packed.reshape(-1)
    out, place = [], 0
    for p in like:
        out.append(flat[place : place + p.size].reshape(p.shape))
        place += p.size
    return out


def sum_all(value, axis):
    bit = 1
    while bit < lax.axis_size(axis):
        value = value + swap(value, axis, bit)
        bit *= 2
    return value


def matmul(spec, left, right):
    return jnp.einsum(spec, left, right, preferred_element_type=F32)


def normalise(value):
    centred = value - jnp.mean(value, axis=-1, keepdims=True)
    scale = lax.rsqrt(jnp.mean(centred * centred, axis=-1, keepdims=True) + EPSILON)
    return centred * scale, scale


def norm_back(grad, normal, scale, gain):
    e = grad * gain
    mean_e = jnp.mean(e, axis=-1, keepdims=True)
    mean_en = jnp.mean(e * normal, axis=-1, keepdims=True)
    return (e - mean_e - normal * mean_en) * scale


def on_device(
    tokens,
    cotangent,
    norm1_gain,
    norm1_bias,
    in_weight,
    in_bias,
    short_weight,
    short_bias,
    filter_in,
    filter_in_bias,
    sine_freq,
    filter_out,
    decay_rates,
    filter_bias,
    out_weight,
    out_bias,
    norm2_gain,
    norm2_bias,
    up_weight,
    up_bias,
    down_weight,
    down_bias,
):
    width = in_weight.shape[0]
    ff = up_weight.shape[1]
    rows = tokens.shape[1]
    seq = lax.axis_size("seq")
    me = lax.axis_index("seq")
    length = rows * seq
    chans = width // seq
    halo = 8
    up_shift = [(i, i + 1) for i in range(seq - 1)]
    down_shift = [(i + 1, i) for i in range(seq - 1)]

    mine = jnp.concatenate([short_weight.reshape(9, chans), short_bias], axis=0)
    all_taps = lax.all_to_all(
        jnp.broadcast_to(mine[None], (seq, 12, chans)), "seq", split_axis=0, concat_axis=0, tiled=True
    )
    all_taps = all_taps.reshape(seq, 12, chans).transpose(1, 0, 2).reshape(12, width)
    taps, tap_shift = all_taps[:9].reshape(3, 3, width), all_taps[9:]

    mixer = (FastMixer if length // BLOCK <= 64 else PlainMixer)(length, chans)
    features = position_features(length)
    hidden_pre = jnp.dot(filter_in.T, features, precision=HIGH) + filter_in_bias[:, None]
    phase = sine_freq[:, None] * hidden_pre
    hidden = jnp.sin(phase)
    window = jnp.exp(-features[0][:, None] * decay_rates[None, :])
    kernel = jnp.einsum("hn,hc->nc", hidden, filter_out, precision=HIGH) * window
    kernel_spec = mixer.spectrum(kernel)

    x = tokens[0]
    before = lax.ppermute(x[rows - halo :], "seq", up_shift)
    x32 = x.astype(F32)
    ext = jnp.concatenate([before.astype(F32), x32], axis=0)
    normal1_ext, scale1_ext = normalise(ext)
    normed_ext = (normal1_ext * norm1_gain + norm1_bias).astype(BF16)
    normal1, scale1 = normal1_ext[halo:], scale1_ext[halo:]
    normed = normed_ext[halo:]
    proj = (matmul("td,dn->tn", normed_ext, in_weight) + in_bias).astype(BF16)
    live = (me > 0) | (jnp.arange(rows + halo)[:, None] >= halo)
    proj = jnp.where(live, proj, 0).astype(F32)

    def lagged(k, j):
        part = proj[:, k * width : (k + 1) * width]
        return part[halo - 2 + j : halo - 2 + j + rows]

    short = [
        tap_shift[k] + sum(taps[j, k] * lagged(k, j) for j in range(3)) for k in range(3)
    ]
    gate_out, gate_in, values = short
    inner = (values * gate_in).astype(BF16)

    def to_channels(value):
        blocks = value.reshape(rows, seq, chans).transpose(1, 0, 2)
        got = lax.all_to_all(blocks, "seq", split_axis=0, concat_axis=0, tiled=True)
        return got.reshape(length, chans)

    def to_tokens(value):
        blocks = value.reshape(seq, rows, chans)
        got = lax.all_to_all(blocks, "seq", split_axis=0, concat_axis=0, tiled=True)
        return got.transpose(1, 0, 2).reshape(rows, width)

    inner_chan = to_channels(inner)
    conv_chan, inner_spec = mixer.convolve(inner_chan, kernel_spec, filter_bias, False)
    conv = to_tokens(conv_chan).astype(F32)

    mixed = (conv * gate_out).astype(BF16)
    resid = x32 + matmul("tc,ce->te", mixed, out_weight) + out_bias
    normal2, scale2 = normalise(resid)
    normed2 = (normal2 * norm2_gain + norm2_bias).astype(BF16)
    up_pre = matmul("td,df->tf", normed2, up_weight) + up_bias
    activated, gelu_pull = jax.vjp(jax.nn.gelu, up_pre)
    activated = activated.astype(BF16)
    block_out = resid + matmul("tf,fd->td", activated, down_weight) + down_bias
    dy = cotangent[0]
    dy32 = dy.astype(F32)
    grad_activated = matmul("td,fd->tf", dy, down_weight)
    grad_up_pre = gelu_pull(grad_activated)[0].astype(BF16)
    down_start = scatter_start(activated, dy, 0, width // 4, width // 4, False)
    d2 = matmul("tf,df->td", grad_up_pre, up_weight)
    up_start = scatter_start(normed2, grad_up_pre, 0, ff // 4, ff // 4, True)
    grad_resid = dy32 + norm_back(d2, normal2, scale2, norm2_gain)
    grad_attn = grad_resid.astype(BF16)
    out_start = scatter_start(mixed, grad_attn, 0, width // 4, width // 4, False)
    grad_mixed = matmul("te,ce->tc", grad_attn, out_weight)
    grad_conv = (grad_mixed * gate_out).astype(BF16)
    grad_gate_out = grad_mixed * conv

    grad_chan = to_channels(grad_conv)
    grad_chan, down_start, up_start, out_start = lax.optimization_barrier(
        (grad_chan, down_start, up_start, out_start)
    )
    down_mid = scatter_middle(*down_start, False)
    up_mid = scatter_middle(*up_start, True)
    out_mid = scatter_middle(*out_start, False)
    grad_inner_chan, grad_spec = mixer.convolve(grad_chan, kernel_spec, filter_bias, True)
    grad_inner = to_tokens(grad_inner_chan)
    grad_inner, down_mid, up_mid, out_mid = lax.optimization_barrier(
        (grad_inner, down_mid, up_mid, out_mid)
    )
    grad_inner = grad_inner.astype(F32)
    grad_down = scatter_finish(*down_mid, False)
    grad_up = scatter_finish(*up_mid, True)
    grad_out_weight = scatter_finish(*out_mid, False)

    grad_kernel, grad_filter_bias = mixer.kernel_grad(grad_spec, inner_spec, grad_chan, inner_chan)
    grad_raw = grad_kernel * window
    grad_filter_out = jnp.einsum("hn,nc->hc", hidden, grad_raw, precision=HIGH)
    grad_phase = jnp.einsum("nc,hc->hn", grad_raw, filter_out, precision=HIGH) * jnp.cos(phase)
    grad_freq = jnp.sum(grad_phase * hidden_pre, axis=1)
    grad_hidden_pre = grad_phase * sine_freq[:, None]
    grad_filter_in = jnp.einsum("en,hn->eh", features, grad_hidden_pre, precision=HIGH)
    grad_filter_in_bias = jnp.sum(grad_hidden_pre, axis=1)

    grad_short = [grad_gate_out, grad_inner * values, grad_inner * gate_in]
    edge = jnp.stack([g[:halo] for g in grad_short]).astype(BF16)
    after = lax.ppermute(edge, "seq", down_shift).astype(F32)
    grad_proj = []
    grad_taps = []
    for k in range(3):
        longer = jnp.concatenate([grad_short[k], after[k]], axis=0)
        grad_proj.append(sum(taps[j, k] * longer[2 - j : 2 - j + rows] for j in range(3)))
        grad_taps.append(jnp.stack([jnp.sum(grad_short[k] * lagged(k, j), axis=0) for j in range(3)]))
    grad_proj = jnp.concatenate(grad_proj, axis=1).astype(BF16)
    grad_taps = jnp.stack(grad_taps, axis=1)
    grad_tap_shift = jnp.stack([jnp.sum(g, axis=0) for g in grad_short])
    part, half = 3 * width // 4, 3 * width // 8
    in_start = [scatter_start(normed, grad_proj, i * half, half, part, bool(i)) for i in range(2)]
    grad_in_bias = jnp.sum(grad_proj.astype(F32), axis=0)
    d1 = matmul("tn,dn->td", grad_proj, in_weight)
    grad_tokens = grad_resid + norm_back(d1, normal1, scale1, norm1_gain)

    shared = (
        jnp.sum(d1 * normal1, axis=0),
        jnp.sum(d1, axis=0),
        grad_in_bias,
        jnp.sum(grad_attn.astype(F32), axis=0),
        jnp.sum(d2 * normal2, axis=0),
        jnp.sum(d2, axis=0),
        jnp.sum(grad_up_pre.astype(F32), axis=0),
        jnp.sum(dy32, axis=0),
        grad_filter_in,
        grad_filter_in_bias,
        grad_freq,
        grad_taps,
        grad_tap_shift,
    )
    channel = (grad_filter_out, grad_filter_bias)
    packed = pack(shared)
    rows_shared = packed.shape[0]
    packed, in_start = lax.optimization_barrier((packed, in_start))
    in_mid = [scatter_middle(*in_start[i], bool(i)) for i in range(2)]
    grad_in = jnp.concatenate([scatter_finish(*in_mid[i], bool(i)) for i in range(2)], axis=1)
    packed = sum_all(jnp.concatenate([packed, pack(channel)], axis=0), "dp")
    channel = unpack(packed[rows_shared:], channel)
    shared = unpack(sum_all(packed[:rows_shared], "seq"), shared)
    own_taps = lax.dynamic_slice_in_dim(shared[11], me * chans, chans, 2)
    own_shift = lax.dynamic_slice_in_dim(shared[12], me * chans, chans, 1)
    return (
        block_out.astype(BF16)[None],
        grad_tokens[None],
        shared[0],
        shared[1],
        grad_in,
        shared[2],
        own_taps,
        own_shift,
        shared[8],
        shared[9],
        shared[10],
        channel[0],
        channel[1],
        grad_out_weight,
        shared[3],
        shared[4],
        shared[5],
        grad_up,
        shared[6],
        grad_down,
        shared[7],
    )


def solution(mesh):
    everywhere, by_token, by_rows = P(), P("dp", "seq", None), P("seq", "dp")
    taps, shift, chan = P(None, None, "seq"), P(None, "seq"), P("seq")
    in_specs = (by_token,) * 2 + (everywhere,) * 4 + (taps, shift) + (everywhere,) * 3
    in_specs += (shift, chan, chan) + (everywhere,) * 8
    out_specs = (by_token, by_token, everywhere, everywhere, by_rows, everywhere, taps, shift)
    out_specs += (everywhere,) * 3 + (shift, chan, by_rows) + (everywhere,) * 3
    out_specs += (by_rows, everywhere, by_rows, everywhere)
    return jax.shard_map(
        on_device, mesh=mesh, in_specs=in_specs, out_specs=out_specs, check_vma=False
    )
```

```python
import functools
import math

import jax
import jax.numpy as jnp
import numpy as np
from jax import lax
from jax.experimental import pallas as pl
from jax.experimental.pallas import tpu as pltpu
from jax.sharding import PartitionSpec as P

EMB = 33
HIGH = lax.Precision.HIGHEST
EPSILON = 1e-05
BLOCK = 128
LANES = 128
ROWS = 16
CHUNK = 64
GRANT = 60 << 20
COST = 8
F32 = jnp.float32
BF16 = jnp.bfloat16


def times_root(re, im, num, den):
    num = num % den
    if num == 0:
        return re, im
    if 4 * num == den:
        return -im, re
    if 2 * num == den:
        return -re, -im
    if 4 * num == 3 * den:
        return im, -re
    angle = 2.0 * math.pi * num / den
    cos, sin = math.cos(angle), math.sin(angle)
    if abs(abs(cos) - abs(sin)) < 1e-12:
        sc, ss = (1.0 if cos > 0 else -1.0), (1.0 if sin > 0 else -1.0)
        root = abs(cos)
        return root * (sc * re - ss * im), root * (sc * im + ss * re)
    return re * cos - im * sin, im * cos + re * sin


def small_fft(re, im, sign):
    count = len(re)
    if count == 1:
        return re, im
    if count == 2:
        return [re[0] + re[1], re[0] - re[1]], [im[0] + im[1], im[0] - im[1]]
    even_re, even_im = small_fft(re[0::2], im[0::2], sign)
    odd_re, odd_im = small_fft(re[1::2], im[1::2], sign)
    low_re, low_im, top_re, top_im = [], [], [], []
    for k in range(count // 2):
        tr, ti = times_root(odd_re[k], odd_im[k], sign * k, count)
        low_re.append(even_re[k] + tr)
        low_im.append(even_im[k] + ti)
        top_re.append(even_re[k] - tr)
        top_im.append(even_im[k] - ti)
    return low_re + top_re, low_im + top_im


def blocks_forward(source, target, count):
    def body(step, carry):
        row = pl.multiple_of(step * ROWS, ROWS)
        re, im = [], []
        for a in range(count):
            value = source[a, pl.ds(row, ROWS), :].astype(F32)
            angle = 2.0 * math.pi * a / (4 * count)
            re.append(value * math.cos(angle))
            im.append(value * math.sin(angle))
        re, im = small_fft(re, im, -1)
        for k in range(count):
            target[k, pl.ds(row, ROWS), :] = re[k].astype(BF16)
            target[k, pl.ds(BLOCK + row, ROWS), :] = im[k].astype(BF16)
        return carry

    lax.fori_loop(0, BLOCK // ROWS, body, 0)


def blocks_inverse(source, emit, count):
    def body(step, carry):
        row = pl.multiple_of(step * ROWS, ROWS)
        re = [source[k, pl.ds(row, ROWS), :] for k in range(count)]
        im = [source[k, pl.ds(BLOCK + row, ROWS), :] for k in range(count)]
        re, im = small_fft(re, im, 1)
        for a in range(count):
            angle = 2.0 * math.pi * a / (4 * count)
            emit(a, row, re[a] * math.cos(angle) + im[a] * math.sin(angle))
        return carry

    lax.fori_loop(0, BLOCK // ROWS, body, 0)


def cost(flops, bytes_accessed):
    return pl.CostEstimate(flops=flops // COST, bytes_accessed=bytes_accessed // COST, transcendentals=0)


def mxu(left, right):
    return jnp.dot(left, right, preferred_element_type=F32)

def mxu_nt(left, right):
    return lax.dot_general(left, right, (((1,), (1,)), ((), ())), preferred_element_type=F32)

def mxu_tn(left, right):
    return lax.dot_general(left, right, (((0,), (0,)), ((), ())), preferred_element_type=F32)

def rows_loop(total, chunk, body, unroll=1):
    def step(i, carry):
        return body(pl.ds(pl.multiple_of(i * chunk, chunk), chunk), carry)
    return lambda init: lax.fori_loop(0, total // chunk, step, init, unroll=unroll)

def fold8(v):
    return jnp.sum(v.reshape(v.shape[0] // 8, 8, v.shape[1]), axis=0)


def table_kernel(alpha_cos, alpha_sin, beta_cos, beta_sin, forward, inverse, *, scale):
    cb, sb = beta_cos[...], beta_sin[...]
    for i in range(forward.shape[0]):
        ca, sa = alpha_cos[i], alpha_sin[i]
        cos = ca * cb - sa * sb
        sin = sa * cb + ca * sb
        low_cos, low_sin = cos.astype(BF16), sin.astype(BF16)
        forward[i, :BLOCK, :BLOCK] = low_cos
        forward[i, :BLOCK, BLOCK:] = low_sin
        forward[i, BLOCK:, :BLOCK] = -low_sin
        forward[i, BLOCK:, BLOCK:] = low_cos
        low_cos, low_sin = (cos.T * scale).astype(BF16), (sin.T * scale).astype(BF16)
        inverse[i, :BLOCK, :BLOCK] = low_cos
        inverse[i, :BLOCK, BLOCK:] = -low_sin
        inverse[i, BLOCK:, :BLOCK] = low_sin
        inverse[i, BLOCK:, BLOCK:] = low_cos


def make_tables(length):
    count = length // BLOCK
    alpha = 2.0 * np.pi * np.arange(BLOCK)[None, :] * (np.arange(count)[:, None] - 0.25) / length
    beta = 2.0 * np.pi * ((np.arange(BLOCK)[:, None] * np.arange(BLOCK)[None, :]) % BLOCK) / BLOCK
    alpha = alpha[:, None, :]
    consts = [jnp.asarray(f(v), F32) for v in (alpha, beta) for f in (np.cos, np.sin)]
    each = math.gcd(count, 4)
    row = pl.BlockSpec((each, 1, BLOCK), lambda i: (i, 0, 0))
    flat = pl.BlockSpec((BLOCK, BLOCK), lambda i: (0, 0))
    out = pl.BlockSpec((each, 2 * BLOCK, 2 * BLOCK), lambda i: (i, 0, 0))
    shape = jax.ShapeDtypeStruct((count, 2 * BLOCK, 2 * BLOCK), BF16)
    return pl.pallas_call(
        functools.partial(table_kernel, scale=1.0 / length),
        grid=(count // each,),
        in_specs=[row, row, flat, flat],
        out_specs=[out, out],
        out_shape=[shape, shape],
        cost_estimate=cost(16 * count * BLOCK * BLOCK, 8 << 20),
        name="tables",
    )(*consts)


def split_spec(value):
    return value[:BLOCK], value[BLOCK:]


def turn_back(prod, inverse, back):
    def body(k, carry):
        back[k] = mxu(inverse[k], prod[k])
        return carry

    lax.fori_loop(0, prod.shape[0], body, 0, unroll=8)


def spectrum_kernel(signal, forward, spectrum, mid):
    (signal, have_signal), (forward, have_forward) = signal, forward
    count = signal.shape[0]
    have_signal()
    blocks_forward(signal, mid, count)
    have_forward()

    def body(k, carry):
        spectrum[k] = mxu(forward[k], mid[k]).astype(BF16)
        return carry

    lax.fori_loop(0, count, body, 0, unroll=8)


def conv_kernel(signal, kernel_spec, bias, forward, inverse, result, spectrum, mid, prod, back, *, conjugate):
    (signal, have_signal), (kernel_spec, have_spec), (bias, have_bias) = signal, kernel_spec, bias
    (forward, have_forward), (inverse, have_inverse) = forward, inverse
    count = signal.shape[0]
    have_signal()
    blocks_forward(signal, mid, count)
    have_spec()
    have_bias()
    have_forward()

    def body(k, carry):
        spec = mxu(forward[k], mid[k])
        spectrum[k] = spec.astype(BF16)
        a_re, a_im = split_spec(spec)
        b_re, b_im = split_spec(kernel_spec[k].astype(F32))
        if conjugate:
            b_im = -b_im
        prod[k, :BLOCK, :] = (a_re * b_re - a_im * b_im).astype(BF16)
        prod[k, BLOCK:, :] = (a_re * b_im + a_im * b_re).astype(BF16)
        return carry

    lax.fori_loop(0, count, body, 0, unroll=8)
    have_inverse()
    turn_back(prod, inverse, back)
    gain = bias[...]
    devices, rows, _ = result.shape
    per = count // devices
    size = per * BLOCK

    def emit(a, row, value):
        direct = signal[a, pl.ds(row, ROWS), :].astype(F32) * gain
        result[a // per, pl.ds((a % per) * BLOCK + row, ROWS), :] = (value + direct).astype(result.dtype)

    blocks_inverse(back, emit, count)
    if rows > size:
        for j in range(devices - 1):
            result[j, size:, :] = result[j + 1, : rows - size, :]
        result[devices - 1, size:, :] = jnp.zeros((rows - size, result.shape[2]), result.dtype)


def filter_grad_kernel(
    grad_spec, signal_spec, grad, signal, inverse, window, hidden, slope, hidden_pre, features, filter_out,
    out_grad, in_grad, sums, bias_grad, prod, back, raw,
):
    (grad_spec, have_grad_spec), (signal_spec, have_signal_spec) = grad_spec, signal_spec
    count = grad_spec.shape[0]
    have_grad_spec()
    have_signal_spec()

    def body(k, carry):
        a_re, a_im = split_spec(grad_spec[k].astype(F32))
        b_re, b_im = split_spec(signal_spec[k].astype(F32))
        prod[k, :BLOCK, :] = (a_re * b_re + a_im * b_im).astype(BF16)
        prod[k, BLOCK:, :] = (a_im * b_re - a_re * b_im).astype(BF16)
        return carry

    lax.fori_loop(0, count, body, 0, unroll=2)
    for _, wait in (grad, signal, inverse, window, hidden, slope, hidden_pre, features, filter_out):
        wait()
    grad, signal, inverse, window, hidden, slope, hidden_pre, features, filter_out = (
        v[0] for v in (grad, signal, inverse, window, hidden, slope, hidden_pre, features, filter_out)
    )
    turn_back(prod, inverse, back)

    def emit(a, row, value):
        at = pl.ds(a * BLOCK + row, ROWS)
        raw[at, :] = (value * window[at, :]).astype(BF16)

    blocks_inverse(back, emit, count)

    def total(a, acc):
        return acc + fold8(grad[a].astype(F32) * signal[a].astype(F32))

    acc = lax.fori_loop(0, count, total, jnp.zeros((8, grad.shape[-1]), F32))
    bias_grad[...] = jnp.sum(acc, axis=0, keepdims=True)
    out_grad[...] = mxu(hidden[...], raw[...])
    turned = mxu_nt(filter_out[...], raw[...]) * slope[...]
    sums[...] = jnp.concatenate(
        [jnp.sum(turned * hidden_pre[...], axis=1, keepdims=True), jnp.sum(turned, axis=1, keepdims=True)], axis=1
    )
    in_grad[...] = mxu_nt(features[...], turned.astype(BF16))


def vmem_call(kernel, outs, scratch, args, name):
    count = len(args)

    def body(*refs):
        ins, rest = refs[:count], refs[count:]
        results, local = rest[: len(outs)], rest[len(outs) : len(outs) + len(scratch)]
        bufs, sems = rest[len(outs) + len(scratch) : -1], rest[-1]
        copies = [pltpu.make_async_copy(src, dst, sems.at[i]) for i, (src, dst) in enumerate(zip(ins, bufs))]
        for copy in copies:
            copy.start()
        kernel(*[(buf, copy.wait) for buf, copy in zip(bufs, copies)], *results, *local)

    scratch = list(scratch)
    held = [pltpu.VMEM(a.shape, a.dtype) for a in args]
    return pl.pallas_call(
        body,
        in_specs=[pl.BlockSpec(memory_space=pl.ANY)] * count,
        out_specs=[pl.BlockSpec(o.shape, lambda n=len(o.shape): (0,) * n) for o in outs],
        out_shape=outs,
        scratch_shapes=scratch + held + [pltpu.SemaphoreType.DMA((count,))],
        cost_estimate=cost(4 << 30, 16 << 20),
        compiler_params=pltpu.CompilerParams(vmem_limit_bytes=GRANT),
        name=name,
    )(*args)


class FastMixer:
    def __init__(self, length, channels, devices, tables):
        self.count = length // BLOCK
        self.channels = channels
        self.devices = devices
        self.forward, self.inverse = tables
        self.mid = pltpu.VMEM((self.count, 2 * BLOCK, channels), BF16)
        self.back = pltpu.VMEM((self.count, 2 * BLOCK, channels), F32)
        self.spec = jax.ShapeDtypeStruct((self.count, 2 * BLOCK, channels), BF16)

    def blocked(self, value):
        return value.reshape(self.count, BLOCK, self.channels)

    def spectrum(self, signal):
        args = (self.blocked(signal), self.forward)
        return vmem_call(spectrum_kernel, [self.spec], [self.mid], args, "spectrum")[0]

    def convolve(self, signal, kernel_spec, bias, conjugate, extra):
        rows = self.count * BLOCK // self.devices + extra
        out = jax.ShapeDtypeStruct((self.devices, rows, self.channels), BF16)
        return vmem_call(
            functools.partial(conv_kernel, conjugate=conjugate),
            [out, self.spec],
            [self.mid, self.mid, self.back],
            (self.blocked(signal), kernel_spec, bias[None, :], self.forward, self.inverse),
            "correlate" if conjugate else "convolve",
        )

    def filter_grad(self, grad_spec, signal_spec, grad, signal, filt):
        features, hidden_pre, phase, hidden, window, filter_out = filt
        units = hidden.shape[0]
        outs = [
            jax.ShapeDtypeStruct((units, self.channels), F32),
            jax.ShapeDtypeStruct((48, units), F32),
            jax.ShapeDtypeStruct((units, 2), F32),
            jax.ShapeDtypeStruct((1, self.channels), F32),
        ]
        padded = jnp.pad(features.astype(BF16), ((0, 48 - EMB), (0, 0)))
        raw = pltpu.VMEM((self.count * BLOCK, self.channels), BF16)
        out_grad, in_grad, sums, bias_grad = vmem_call(
            filter_grad_kernel,
            outs,
            [self.mid, self.back, raw],
            (grad_spec, signal_spec, self.blocked(grad), self.blocked(signal), self.inverse, window)
            + (hidden.astype(BF16), jnp.cos(phase), hidden_pre, padded, filter_out.astype(BF16)),
            "filter_grad",
        )
        return out_grad, in_grad[:EMB], sums.T, bias_grad[0]


class PlainMixer:
    def __init__(self, length, channels, devices, tables):
        self.length = length
        self.devices = devices
        self.channels = channels
        full = 2 * length
        p = 2
        while p * p * 2 <= full and full % (p * 2) == 0:
            p = p * 2
        q = full // p
        self.p, self.q = p, q
        ip, iq = jnp.arange(p, dtype=jnp.int32), jnp.arange(q, dtype=jnp.int32)
        tp = 2.0 * math.pi * (ip[:, None] * ip[None, :] % p).astype(F32) / p
        tq = 2.0 * math.pi * (iq[:, None] * iq[None, :] % q).astype(F32) / q
        tt = 2.0 * math.pi * (ip[:, None] * iq[None, :] % full).astype(F32) / full
        self.cp, self.sp, self.cq, self.sq = jnp.cos(tp), jnp.sin(tp), jnp.cos(tq), jnp.sin(tq)
        self.ct, self.st = jnp.cos(tt), jnp.sin(tt)

    def spectrum(self, signal):
        half = self.p // 2
        x = signal.astype(F32).T.reshape(self.channels, half, self.q)
        ein = functools.partial(jnp.einsum, precision=HIGH)
        re = ein("kn,cnq->ckq", self.cp[:, :half], x)
        im = -ein("kn,cnq->ckq", self.sp[:, :half], x)
        re, im = re * self.ct + im * self.st, im * self.ct - re * self.st
        return (
            ein("ckn,nm->ckm", re, self.cq) + ein("ckn,nm->ckm", im, self.sq),
            ein("ckn,nm->ckm", im, self.cq) - ein("ckn,nm->ckm", re, self.sq),
        )

    def back(self, re, im):
        half = self.p // 2
        ein = functools.partial(jnp.einsum, precision=HIGH)
        br = ein("ckm,nm->ckn", re, self.cq) - ein("ckm,nm->ckn", im, self.sq)
        bi = ein("ckm,nm->ckn", im, self.cq) + ein("ckm,nm->ckn", re, self.sq)
        br, bi = br * self.ct - bi * self.st, bi * self.ct + br * self.st
        out = ein("nk,ckq->cnq", self.cp[:half], br) - ein("nk,ckq->cnq", self.sp[:half], bi)
        return (out.reshape(self.channels, self.length) / (2 * self.length)).T

    def convolve(self, signal, kernel_spec, bias, conjugate, extra):
        a_re, a_im = self.spectrum(signal)
        b_re, b_im = kernel_spec
        if conjugate:
            b_im = -b_im
        out = self.back(a_re * b_re - a_im * b_im, a_re * b_im + a_im * b_re)
        out = out + signal.astype(F32) * bias[None, :]
        out = jnp.pad(out.astype(BF16), ((0, extra), (0, 0)))
        rows = self.length // self.devices
        parts = [out[j * rows : (j + 1) * rows + extra] for j in range(self.devices)]
        return jnp.stack(parts), (a_re, a_im)

    def filter_grad(self, grad_spec, signal_spec, grad, signal, filt):
        features, hidden_pre, phase, hidden, window, filter_out = filt
        a_re, a_im = grad_spec
        b_re, b_im = signal_spec
        raw = self.back(a_re * b_re + a_im * b_im, a_im * b_re - a_re * b_im) * window
        out_grad = jnp.einsum("hn,nc->hc", hidden, raw, precision=HIGH)
        turned = jnp.einsum("nc,hc->hn", raw, filter_out, precision=HIGH) * jnp.cos(phase)
        in_grad = jnp.einsum("en,hn->eh", features, turned, precision=HIGH)
        sums = jnp.stack([jnp.sum(turned * hidden_pre, axis=1), jnp.sum(turned, axis=1)])
        return out_grad, in_grad, sums, jnp.sum(grad.astype(F32) * signal.astype(F32), axis=0)


def position_features(length):
    steps = jnp.arange(length, dtype=F32)
    scaled = steps / (length - 1)
    angles = 2.0 * math.pi * steps / length
    bands = (EMB - 1) // 2
    freqs = 0.0001 + jnp.arange(bands, dtype=F32) * (bands - 1 - 0.0001) / (bands - 1)
    phase = freqs[:, None] * angles[None, :]
    return jnp.concatenate([scaled[None, :], jnp.cos(phase), -jnp.sin(phase)], axis=0)


def swap(value, axis, bit):
    size = lax.axis_size(axis)
    return lax.ppermute(value, axis, [(i, i ^ bit) for i in range(size)])


def pick(value, index, axis):
    return lax.dynamic_index_in_dim(value, index, axis, keepdims=False)


def add(left, right):
    return (left.astype(F32) + right.astype(F32)).astype(BF16)


def seq_bits():
    bit, bits = 1, []
    while bit < lax.axis_size("seq"):
        bits.append(bit)
        bit *= 2
    return bits


def block_order(bits):
    order = [0]
    for bit in reversed(bits):
        order = [r ^ bit for r in order] + order
    return jnp.bitwise_xor(lax.axis_index("seq"), jnp.array(order, jnp.int32))


def chip_units(right, unit, which):
    per = right.shape[0] * right.shape[2] // (4 * unit)
    me = lax.axis_index("dp")
    return jnp.concatenate([jnp.bitwise_xor(me, w) * per + jnp.arange(per, dtype=jnp.int32) for w in which])


def halve(kept, got):
    half = kept.shape[0] // 2
    return add(kept[:half], got[:half]), add(kept[half:], got[half:])


def last(kept, got):
    return (kept.astype(F32) + got.astype(F32))[0]


def tie(*values):
    return lax.optimization_barrier(values)


def pack(parts):
    flat = jnp.concatenate([p.reshape(-1) for p in parts])
    short = -flat.shape[0] % 1024
    return jnp.pad(flat, (0, short)).reshape(-1, 128)


def unpack(packed, like):
    flat = packed.reshape(-1)
    out, place = [], 0
    for p in like:
        out.append(flat[place : place + p.size].reshape(p.shape))
        place += p.size
    return out


def back_act_kernel(dy, down, out, dy_sum):
    out[...] = mxu_nt(dy[...], down[...]).astype(BF16)
    @pl.when(pl.program_id(0) == 0)
    def _():
        acc = rows_loop(dy.shape[0], 16, lambda r, c: c + fold8(dy[r, :].astype(F32)))(jnp.zeros((8, dy.shape[1]), F32))
        dy_sum[...] = jnp.sum(acc, axis=0, keepdims=True)

def back_act(dy, down, block=512):
    rows, width = dy.shape
    ff = down.shape[0]
    return pl.pallas_call(
        back_act_kernel, grid=(ff // block,),
        in_specs=[pl.BlockSpec((rows, width), lambda f: (0, 0)), pl.BlockSpec((block, width), lambda f: (f, 0))],
        out_specs=[pl.BlockSpec((rows, block), lambda f: (0, f)), pl.BlockSpec((1, width), lambda f: (0, 0))],
        out_shape=[jax.ShapeDtypeStruct((rows, ff), BF16), jax.ShapeDtypeStruct((1, width), F32)],
        cost_estimate=cost(2 * rows * width * ff, 13 << 20),
        compiler_params=pltpu.CompilerParams(vmem_limit_bytes=GRANT), name="back_act")(dy, down)

def block_out_kernel(act, down, resid, bias, out, acc):
    f = pl.program_id(0)
    part = mxu(act[...], down[...])
    @pl.when(f == 0)
    def _():
        acc[...] = part + bias[...]
    @pl.when((f > 0) & (f < pl.num_programs(0) - 1))
    def _():
        acc[...] += part
    @pl.when(f == pl.num_programs(0) - 1)
    def _():
        out[...] = (acc[...] + part + resid[...].astype(F32)).astype(BF16)

def block_out(act, down, resid, bias, block=1024):
    rows, ff = act.shape
    width = down.shape[1]
    return pl.pallas_call(
        block_out_kernel, grid=(ff // block,),
        in_specs=[pl.BlockSpec((rows, block), lambda f: (0, f)), pl.BlockSpec((block, width), lambda f: (f, 0)),
                  pl.BlockSpec((rows, width), lambda f: (0, 0)), pl.BlockSpec((1, width), lambda f: (0, 0))],
        out_specs=pl.BlockSpec((rows, width), lambda f: (0, 0)),
        out_shape=jax.ShapeDtypeStruct((rows, width), BF16),
        scratch_shapes=[pltpu.VMEM((rows, width), F32)],
        cost_estimate=cost(2 * rows * width * ff, 15 << 20),
        compiler_params=pltpu.CompilerParams(vmem_limit_bytes=GRANT), name="block_out")(act, down, resid, bias)

C0 = math.sqrt(2.0 / math.pi)
C1 = C0 * 0.044715

def middle_kernel(conv, gate, x, dy, ga, wout, bout, gain, bias, up, up_bias,
                  act, gup, gup_sum, resid, normed, mixed, gattn, gconv, ggate, sums,
                  d2, normal, scale):
    f = pl.program_id(0)
    last = pl.num_programs(0) - 1
    rows, width = x.shape
    nb = width // LANES

    @pl.when((f == 0))
    def _():
        def mix(r, c):
            for j in range(nb):
                lanes = slice(j * LANES, (j + 1) * LANES)
                mixed[r, lanes] = (conv[j, r, :].astype(F32) * gate[r, lanes].astype(F32)).astype(BF16)
            return c
        rows_loop(rows, CHUNK, mix)(0)
        for h in range(2):
            half = slice(h * rows // 2, (h + 1) * rows // 2)
            d2[half, :] = mxu(mixed[half, :], wout[...])

        def norm(r, c):
            v = x[r, :].astype(F32) + d2[r, :] + bout[...]
            resid[r, :] = v.astype(BF16)
            mean = jnp.mean(v, axis=-1, keepdims=True)
            v = v - mean
            s = lax.rsqrt(jnp.mean(v * v, axis=-1, keepdims=True) + EPSILON)
            n = v * s
            scale[r, :] = s
            normal[r, :] = n
            normed[r, :] = (n * gain[...] + bias[...]).astype(BF16)
            return c
        rows_loop(rows, CHUNK, norm)(0)

    total = jnp.zeros((8, up.shape[1]), F32)
    pieces = 1
    for h in range(pieces):
        part = slice(h * rows // pieces, (h + 1) * rows // pieces)
        v = mxu(normed[part, :], up[...]) + up_bias[...]
        v2 = v * v
        t = jnp.tanh(v * (C0 + C1 * v2))
        half = 0.5 + 0.5 * t
        act[part, :] = (v * half).astype(BF16)
        slope = half + (0.5 * v) * (1.0 - t * t) * (C0 + (3.0 * C1) * v2)
        g = (ga[part, :].astype(F32) * slope).astype(BF16)
        gup[part, :] = g
        total += fold8(g.astype(F32))
        back = mxu_nt(g, up[...])
        @pl.when(f == 0)
        def _():
            d2[part, :] = back
        @pl.when(f > 0)
        def _():
            d2[part, :] += back
    gup_sum[...] = jnp.sum(total, axis=0, keepdims=True)

    @pl.when((f == last))
    def _():
        def norm_back(r, carry):
            a, b, o = carry
            d, n = d2[r, :], normal[r, :]
            a += fold8(d * n)
            b += fold8(d)
            e = d * gain[...]
            m1 = jnp.mean(e, axis=-1, keepdims=True)
            m2 = jnp.mean(e * n, axis=-1, keepdims=True)
            g = dy[r, :].astype(F32) + (e - m1 - n * m2) * scale[r, :]
            low = g.astype(BF16)
            gattn[r, :] = low
            o += fold8(low.astype(F32))
            return a, b, o
        zero = jnp.zeros((8, width), F32)
        a, b, o = rows_loop(rows, CHUNK, norm_back)((zero, zero, zero))
        sums[0:1, :] = jnp.sum(a, axis=0, keepdims=True)
        sums[1:2, :] = jnp.sum(b, axis=0, keepdims=True)
        sums[2:3, :] = jnp.sum(o, axis=0, keepdims=True)
        for h in range(2):
            half = slice(h * rows // 2, (h + 1) * rows // 2)
            d2[half, :] = mxu_nt(gattn[half, :], wout[...])
        def out(r, c):
            for j in range(nb):
                lanes = slice(j * LANES, (j + 1) * LANES)
                g = d2[r, lanes]
                gconv[j, r, :] = (g * gate[r, lanes].astype(F32)).astype(BF16)
                ggate[r, lanes] = (g * conv[j, r, :].astype(F32)).astype(BF16)
            return c
        rows_loop(rows, CHUNK, out)(0)

def middle(conv, gate, x, dy, ga, wout, bout, gain, bias, up, up_bias, block=512):
    rows, width = x.shape
    ff = up.shape[1]
    nb = width // LANES
    whole = lambda *s: pl.BlockSpec(s, lambda f: (0,) * len(s))
    flat = whole(rows, width)
    row = whole(1, width)
    cols = pl.BlockSpec((rows, block), lambda f: (0, f))
    bar = pl.BlockSpec((1, block), lambda f: (0, f))
    sd = jax.ShapeDtypeStruct
    return pl.pallas_call(
        middle_kernel, grid=(ff // block,),
        in_specs=[whole(nb, rows, LANES), flat, flat, flat, cols, whole(width, width), row, row, row,
                  pl.BlockSpec((width, block), lambda f: (0, f)), bar],
        out_specs=[cols, cols, bar, flat, flat, flat, flat, whole(nb, rows, LANES), flat, whole(3, width)],
        out_shape=[sd((rows, ff), BF16), sd((rows, ff), BF16), sd((1, ff), F32), sd((rows, width), BF16),
                   sd((rows, width), BF16), sd((rows, width), BF16), sd((rows, width), BF16),
                   sd((nb, rows, LANES), BF16), sd((rows, width), BF16), sd((3, width), F32)],
        scratch_shapes=[pltpu.VMEM((rows, width), F32), pltpu.VMEM((rows, width), F32), pltpu.VMEM((rows, 1), F32)],
        cost_estimate=cost(4 * rows * width * (ff + width), 34 << 20),
        compiler_params=pltpu.CompilerParams(vmem_limit_bytes=GRANT), name="middle")(
            conv, gate, x, dy, ga, wout, bout, gain, bias, up, up_bias)

PRE = 16

def enter_kernel(first, x, before, gain, bias, w0, w1, w2, b0, b1, b2, taps, inner, gate, proj, normed_out, normed, shifted):
    rows, width = x.shape
    def norm(src, base):
        def body(r, c):
            v = src[r, :].astype(F32)
            v = v - jnp.mean(v, axis=-1, keepdims=True)
            s = lax.rsqrt(jnp.mean(v * v, axis=-1, keepdims=True) + EPSILON)
            normed[pl.ds(r.start + base, r.size), :] = (v * s * gain[...] + bias[...]).astype(BF16)
            return c
        return body
    @pl.when(pl.program_id(0) == 0)
    def _():
        rows_loop(PRE, 16, norm(before, 0))(0)
        rows_loop(rows, CHUNK, norm(x, PRE))(0)
        normed_out[...] = normed[PRE:, :]
    cb = w0.shape[1]
    short = []
    keep = jnp.where(first[0] == 0, 0.0, 1.0)
    for k, (w, b) in enumerate(((w0, b0), (w1, b1), (w2, b2))):
        p = (mxu(normed[...], w[...]) + b[...]).astype(BF16)
        proj[k, PRE:, :] = p[PRE:]
        proj[k, :PRE, :] = (p[:PRE].astype(F32) * keep).astype(BF16)
        shifted[k, PRE:, :] = p[PRE:].astype(F32)
        shifted[k, :PRE, :] = p[:PRE].astype(F32) * keep
    def gates(r, c):
        s = []
        for k in range(3):
            p = shifted[k, pl.ds(r.start + (PRE - 8), r.size + 8), :]
            v = taps[9 + k : 10 + k, :] + sum(
                taps[3 * j + k : 3 * j + k + 1, :] * p[6 + j : 6 + j + r.size] for j in range(3))
            s.append(v)
        gate[r, :] = s[0].astype(BF16)
        v = (s[1] * s[2]).astype(BF16)
        for j in range(cb // LANES):
            inner[j, r, :] = v[:, j * LANES : (j + 1) * LANES]
        return c
    rows_loop(rows, CHUNK, gates)(0)

def enter(first, x, before, gain, bias, weight, in_bias, taps, block=256):
    rows, width = x.shape
    nb = width // LANES
    steps = width // block
    whole = lambda *s: pl.BlockSpec(s, lambda c: (0,) * len(s))
    wspec = lambda k: pl.BlockSpec((width, block), lambda c, k=k: (0, k * steps + c))
    bspec = lambda k: pl.BlockSpec((1, block), lambda c, k=k: (0, k * steps + c))
    sd = jax.ShapeDtypeStruct
    return pl.pallas_call(
        enter_kernel, grid=(steps,),
        in_specs=[pl.BlockSpec(memory_space=pltpu.SMEM), whole(rows, width), whole(PRE, width), whole(1, width), whole(1, width),
                  wspec(0), wspec(1), wspec(2), bspec(0), bspec(1), bspec(2), pl.BlockSpec((12, block), lambda c: (0, c))],
        out_specs=[pl.BlockSpec((block // LANES, rows, LANES), lambda c: (c, 0, 0)), pl.BlockSpec((rows, block), lambda c: (0, c)),
                   pl.BlockSpec((3, PRE + rows, block), lambda c: (0, 0, c)), whole(rows, width)],
        out_shape=[sd((nb, rows, LANES), BF16), sd((rows, width), BF16), sd((3, PRE + rows, width), BF16), sd((rows, width), BF16)],
        scratch_shapes=[pltpu.VMEM((PRE + rows, width), BF16), pltpu.VMEM((3, PRE + rows, block), F32)],
        cost_estimate=cost(6 * rows * width * width, 14 << 20),
        compiler_params=pltpu.CompilerParams(vmem_limit_bytes=GRANT), name="enter")(
            first, x, before, gain, bias, weight, weight, weight, in_bias, in_bias, in_bias, taps)

POST = 16

def leave_kernel(ginner, ggate, ggate_after, proj, proj_after, taps, gproj, sums, pbuf, gbuf):
    rows = ggate.shape[0]
    cb = ggate.shape[1]
    for k in range(3):
        pbuf[k, : PRE + rows, :] = proj[k].astype(F32)
        pbuf[k, PRE + rows :, :] = proj_after[k].astype(F32)
    tap = lambda j, k: taps[3 * j + k : 3 * j + k + 1, :]

    def lags(k, start, size):
        p = pbuf[k, pl.ds(start + (PRE - 8), size + 8), :]
        return [p[6 + j : 6 + j + size] for j in range(3)]

    def grads(start, size, g0):
        gi = jnp.concatenate([ginner[j, pl.ds(start, size), :] for j in range(cb // LANES)], axis=1).astype(F32)
        p1 = lags(1, start, size)
        p2 = lags(2, start, size)
        s1 = taps[10:11, :] + sum(tap(j, 1) * p1[j] for j in range(3))
        s2 = taps[11:12, :] + sum(tap(j, 2) * p2[j] for j in range(3))
        return (g0, gi * s2, gi * s1), p1, p2

    def first(r, carry):
        g, p1, p2 = grads(r.start, r.size, ggate[r, :].astype(F32))
        p0 = lags(0, r.start, r.size)
        out = []
        for k in range(3):
            gbuf[k, r, :] = g[k]
        for j in range(3):
            for k, p in enumerate((p0, p1, p2)):
                out.append(carry[3 * j + k] + fold8(g[k] * p[j]))
        for k in range(3):
            out.append(carry[9 + k] + fold8(g[k]))
        return tuple(out)

    acc = rows_loop(rows, CHUNK, first)(tuple(jnp.zeros((8, cb), F32) for _ in range(12)))
    for i in range(12):
        sums[i : i + 1, :] = jnp.sum(acc[i], axis=0, keepdims=True)
    g, _, _ = grads(rows, POST, ggate_after[...].astype(F32))
    for k in range(3):
        gbuf[k, rows:, :] = g[k]

    def second(r, carry):
        out = []
        for k in range(3):
            g = gbuf[k, pl.ds(r.start, r.size + 8), :]
            v = sum(tap(j, k) * g[2 - j : 2 - j + r.size] for j in range(3)).astype(BF16)
            gproj[k, r, :] = v
            out.append(carry[k] + fold8(v.astype(F32)))
        return tuple(out)

    acc = rows_loop(rows, CHUNK, second)(tuple(jnp.zeros((8, cb), F32) for _ in range(3)))
    for i in range(3):
        sums[12 + i : 13 + i, :] = jnp.sum(acc[i], axis=0, keepdims=True)
    sums[15:16, :] = jnp.zeros((1, cb), F32)

def leave(ginner, ggate, ggate_after, proj, proj_after, taps, block=256):
    rows, width = ggate.shape
    steps = width // block
    sd = jax.ShapeDtypeStruct
    return pl.pallas_call(
        leave_kernel, grid=(steps,),
        in_specs=[pl.BlockSpec((block // LANES, rows + POST, LANES), lambda c: (c, 0, 0)),
                  pl.BlockSpec((rows, block), lambda c: (0, c)), pl.BlockSpec((POST, block), lambda c: (0, c)),
                  pl.BlockSpec((3, PRE + rows, block), lambda c: (0, 0, c)), pl.BlockSpec((3, POST, block), lambda c: (0, 0, c)),
                  pl.BlockSpec((12, block), lambda c: (0, c))],
        out_specs=[pl.BlockSpec((3, rows, block), lambda c: (0, 0, c)), pl.BlockSpec((16, block), lambda c: (0, c))],
        out_shape=[sd((3, rows, width), BF16), sd((16, width), F32)],
        scratch_shapes=[pltpu.VMEM((3, PRE + rows + POST, block), F32), pltpu.VMEM((3, rows + POST, block), F32)],
        cost_estimate=cost(60 * rows * width, 9 << 20),
        compiler_params=pltpu.CompilerParams(vmem_limit_bytes=GRANT), name="leave")(ginner, ggate, ggate_after, proj, proj_after, taps)

def tokens_kernel(gproj, weight, x, gres, gain, out, sums, acc):
    k = pl.program_id(0)
    rows, width = x.shape
    part = mxu_nt(gproj[0], weight[...])
    @pl.when(k == 0)
    def _():
        acc[...] = part
    @pl.when(k > 0)
    def _():
        acc[...] += part
    @pl.when(k == pl.num_programs(0) - 1)
    def _():
        def body(r, carry):
            a, b = carry
            v = x[r, :].astype(F32)
            v = v - jnp.mean(v, axis=-1, keepdims=True)
            s = lax.rsqrt(jnp.mean(v * v, axis=-1, keepdims=True) + EPSILON)
            n = v * s
            d = acc[r, :]
            a += fold8(d * n)
            b += fold8(d)
            e = d * gain[...]
            m1 = jnp.mean(e, axis=-1, keepdims=True)
            m2 = jnp.mean(e * n, axis=-1, keepdims=True)
            out[r, :] = gres[r, :].astype(F32) + (e - m1 - n * m2) * s
            return a, b
        zero = jnp.zeros((8, width), F32)
        a, b = rows_loop(rows, CHUNK, body)((zero, zero))
        sums[0:1, :] = jnp.sum(a, axis=0, keepdims=True)
        sums[1:2, :] = jnp.sum(b, axis=0, keepdims=True)

def tokens_back(gproj, weight, x, gres, gain):
    rows, width = x.shape
    whole = lambda *s: pl.BlockSpec(s, lambda k: (0,) * len(s))
    sd = jax.ShapeDtypeStruct
    return pl.pallas_call(
        tokens_kernel, grid=(3,),
        in_specs=[pl.BlockSpec((1, rows, width), lambda k: (k, 0, 0)), pl.BlockSpec((width, width), lambda k: (0, k)),
                  whole(rows, width), whole(rows, width), whole(1, width)],
        out_specs=[whole(rows, width), whole(2, width)],
        out_shape=[sd((rows, width), F32), sd((2, width), F32)],
        scratch_shapes=[pltpu.VMEM((rows, width), F32)],
        cost_estimate=cost(6 * rows * width * width, 14 << 20),
        compiler_params=pltpu.CompilerParams(vmem_limit_bytes=GRANT), name="tokens_back")(gproj, weight, x, gres, gain)


def wgrad_kernel(row_order, units, *refs, lefts, rights, held, mode):
    acc = None
    for side in range(2):
        refs_left, refs = refs[:lefts], refs[lefts:]
        left = jnp.concatenate([r[...] for r in refs_left], axis=1)
        refs_right, refs = refs[:rights], refs[rights:]
        right = jnp.concatenate([r[0] for r in refs_right], axis=1)
        part = mxu_tn(left, right)
        acc = part if acc is None else acc + part
    outs = refs[held:]
    count, height, _ = outs[0].shape
    width = acc.shape[1] // 2
    value = acc.reshape(count, height, acc.shape[1]).astype(BF16)
    if mode == "x":
        outs[0][...] = value[..., :width]
        outs[1][...] = value[..., width:]
    if mode == "xy":
        cut = width // 2
        outs[0][...] = value[..., :cut]
        outs[1][...] = value[..., width : width + cut]
        value = jnp.concatenate([value[..., cut:width], value[..., width + cut :]], axis=2)
        outs = outs[2:]
    if mode in ("y", "xy"):
        early = pl.program_id(0) < pl.num_programs(0) // 2

        @pl.when(early)
        def _():
            outs[0][...] = value

        @pl.when(jnp.logical_not(early))
        def _():
            outs[1][...] = value


def wgrad(left, right, row_order, units, unit, mode, each, held=(), tall=None, start=0):
    rows, m = left[0].shape
    blocks, count = row_order.shape[0], units.shape[0]
    height = m // blocks
    tall = tall or height
    at = start // height
    per = right[0].shape[2] // unit
    wide = count * unit
    half = wide // 2
    if height % LANES:
        left = [v.reshape(rows, blocks, height)[:, row_order].reshape(rows, m) for v in left]
        each = max(each, LANES // height)
        left_specs = [pl.BlockSpec((rows, each * height), lambda i, r, u: (0, i))]
    else:
        left_specs = [pl.BlockSpec((rows, height), lambda i, r, u, q=q: (0, r[i * each + q])) for q in range(each)]
    lefts, steps = len(left_specs), blocks // each
    right_specs = [
        pl.BlockSpec((1, rows, unit), lambda i, r, u, j=j: (u[j] // per, 0, u[j] % per)) for j in range(count)
    ]
    in_specs, args = [], []
    for side in range(2):
        in_specs += left_specs + right_specs
        args += [left[side]] * lefts + [right[side]] * count
    aliases = {2 + len(args) + i: i for i in range(len(held))}
    in_specs += [pl.BlockSpec(memory_space=pl.ANY)] * len(held)
    args += list(held)
    full = lambda w: ((blocks, tall, w), pl.BlockSpec((each, height, w), lambda i, r, u: (i, at, 0)))
    first = ((blocks // 2, tall, wide), lambda i: jnp.minimum(i, steps // 2 - 1))
    second = ((blocks // 2, tall, wide), lambda i: jnp.maximum(i - steps // 2, 0))
    part = lambda s, w: ((s[0][0], tall, w), pl.BlockSpec((each, height, w), lambda i, r, u: (s[1](i), at, 0)))
    outs = {
        "x": [full(half)] * 2,
        "y": [part(first, wide), part(second, wide)],
        "xy": [full(half // 2)] * 2 + [part(first, half), part(second, half)],
    }[mode]
    return pl.pallas_call(
        functools.partial(wgrad_kernel, lefts=lefts, rights=count, held=len(held), mode=mode),
        grid_spec=pltpu.PrefetchScalarGridSpec(
            num_scalar_prefetch=2, grid=(steps,), in_specs=in_specs, out_specs=[o[1] for o in outs]
        ),
        out_shape=[jax.ShapeDtypeStruct(o[0], BF16) for o in outs],
        input_output_aliases=aliases,
        cost_estimate=cost(4 * rows * m * wide, 4 * (rows * m + rows * wide + m * wide)),
        compiler_params=pltpu.CompilerParams(vmem_limit_bytes=GRANT),
        name="wgrad",
    )(row_order, units, *args)


def on_device(
    tokens,
    cotangent,
    norm1_gain,
    norm1_bias,
    in_weight,
    in_bias,
    short_weight,
    short_bias,
    filter_in,
    filter_in_bias,
    sine_freq,
    filter_out,
    decay_rates,
    filter_bias,
    out_weight,
    out_bias,
    norm2_gain,
    norm2_bias,
    up_weight,
    up_bias,
    down_weight,
    down_bias,
):
    width = in_weight.shape[0]
    ff = up_weight.shape[1]
    rows = tokens.shape[1]
    seq = lax.axis_size("seq")
    me = lax.axis_index("seq")
    length = rows * seq
    chans = width // seq
    down_shift = [(i + 1, i) for i in range(seq - 1)]

    x, dy = tokens[0], cotangent[0]
    mine = jnp.concatenate([short_weight.reshape(9 * chans), short_bias.reshape(3 * chans), x[rows - 2 :].reshape(-1).astype(F32)])
    used = mine.size
    mine = jnp.pad(mine, (0, -used % (8 * LANES)))
    got = lax.all_to_all(
        jnp.broadcast_to(mine.reshape(1, -1, LANES), (seq, mine.size // LANES, LANES)),
        "seq", split_axis=0, concat_axis=0, tiled=True,
    ).reshape(seq, -1)
    all_taps = got[:, : 12 * chans].reshape(seq, 12, chans).transpose(1, 0, 2).reshape(12, width)
    before = pick(got, jnp.maximum(me - 1, 0), 0)[12 * chans : used].reshape(2, width)
    before = jnp.concatenate([jnp.zeros((PRE - 2, width), BF16), before.astype(BF16)], axis=0)

    row = lambda v: v[None, :]
    first = me.reshape(1).astype(jnp.int32)
    fast = length // BLOCK <= 64
    tables = make_tables(length) if fast else None
    before, all_taps, tables = lax.optimization_barrier((before, all_taps, tables))
    inner, gate, proj, normed = enter(
        first, x, before, row(norm1_gain), row(norm1_bias), in_weight, row(in_bias), all_taps
    )
    proj_after = lax.ppermute(proj[:, PRE : PRE + POST], "seq", down_shift)

    def to_channels(value):
        if chans != LANES:
            value = value.transpose(1, 0, 2).reshape(rows, seq, chans).transpose(1, 0, 2)
        got = lax.all_to_all(value, "seq", split_axis=0, concat_axis=0, tiled=True)
        return got.reshape(length, chans)

    def to_tokens(value):
        got = lax.all_to_all(value, "seq", split_axis=0, concat_axis=0, tiled=True)
        if chans != LANES:
            got = got.transpose(1, 0, 2).reshape(got.shape[1], width // LANES, LANES).transpose(1, 0, 2)
        return got

    inner_chan = to_channels(inner)

    mixer = (FastMixer if fast else PlainMixer)(length, chans, seq, tables)
    features = position_features(length)
    hidden_pre = jnp.dot(filter_in.T, features, precision=HIGH) + filter_in_bias[:, None]
    phase = sine_freq[:, None] * hidden_pre
    hidden = jnp.sin(phase)
    window = jnp.exp(-features[0][:, None] * decay_rates[None, :])
    kernel = jnp.einsum("hn,hc->nc", hidden, filter_out, precision=HIGH) * window
    kernel_spec = mixer.spectrum(kernel)

    conv_chan, inner_spec = mixer.convolve(inner_chan, kernel_spec, filter_bias, False, 0)
    conv_chan, proj_after = tie(conv_chan, proj_after)
    conv = to_tokens(conv_chan)
    dy_other, normed_other = swap(dy, "dp", 1), swap(normed, "dp", 1)
    grad_act, dy_sum = back_act(dy, down_weight)
    conv, dy_other, normed_other = tie(conv, dy_other, normed_other)
    act, gup, gup_sum, resid, normed2, mixed, grad_attn, grad_conv, grad_gate, mid_sums = middle(
        conv, gate, x, dy, grad_act, out_weight, row(out_bias), row(norm2_gain), row(norm2_bias), up_weight, row(up_bias)
    )
    grad_chan = to_channels(grad_conv)
    gate_after = lax.ppermute(grad_gate[:POST], "seq", down_shift)

    bits = seq_bits()
    order = block_order(bits)
    up_bits = [bits[1], bits[0]] + bits[2:]
    up_order = block_order(up_bits)
    unit = width // 4
    tall = (ff + width) // seq
    wide = ff // seq

    pair = lambda value: (value, swap(value, "dp", 1))
    near_units, near_up = chip_units(dy[None], unit, (2, 0)), chip_units(gup[None], ff // 4, (2, 0))
    dy_pair, act_pair = (dy[None], dy_other[None]), pair(act)
    mixed_pair, attn_pair = pair(mixed), pair(grad_attn[None])
    gup_pair, normed2_pair = pair(gup[None]), pair(normed2)
    block_output = block_out(act, down_weight, resid, row(down_bias))
    block_output, act_pair = tie(block_output, act_pair)
    parts = wgrad(act_pair, dy_pair, order, near_units, unit, "x", 2, tall=tall)
    each = 8 if seq == 8 else 4
    tall_send, tall_kept = wgrad(
        mixed_pair, attn_pair, order, near_units, unit, "x", each, held=parts, tall=tall, start=wide
    )
    tall_got = swap(tall_send, "dp", 2)
    grad_chan, tall_kept = tie(grad_chan, tall_kept)
    grad_inner_chan, grad_spec = mixer.convolve(grad_chan, kernel_spec, filter_bias, True, POST)
    gup_pair, normed2_pair, grad_inner_chan, gate_after = tie(gup_pair, normed2_pair, grad_inner_chan, gate_after)
    grad_inner = to_tokens(grad_inner_chan)
    up_send, up_kept = wgrad(normed2_pair, gup_pair, up_order, near_up, ff // 4, "y", 4)

    grad_filter_out, grad_filter_in, filter_sums, grad_filter_bias = mixer.filter_grad(
        grad_spec, inner_spec, grad_chan, inner_chan, (features, hidden_pre, phase, hidden, window, filter_out)
    )
    grad_freq = filter_sums[0]
    grad_filter_in_bias = filter_sums[1] * sine_freq
    grad_filter_in = grad_filter_in * sine_freq[None, :]

    grad_inner, grad_filter_out, up_send = tie(grad_inner, grad_filter_out, up_send)
    up_got = swap(up_send, "seq", up_bits[0])
    grad_proj, leave_sums = leave(grad_inner, grad_gate, gate_after, proj, proj_after, all_taps)
    grad_proj, tall_got = tie(grad_proj, tall_got)
    tall_send, tall_kept = halve(tall_kept, tall_got)
    tall_got = swap(tall_send, "seq", bits[0])

    in_units = chip_units(grad_proj, unit, (2, 0))
    proj_pair = pair(grad_proj)
    in_parts = wgrad((normed, normed_other), proj_pair, order, in_units, unit, "xy", 4)
    grad_proj, in_a_send, in_b_send = tie(grad_proj, in_parts[0], in_parts[2])
    in_a_got = swap(in_a_send, "dp", 2)
    in_b_got = swap(in_b_send, "seq", bits[0])

    grad_tokens, token_sums = tokens_back(grad_proj, in_weight, x, grad_attn, row(norm1_gain))
    shared = (token_sums, leave_sums, mid_sums, gup_sum, dy_sum, grad_filter_in, grad_filter_in_bias, grad_freq)
    channel = (grad_filter_out, grad_filter_bias)
    packed, extra = pack(shared), pack(channel)
    rows_shared = packed.shape[0]
    packed = jnp.concatenate([packed, extra], axis=0)
    packed = packed + swap(packed, "dp", 1)
    packed, up_got, tall_got, in_a_got = tie(packed, up_got, tall_got, in_a_got)
    packed, extra = packed[:rows_shared], packed[rows_shared:]
    small = swap(packed, "seq", bits[0])
    cut = ff // 4
    up_send, up_kept = add(up_kept[..., :cut], up_got[..., :cut]), add(up_kept[..., cut:], up_got[..., cut:])
    up_got = swap(up_send, "dp", 2)
    tall_send, tall_kept = halve(tall_kept, tall_got)
    tall_got = swap(tall_send, "seq", bits[1])
    a_send, a_kept = halve(in_parts[1], in_a_got)
    a_got = swap(a_send, "seq", bits[0])

    in_b_got, tall_got, small = tie(in_b_got, tall_got, small)
    packed = packed + small
    small = swap(packed, "seq", bits[1])
    cut = in_b_got.shape[2] // 2
    b_send, b_kept = add(in_parts[3][..., :cut], in_b_got[..., :cut]), add(in_parts[3][..., cut:], in_b_got[..., cut:])
    b_got = swap(b_send, "dp", 2)
    tall_send, tall_kept = halve(tall_kept, tall_got)
    tall_got = swap(tall_send, "seq", bits[2])

    up_got, a_got, small = tie(up_got, a_got, small)
    both = jnp.concatenate([packed + small, extra], axis=0)
    small = swap(both, "dp", 2)
    up_send, up_kept = halve(up_kept, up_got)
    up_got = swap(up_send, "seq", up_bits[1])

    b_got, small = tie(b_got, small)
    both = both + small
    packed, extra = both[:rows_shared], both[rows_shared:]
    small = swap(packed, "seq", bits[2])
    kept, got = jnp.concatenate([a_kept, b_kept], axis=2), jnp.concatenate([a_got, b_got], axis=2)
    send, kept = halve(kept, got)
    got = swap(send, "seq", bits[1])

    for i in range(2, len(bits)):
        got, up_got, small, tall_got = tie(got, up_got, small, tall_got)
        packed = packed + small
        send, kept = halve(kept, got)
        got = swap(send, "seq", bits[i])
        up_send, up_kept = halve(up_kept, up_got)
        up_got = swap(up_send, "seq", bits[i])
        if i + 1 < len(bits):
            small = swap(packed, "seq", bits[i + 1])
            tall_send, tall_kept = halve(tall_kept, tall_got)
            tall_got = swap(tall_send, "seq", bits[i + 1])
    grad_in, grad_up, both = last(kept, got), last(up_kept, up_got), last(tall_kept, tall_got)
    grad_down, grad_out_weight = both[:wide], both[wide:]
    channel = unpack(extra, channel)
    shared = unpack(packed, shared)
    token_sums, leave_sums, mid_sums, gup_sum, dy_sum = shared[:5]
    own = lax.dynamic_slice_in_dim(leave_sums[:12], me * chans, chans, 1)
    return (
        block_output[None],
        grad_tokens[None],
        token_sums[0],
        token_sums[1],
        grad_in,
        leave_sums[12:15].reshape(-1),
        own[:9].reshape(3, 3, chans),
        own[9:],
        shared[5],
        shared[6],
        shared[7],
        channel[0],
        channel[1],
        grad_out_weight,
        mid_sums[2],
        mid_sums[0],
        mid_sums[1],
        grad_up,
        gup_sum[0],
        grad_down,
        dy_sum[0],
    )


def solution(mesh):
    everywhere, by_token, by_rows = P(), P("dp", "seq", None), P("seq", "dp")
    taps, shift, chan = P(None, None, "seq"), P(None, "seq"), P("seq")
    in_specs = (by_token,) * 2 + (everywhere,) * 4 + (taps, shift) + (everywhere,) * 3
    in_specs += (shift, chan, chan) + (everywhere,) * 8
    out_specs = (by_token, by_token, everywhere, everywhere, by_rows, everywhere, taps, shift)
    out_specs += (everywhere,) * 3 + (shift, chan, by_rows) + (everywhere,) * 3
    out_specs += (by_rows, everywhere, by_rows, everywhere)
    return jax.shard_map(
        on_device, mesh=mesh, in_specs=in_specs, out_specs=out_specs, check_vma=False
    )
```

```python
import functools
import math

import jax
import jax.numpy as jnp
import numpy as np
from jax import lax
from jax.experimental import pallas as pl
from jax.experimental.pallas import tpu as pltpu
from jax.sharding import PartitionSpec as P

EMB = 33
HIGH = lax.Precision.HIGHEST
EPSILON = 1e-05
BLOCK = 128
LANES = 128
ROWS = 16
CHUNK = 64
GRANT = 60 << 20
COST = 8
F32 = jnp.float32
BF16 = jnp.bfloat16


def times_root(re, im, num, den):
    num = num % den
    if num == 0:
        return re, im
    if 4 * num == den:
        return -im, re
    if 2 * num == den:
        return -re, -im
    if 4 * num == 3 * den:
        return im, -re
    angle = 2.0 * math.pi * num / den
    cos, sin = math.cos(angle), math.sin(angle)
    if abs(abs(cos) - abs(sin)) < 1e-12:
        sc, ss = (1.0 if cos > 0 else -1.0), (1.0 if sin > 0 else -1.0)
        root = abs(cos)
        return root * (sc * re - ss * im), root * (sc * im + ss * re)
    return re * cos - im * sin, im * cos + re * sin


def small_fft(re, im, sign):
    count = len(re)
    if count == 1:
        return re, im
    if count == 2:
        return [re[0] + re[1], re[0] - re[1]], [im[0] + im[1], im[0] - im[1]]
    even_re, even_im = small_fft(re[0::2], im[0::2], sign)
    odd_re, odd_im = small_fft(re[1::2], im[1::2], sign)
    low_re, low_im, top_re, top_im = [], [], [], []
    for k in range(count // 2):
        tr, ti = times_root(odd_re[k], odd_im[k], sign * k, count)
        low_re.append(even_re[k] + tr)
        low_im.append(even_im[k] + ti)
        top_re.append(even_re[k] - tr)
        top_im.append(even_im[k] - ti)
    return low_re + top_re, low_im + top_im


def blocks_forward(source, target, count):
    def body(step, carry):
        row = pl.multiple_of(step * ROWS, ROWS)
        re, im = [], []
        for a in range(count):
            value = source[a, pl.ds(row, ROWS), :].astype(F32)
            angle = 2.0 * math.pi * a / (4 * count)
            re.append(value * math.cos(angle))
            im.append(value * math.sin(angle))
        re, im = small_fft(re, im, -1)
        for k in range(count):
            target[k, pl.ds(row, ROWS), :] = re[k].astype(BF16)
            target[k, pl.ds(BLOCK + row, ROWS), :] = im[k].astype(BF16)
        return carry

    lax.fori_loop(0, BLOCK // ROWS, body, 0)


def blocks_inverse(source, emit, count):
    def body(step, carry):
        row = pl.multiple_of(step * ROWS, ROWS)
        re = [source[k, pl.ds(row, ROWS), :] for k in range(count)]
        im = [source[k, pl.ds(BLOCK + row, ROWS), :] for k in range(count)]
        re, im = small_fft(re, im, 1)
        for a in range(count):
            angle = 2.0 * math.pi * a / (4 * count)
            emit(a, row, re[a] * math.cos(angle) + im[a] * math.sin(angle))
        return carry

    lax.fori_loop(0, BLOCK // ROWS, body, 0)


def cost(flops, bytes_accessed):
    return pl.CostEstimate(flops=flops // COST, bytes_accessed=bytes_accessed // COST, transcendentals=0)


def mxu(left, right):
    return jnp.dot(left, right, preferred_element_type=F32)

def mxu_nt(left, right):
    return lax.dot_general(left, right, (((1,), (1,)), ((), ())), preferred_element_type=F32)

def mxu_tn(left, right):
    return lax.dot_general(left, right, (((0,), (0,)), ((), ())), preferred_element_type=F32)

def rows_loop(total, chunk, body, unroll=1):
    def step(i, carry):
        return body(pl.ds(pl.multiple_of(i * chunk, chunk), chunk), carry)
    return lambda init: lax.fori_loop(0, total // chunk, step, init, unroll=unroll)

def fold8(v):
    return jnp.sum(v.reshape(v.shape[0] // 8, 8, v.shape[1]), axis=0)


def table_kernel(alpha_cos, alpha_sin, beta_cos, beta_sin, forward, inverse, *, scale):
    cb, sb = beta_cos[...], beta_sin[...]
    for i in range(forward.shape[0]):
        ca, sa = alpha_cos[i], alpha_sin[i]
        cos = ca * cb - sa * sb
        sin = sa * cb + ca * sb
        low_cos, low_sin = cos.astype(BF16), sin.astype(BF16)
        forward[i, :BLOCK, :BLOCK] = low_cos
        forward[i, :BLOCK, BLOCK:] = low_sin
        forward[i, BLOCK:, :BLOCK] = -low_sin
        forward[i, BLOCK:, BLOCK:] = low_cos
        low_cos, low_sin = (cos.T * scale).astype(BF16), (sin.T * scale).astype(BF16)
        inverse[i, :BLOCK, :BLOCK] = low_cos
        inverse[i, :BLOCK, BLOCK:] = -low_sin
        inverse[i, BLOCK:, :BLOCK] = low_sin
        inverse[i, BLOCK:, BLOCK:] = low_cos


def make_tables(length):
    count = length // BLOCK
    alpha = 2.0 * np.pi * np.arange(BLOCK)[None, :] * (np.arange(count)[:, None] - 0.25) / length
    beta = 2.0 * np.pi * ((np.arange(BLOCK)[:, None] * np.arange(BLOCK)[None, :]) % BLOCK) / BLOCK
    alpha = alpha[:, None, :]
    consts = [jnp.asarray(f(v), F32) for v in (alpha, beta) for f in (np.cos, np.sin)]
    each = math.gcd(count, 4)
    row = pl.BlockSpec((each, 1, BLOCK), lambda i: (i, 0, 0))
    flat = pl.BlockSpec((BLOCK, BLOCK), lambda i: (0, 0))
    out = pl.BlockSpec((each, 2 * BLOCK, 2 * BLOCK), lambda i: (i, 0, 0))
    shape = jax.ShapeDtypeStruct((count, 2 * BLOCK, 2 * BLOCK), BF16)
    return pl.pallas_call(
        functools.partial(table_kernel, scale=1.0 / length),
        grid=(count // each,),
        in_specs=[row, row, flat, flat],
        out_specs=[out, out],
        out_shape=[shape, shape],
        cost_estimate=cost(16 * count * BLOCK * BLOCK, 8 << 20),
        name="tables",
    )(*consts)


def split_spec(value):
    return value[:BLOCK], value[BLOCK:]


def turn_back(prod, inverse, back):
    def body(k, carry):
        back[k] = mxu(inverse[k], prod[k])
        return carry

    lax.fori_loop(0, prod.shape[0], body, 0, unroll=8)


def spectrum_kernel(signal, forward, spectrum, mid):
    (signal, have_signal), (forward, have_forward) = signal, forward
    count = signal.shape[0]
    have_signal()
    blocks_forward(signal, mid, count)
    have_forward()

    def body(k, carry):
        spectrum[k] = mxu(forward[k], mid[k]).astype(BF16)
        return carry

    lax.fori_loop(0, count, body, 0, unroll=8)


def conv_kernel(signal, kernel_spec, bias, forward, inverse, result, spectrum, mid, prod, back, *, conjugate):
    (signal, have_signal), (kernel_spec, have_spec), (bias, have_bias) = signal, kernel_spec, bias
    (forward, have_forward), (inverse, have_inverse) = forward, inverse
    count = signal.shape[0]
    have_signal()
    blocks_forward(signal, mid, count)
    have_spec()
    have_bias()
    have_forward()

    def body(k, carry):
        spec = mxu(forward[k], mid[k])
        spectrum[k] = spec.astype(BF16)
        a_re, a_im = split_spec(spec)
        b_re, b_im = split_spec(kernel_spec[k].astype(F32))
        if conjugate:
            b_im = -b_im
        prod[k, :BLOCK, :] = (a_re * b_re - a_im * b_im).astype(BF16)
        prod[k, BLOCK:, :] = (a_re * b_im + a_im * b_re).astype(BF16)
        return carry

    lax.fori_loop(0, count, body, 0, unroll=8)
    have_inverse()
    turn_back(prod, inverse, back)
    gain = bias[...]
    devices, rows, _ = result.shape
    per = count // devices
    size = per * BLOCK

    def emit(a, row, value):
        direct = signal[a, pl.ds(row, ROWS), :].astype(F32) * gain
        result[a // per, pl.ds((a % per) * BLOCK + row, ROWS), :] = (value + direct).astype(result.dtype)

    blocks_inverse(back, emit, count)
    if rows > size:
        for j in range(devices - 1):
            result[j, size:, :] = result[j + 1, : rows - size, :]
        result[devices - 1, size:, :] = jnp.zeros((rows - size, result.shape[2]), result.dtype)


def filter_grad_kernel(
    grad_spec, signal_spec, grad, signal, inverse, window, hidden, slope, hidden_pre, features, filter_out,
    out_grad, in_grad, sums, bias_grad, prod, back, raw,
):
    (grad_spec, have_grad_spec), (signal_spec, have_signal_spec) = grad_spec, signal_spec
    count = grad_spec.shape[0]
    have_grad_spec()
    have_signal_spec()

    def body(k, carry):
        a_re, a_im = split_spec(grad_spec[k].astype(F32))
        b_re, b_im = split_spec(signal_spec[k].astype(F32))
        prod[k, :BLOCK, :] = (a_re * b_re + a_im * b_im).astype(BF16)
        prod[k, BLOCK:, :] = (a_im * b_re - a_re * b_im).astype(BF16)
        return carry

    lax.fori_loop(0, count, body, 0, unroll=2)
    for _, wait in (grad, signal, inverse, window, hidden, slope, hidden_pre, features, filter_out):
        wait()
    grad, signal, inverse, window, hidden, slope, hidden_pre, features, filter_out = (
        v[0] for v in (grad, signal, inverse, window, hidden, slope, hidden_pre, features, filter_out)
    )
    turn_back(prod, inverse, back)

    def emit(a, row, value):
        at = pl.ds(a * BLOCK + row, ROWS)
        raw[at, :] = (value * window[at, :]).astype(BF16)

    blocks_inverse(back, emit, count)

    def total(a, acc):
        return acc + fold8(grad[a].astype(F32) * signal[a].astype(F32))

    acc = lax.fori_loop(0, count, total, jnp.zeros((8, grad.shape[-1]), F32))
    bias_grad[...] = jnp.sum(acc, axis=0, keepdims=True)
    out_grad[...] = mxu(hidden[...], raw[...])
    turned = mxu_nt(filter_out[...], raw[...]) * slope[...]
    sums[...] = jnp.concatenate(
        [jnp.sum(turned * hidden_pre[...], axis=1, keepdims=True), jnp.sum(turned, axis=1, keepdims=True)], axis=1
    )
    in_grad[...] = mxu_nt(features[...], turned.astype(BF16))


def vmem_call(kernel, outs, scratch, args, name):
    count = len(args)

    def body(*refs):
        ins, rest = refs[:count], refs[count:]
        results, local = rest[: len(outs)], rest[len(outs) : len(outs) + len(scratch)]
        bufs, sems = rest[len(outs) + len(scratch) : -1], rest[-1]
        copies = [pltpu.make_async_copy(src, dst, sems.at[i]) for i, (src, dst) in enumerate(zip(ins, bufs))]
        for copy in copies:
            copy.start()
        kernel(*[(buf, copy.wait) for buf, copy in zip(bufs, copies)], *results, *local)

    scratch = list(scratch)
    held = [pltpu.VMEM(a.shape, a.dtype) for a in args]
    return pl.pallas_call(
        body,
        in_specs=[pl.BlockSpec(memory_space=pl.ANY)] * count,
        out_specs=[pl.BlockSpec(o.shape, lambda n=len(o.shape): (0,) * n) for o in outs],
        out_shape=outs,
        scratch_shapes=scratch + held + [pltpu.SemaphoreType.DMA((count,))],
        cost_estimate=cost(4 << 30, 16 << 20),
        compiler_params=pltpu.CompilerParams(vmem_limit_bytes=GRANT),
        name=name,
    )(*args)


class FastMixer:
    def __init__(self, length, channels, devices, tables):
        self.count = length // BLOCK
        self.channels = channels
        self.devices = devices
        self.forward, self.inverse = tables
        self.mid = pltpu.VMEM((self.count, 2 * BLOCK, channels), BF16)
        self.back = pltpu.VMEM((self.count, 2 * BLOCK, channels), F32)
        self.spec = jax.ShapeDtypeStruct((self.count, 2 * BLOCK, channels), BF16)

    def blocked(self, value):
        return value.reshape(self.count, BLOCK, self.channels)

    def spectrum(self, signal):
        args = (self.blocked(signal), self.forward)
        return vmem_call(spectrum_kernel, [self.spec], [self.mid], args, "spectrum")[0]

    def convolve(self, signal, kernel_spec, bias, conjugate, extra):
        rows = self.count * BLOCK // self.devices + extra
        out = jax.ShapeDtypeStruct((self.devices, rows, self.channels), BF16)
        return vmem_call(
            functools.partial(conv_kernel, conjugate=conjugate),
            [out, self.spec],
            [self.mid, self.mid, self.back],
            (self.blocked(signal), kernel_spec, bias[None, :], self.forward, self.inverse),
            "correlate" if conjugate else "convolve",
        )

    def filter_grad(self, grad_spec, signal_spec, grad, signal, filt):
        features, hidden_pre, phase, hidden, window, filter_out = filt
        units = hidden.shape[0]
        outs = [
            jax.ShapeDtypeStruct((units, self.channels), F32),
            jax.ShapeDtypeStruct((48, units), F32),
            jax.ShapeDtypeStruct((units, 2), F32),
            jax.ShapeDtypeStruct((1, self.channels), F32),
        ]
        padded = jnp.pad(features.astype(BF16), ((0, 48 - EMB), (0, 0)))
        raw = pltpu.VMEM((self.count * BLOCK, self.channels), BF16)
        out_grad, in_grad, sums, bias_grad = vmem_call(
            filter_grad_kernel,
            outs,
            [self.mid, self.back, raw],
            (grad_spec, signal_spec, self.blocked(grad), self.blocked(signal), self.inverse, window)
            + (hidden.astype(BF16), jnp.cos(phase), hidden_pre, padded, filter_out.astype(BF16)),
            "filter_grad",
        )
        return out_grad, in_grad[:EMB], sums.T, bias_grad[0]


class PlainMixer:
    def __init__(self, length, channels, devices, tables):
        self.length = length
        self.devices = devices
        self.channels = channels
        full = 2 * length
        p = 2
        while p * p * 2 <= full and full % (p * 2) == 0:
            p = p * 2
        q = full // p
        self.p, self.q = p, q
        ip, iq = jnp.arange(p, dtype=jnp.int32), jnp.arange(q, dtype=jnp.int32)
        tp = 2.0 * math.pi * (ip[:, None] * ip[None, :] % p).astype(F32) / p
        tq = 2.0 * math.pi * (iq[:, None] * iq[None, :] % q).astype(F32) / q
        tt = 2.0 * math.pi * (ip[:, None] * iq[None, :] % full).astype(F32) / full
        self.cp, self.sp, self.cq, self.sq = jnp.cos(tp), jnp.sin(tp), jnp.cos(tq), jnp.sin(tq)
        self.ct, self.st = jnp.cos(tt), jnp.sin(tt)

    def spectrum(self, signal):
        half = self.p // 2
        x = signal.astype(F32).T.reshape(self.channels, half, self.q)
        ein = functools.partial(jnp.einsum, precision=HIGH)
        re = ein("kn,cnq->ckq", self.cp[:, :half], x)
        im = -ein("kn,cnq->ckq", self.sp[:, :half], x)
        re, im = re * self.ct + im * self.st, im * self.ct - re * self.st
        return (
            ein("ckn,nm->ckm", re, self.cq) + ein("ckn,nm->ckm", im, self.sq),
            ein("ckn,nm->ckm", im, self.cq) - ein("ckn,nm->ckm", re, self.sq),
        )

    def back(self, re, im):
        half = self.p // 2
        ein = functools.partial(jnp.einsum, precision=HIGH)
        br = ein("ckm,nm->ckn", re, self.cq) - ein("ckm,nm->ckn", im, self.sq)
        bi = ein("ckm,nm->ckn", im, self.cq) + ein("ckm,nm->ckn", re, self.sq)
        br, bi = br * self.ct - bi * self.st, bi * self.ct + br * self.st
        out = ein("nk,ckq->cnq", self.cp[:half], br) - ein("nk,ckq->cnq", self.sp[:half], bi)
        return (out.reshape(self.channels, self.length) / (2 * self.length)).T

    def convolve(self, signal, kernel_spec, bias, conjugate, extra):
        a_re, a_im = self.spectrum(signal)
        b_re, b_im = kernel_spec
        if conjugate:
            b_im = -b_im
        out = self.back(a_re * b_re - a_im * b_im, a_re * b_im + a_im * b_re)
        out = out + signal.astype(F32) * bias[None, :]
        out = jnp.pad(out.astype(BF16), ((0, extra), (0, 0)))
        rows = self.length // self.devices
        parts = [out[j * rows : (j + 1) * rows + extra] for j in range(self.devices)]
        return jnp.stack(parts), (a_re, a_im)

    def filter_grad(self, grad_spec, signal_spec, grad, signal, filt):
        features, hidden_pre, phase, hidden, window, filter_out = filt
        a_re, a_im = grad_spec
        b_re, b_im = signal_spec
        raw = self.back(a_re * b_re + a_im * b_im, a_im * b_re - a_re * b_im) * window
        out_grad = jnp.einsum("hn,nc->hc", hidden, raw, precision=HIGH)
        turned = jnp.einsum("nc,hc->hn", raw, filter_out, precision=HIGH) * jnp.cos(phase)
        in_grad = jnp.einsum("en,hn->eh", features, turned, precision=HIGH)
        sums = jnp.stack([jnp.sum(turned * hidden_pre, axis=1), jnp.sum(turned, axis=1)])
        return out_grad, in_grad, sums, jnp.sum(grad.astype(F32) * signal.astype(F32), axis=0)


def position_features(length):
    steps = jnp.arange(length, dtype=F32)
    scaled = steps / (length - 1)
    angles = 2.0 * math.pi * steps / length
    bands = (EMB - 1) // 2
    freqs = 0.0001 + jnp.arange(bands, dtype=F32) * (bands - 1 - 0.0001) / (bands - 1)
    phase = freqs[:, None] * angles[None, :]
    return jnp.concatenate([scaled[None, :], jnp.cos(phase), -jnp.sin(phase)], axis=0)


def swap(value, axis, bit):
    size = lax.axis_size(axis)
    return lax.ppermute(value, axis, [(i, i ^ bit) for i in range(size)])


def pick(value, index, axis):
    return lax.dynamic_index_in_dim(value, index, axis, keepdims=False)


def add(left, right):
    return (left.astype(F32) + right.astype(F32)).astype(BF16)


def seq_bits():
    bit, bits = 1, []
    while bit < lax.axis_size("seq"):
        bits.append(bit)
        bit *= 2
    return bits


def block_order(bits):
    order = [0]
    for bit in reversed(bits):
        order = [r ^ bit for r in order] + order
    return jnp.bitwise_xor(lax.axis_index("seq"), jnp.array(order, jnp.int32))


def chip_units(right, unit, which):
    per = right.shape[0] * right.shape[2] // (4 * unit)
    me = lax.axis_index("dp")
    return jnp.concatenate([jnp.bitwise_xor(me, w) * per + jnp.arange(per, dtype=jnp.int32) for w in which])


def halve(kept, got):
    half = kept.shape[0] // 2
    return add(kept[:half], got[:half]), add(kept[half:], got[half:])


def last(kept, got):
    return (kept.astype(F32) + got.astype(F32))[0]


def tie(*values):
    return lax.optimization_barrier(values)


def pack(parts):
    flat = jnp.concatenate([p.reshape(-1) for p in parts])
    short = -flat.shape[0] % 1024
    return jnp.pad(flat, (0, short)).reshape(-1, 128)


def unpack(packed, like):
    flat = packed.reshape(-1)
    out, place = [], 0
    for p in like:
        out.append(flat[place : place + p.size].reshape(p.shape))
        place += p.size
    return out


def back_act_kernel(dy, down, out, dy_sum):
    out[...] = mxu_nt(dy[...], down[...]).astype(BF16)
    @pl.when(pl.program_id(0) == 0)
    def _():
        acc = rows_loop(dy.shape[0], 16, lambda r, c: c + fold8(dy[r, :].astype(F32)))(jnp.zeros((8, dy.shape[1]), F32))
        dy_sum[...] = jnp.sum(acc, axis=0, keepdims=True)

def back_act(dy, down, block=512):
    rows, width = dy.shape
    ff = down.shape[0]
    return pl.pallas_call(
        back_act_kernel, grid=(ff // block,),
        in_specs=[pl.BlockSpec((rows, width), lambda f: (0, 0)), pl.BlockSpec((block, width), lambda f: (f, 0))],
        out_specs=[pl.BlockSpec((rows, block), lambda f: (0, f)), pl.BlockSpec((1, width), lambda f: (0, 0))],
        out_shape=[jax.ShapeDtypeStruct((rows, ff), BF16), jax.ShapeDtypeStruct((1, width), F32)],
        cost_estimate=cost(2 * rows * width * ff, 13 << 20),
        compiler_params=pltpu.CompilerParams(vmem_limit_bytes=GRANT), name="back_act")(dy, down)

def block_out_kernel(act, down, resid, bias, out, acc):
    f = pl.program_id(0)
    part = mxu(act[...], down[...])
    @pl.when(f == 0)
    def _():
        acc[...] = part + bias[...]
    @pl.when((f > 0) & (f < pl.num_programs(0) - 1))
    def _():
        acc[...] += part
    @pl.when(f == pl.num_programs(0) - 1)
    def _():
        out[...] = (acc[...] + part + resid[...].astype(F32)).astype(BF16)

def block_out(act, down, resid, bias, block=1024):
    rows, ff = act.shape
    width = down.shape[1]
    return pl.pallas_call(
        block_out_kernel, grid=(ff // block,),
        in_specs=[pl.BlockSpec((rows, block), lambda f: (0, f)), pl.BlockSpec((block, width), lambda f: (f, 0)),
                  pl.BlockSpec((rows, width), lambda f: (0, 0)), pl.BlockSpec((1, width), lambda f: (0, 0))],
        out_specs=pl.BlockSpec((rows, width), lambda f: (0, 0)),
        out_shape=jax.ShapeDtypeStruct((rows, width), BF16),
        scratch_shapes=[pltpu.VMEM((rows, width), F32)],
        cost_estimate=cost(2 * rows * width * ff, 15 << 20),
        compiler_params=pltpu.CompilerParams(vmem_limit_bytes=GRANT), name="block_out")(act, down, resid, bias)

C0 = math.sqrt(2.0 / math.pi)
C1 = C0 * 0.044715

def middle_kernel(conv, gate, x, dy, ga, wout, bout, gain, bias, up, up_bias,
                  act, gup, gup_sum, resid, normed, mixed, gattn, gconv, ggate, sums,
                  d2, normal, scale):
    f = pl.program_id(0)
    last = pl.num_programs(0) - 1
    rows, width = x.shape
    nb = width // LANES

    @pl.when((f == 0))
    def _():
        def mix(r, c):
            for j in range(nb):
                lanes = slice(j * LANES, (j + 1) * LANES)
                mixed[r, lanes] = (conv[j, r, :].astype(F32) * gate[r, lanes].astype(F32)).astype(BF16)
            return c
        rows_loop(rows, CHUNK, mix)(0)
        for h in range(2):
            half = slice(h * rows // 2, (h + 1) * rows // 2)
            d2[half, :] = mxu(mixed[half, :], wout[...])

        def norm(r, c):
            v = x[r, :].astype(F32) + d2[r, :] + bout[...]
            resid[r, :] = v.astype(BF16)
            mean = jnp.mean(v, axis=-1, keepdims=True)
            v = v - mean
            s = lax.rsqrt(jnp.mean(v * v, axis=-1, keepdims=True) + EPSILON)
            n = v * s
            scale[r, :] = s
            normal[r, :] = n
            normed[r, :] = (n * gain[...] + bias[...]).astype(BF16)
            return c
        rows_loop(rows, CHUNK, norm)(0)

    total = jnp.zeros((8, up.shape[1]), F32)
    pieces = 1
    for h in range(pieces):
        part = slice(h * rows // pieces, (h + 1) * rows // pieces)
        v = mxu(normed[part, :], up[...]) + up_bias[...]
        v2 = v * v
        t = jnp.tanh(v * (C0 + C1 * v2))
        half = 0.5 + 0.5 * t
        act[part, :] = (v * half).astype(BF16)
        slope = half + (0.5 * v) * (1.0 - t * t) * (C0 + (3.0 * C1) * v2)
        g = (ga[part, :].astype(F32) * slope).astype(BF16)
        gup[part, :] = g
        total += fold8(g.astype(F32))
        back = mxu_nt(g, up[...])
        @pl.when(f == 0)
        def _():
            d2[part, :] = back
        @pl.when(f > 0)
        def _():
            d2[part, :] += back
    gup_sum[...] = jnp.sum(total, axis=0, keepdims=True)

    @pl.when((f == last))
    def _():
        def norm_back(r, carry):
            a, b, o = carry
            d, n = d2[r, :], normal[r, :]
            a += fold8(d * n)
            b += fold8(d)
            e = d * gain[...]
            m1 = jnp.mean(e, axis=-1, keepdims=True)
            m2 = jnp.mean(e * n, axis=-1, keepdims=True)
            g = dy[r, :].astype(F32) + (e - m1 - n * m2) * scale[r, :]
            low = g.astype(BF16)
            gattn[r, :] = low
            o += fold8(low.astype(F32))
            return a, b, o
        zero = jnp.zeros((8, width), F32)
        a, b, o = rows_loop(rows, CHUNK, norm_back)((zero, zero, zero))
        sums[0:1, :] = jnp.sum(a, axis=0, keepdims=True)
        sums[1:2, :] = jnp.sum(b, axis=0, keepdims=True)
        sums[2:3, :] = jnp.sum(o, axis=0, keepdims=True)
        for h in range(2):
            half = slice(h * rows // 2, (h + 1) * rows // 2)
            d2[half, :] = mxu_nt(gattn[half, :], wout[...])
        def out(r, c):
            for j in range(nb):
                lanes = slice(j * LANES, (j + 1) * LANES)
                g = d2[r, lanes]
                gconv[j, r, :] = (g * gate[r, lanes].astype(F32)).astype(BF16)
                ggate[r, lanes] = (g * conv[j, r, :].astype(F32)).astype(BF16)
            return c
        rows_loop(rows, CHUNK, out)(0)

def middle(conv, gate, x, dy, ga, wout, bout, gain, bias, up, up_bias, block=512):
    rows, width = x.shape
    ff = up.shape[1]
    nb = width // LANES
    whole = lambda *s: pl.BlockSpec(s, lambda f: (0,) * len(s))
    flat = whole(rows, width)
    row = whole(1, width)
    cols = pl.BlockSpec((rows, block), lambda f: (0, f))
    bar = pl.BlockSpec((1, block), lambda f: (0, f))
    sd = jax.ShapeDtypeStruct
    return pl.pallas_call(
        middle_kernel, grid=(ff // block,),
        in_specs=[whole(nb, rows, LANES), flat, flat, flat, cols, whole(width, width), row, row, row,
                  pl.BlockSpec((width, block), lambda f: (0, f)), bar],
        out_specs=[cols, cols, bar, flat, flat, flat, flat, whole(nb, rows, LANES), flat, whole(3, width)],
        out_shape=[sd((rows, ff), BF16), sd((rows, ff), BF16), sd((1, ff), F32), sd((rows, width), BF16),
                   sd((rows, width), BF16), sd((rows, width), BF16), sd((rows, width), BF16),
                   sd((nb, rows, LANES), BF16), sd((rows, width), BF16), sd((3, width), F32)],
        scratch_shapes=[pltpu.VMEM((rows, width), F32), pltpu.VMEM((rows, width), F32), pltpu.VMEM((rows, 1), F32)],
        cost_estimate=cost(4 * rows * width * (ff + width), 34 << 20),
        compiler_params=pltpu.CompilerParams(vmem_limit_bytes=GRANT), name="middle")(
            conv, gate, x, dy, ga, wout, bout, gain, bias, up, up_bias)

PRE = 16

def enter_kernel(first, x, before, gain, bias, w0, w1, w2, b0, b1, b2, taps, inner, gate, proj, normed_out, normed, shifted):
    rows, width = x.shape
    def norm(src, base):
        def body(r, c):
            v = src[r, :].astype(F32)
            v = v - jnp.mean(v, axis=-1, keepdims=True)
            s = lax.rsqrt(jnp.mean(v * v, axis=-1, keepdims=True) + EPSILON)
            normed[pl.ds(r.start + base, r.size), :] = (v * s * gain[...] + bias[...]).astype(BF16)
            return c
        return body
    @pl.when(pl.program_id(0) == 0)
    def _():
        rows_loop(PRE, 16, norm(before, 0))(0)
        rows_loop(rows, CHUNK, norm(x, PRE))(0)
        normed_out[...] = normed[PRE:, :]
    cb = w0.shape[1]
    short = []
    keep = jnp.where(first[0] == 0, 0.0, 1.0)
    for k, (w, b) in enumerate(((w0, b0), (w1, b1), (w2, b2))):
        p = (mxu(normed[...], w[...]) + b[...]).astype(BF16)
        proj[k, PRE:, :] = p[PRE:]
        proj[k, :PRE, :] = (p[:PRE].astype(F32) * keep).astype(BF16)
        shifted[k, PRE:, :] = p[PRE:].astype(F32)
        shifted[k, :PRE, :] = p[:PRE].astype(F32) * keep
    def gates(r, c):
        s = []
        for k in range(3):
            p = shifted[k, pl.ds(r.start + (PRE - 8), r.size + 8), :]
            v = taps[9 + k : 10 + k, :] + sum(
                taps[3 * j + k : 3 * j + k + 1, :] * p[6 + j : 6 + j + r.size] for j in range(3))
            s.append(v)
        gate[r, :] = s[0].astype(BF16)
        v = (s[1] * s[2]).astype(BF16)
        for j in range(cb // LANES):
            inner[j, r, :] = v[:, j * LANES : (j + 1) * LANES]
        return c
    rows_loop(rows, CHUNK, gates)(0)

def enter(first, x, before, gain, bias, weight, in_bias, taps, block=256):
    rows, width = x.shape
    nb = width // LANES
    steps = width // block
    whole = lambda *s: pl.BlockSpec(s, lambda c: (0,) * len(s))
    wspec = lambda k: pl.BlockSpec((width, block), lambda c, k=k: (0, k * steps + c))
    bspec = lambda k: pl.BlockSpec((1, block), lambda c, k=k: (0, k * steps + c))
    sd = jax.ShapeDtypeStruct
    return pl.pallas_call(
        enter_kernel, grid=(steps,),
        in_specs=[pl.BlockSpec(memory_space=pltpu.SMEM), whole(rows, width), whole(PRE, width), whole(1, width), whole(1, width),
                  wspec(0), wspec(1), wspec(2), bspec(0), bspec(1), bspec(2), pl.BlockSpec((12, block), lambda c: (0, c))],
        out_specs=[pl.BlockSpec((block // LANES, rows, LANES), lambda c: (c, 0, 0)), pl.BlockSpec((rows, block), lambda c: (0, c)),
                   pl.BlockSpec((3, PRE + rows, block), lambda c: (0, 0, c)), whole(rows, width)],
        out_shape=[sd((nb, rows, LANES), BF16), sd((rows, width), BF16), sd((3, PRE + rows, width), BF16), sd((rows, width), BF16)],
        scratch_shapes=[pltpu.VMEM((PRE + rows, width), BF16), pltpu.VMEM((3, PRE + rows, block), F32)],
        cost_estimate=cost(6 * rows * width * width, 14 << 20),
        compiler_params=pltpu.CompilerParams(vmem_limit_bytes=GRANT), name="enter")(
            first, x, before, gain, bias, weight, weight, weight, in_bias, in_bias, in_bias, taps)

POST = 16

def leave_kernel(ginner, ggate, ggate_after, proj, proj_after, taps, gproj, sums, pbuf, gbuf):
    rows = ggate.shape[0]
    cb = ggate.shape[1]
    for k in range(3):
        pbuf[k, : PRE + rows, :] = proj[k].astype(F32)
        pbuf[k, PRE + rows :, :] = proj_after[k].astype(F32)
    tap = lambda j, k: taps[3 * j + k : 3 * j + k + 1, :]

    def lags(k, start, size):
        p = pbuf[k, pl.ds(start + (PRE - 8), size + 8), :]
        return [p[6 + j : 6 + j + size] for j in range(3)]

    def grads(start, size, g0):
        gi = jnp.concatenate([ginner[j, pl.ds(start, size), :] for j in range(cb // LANES)], axis=1).astype(F32)
        p1 = lags(1, start, size)
        p2 = lags(2, start, size)
        s1 = taps[10:11, :] + sum(tap(j, 1) * p1[j] for j in range(3))
        s2 = taps[11:12, :] + sum(tap(j, 2) * p2[j] for j in range(3))
        return (g0, gi * s2, gi * s1), p1, p2

    def first(r, carry):
        g, p1, p2 = grads(r.start, r.size, ggate[r, :].astype(F32))
        p0 = lags(0, r.start, r.size)
        out = []
        for k in range(3):
            gbuf[k, r, :] = g[k]
        for j in range(3):
            for k, p in enumerate((p0, p1, p2)):
                out.append(carry[3 * j + k] + fold8(g[k] * p[j]))
        for k in range(3):
            out.append(carry[9 + k] + fold8(g[k]))
        return tuple(out)

    acc = rows_loop(rows, CHUNK, first)(tuple(jnp.zeros((8, cb), F32) for _ in range(12)))
    for i in range(12):
        sums[i : i + 1, :] = jnp.sum(acc[i], axis=0, keepdims=True)
    g, _, _ = grads(rows, POST, ggate_after[...].astype(F32))
    for k in range(3):
        gbuf[k, rows:, :] = g[k]

    def second(r, carry):
        out = []
        for k in range(3):
            g = gbuf[k, pl.ds(r.start, r.size + 8), :]
            v = sum(tap(j, k) * g[2 - j : 2 - j + r.size] for j in range(3)).astype(BF16)
            gproj[k, 0, r, :] = v
            out.append(carry[k] + fold8(v.astype(F32)))
        return tuple(out)

    acc = rows_loop(rows, CHUNK, second)(tuple(jnp.zeros((8, cb), F32) for _ in range(3)))
    for i in range(3):
        sums[12 + i : 13 + i, :] = jnp.sum(acc[i], axis=0, keepdims=True)
    sums[15:16, :] = jnp.zeros((1, cb), F32)

def leave(ginner, ggate, ggate_after, proj, proj_after, taps, block=256):
    rows, width = ggate.shape
    steps = width // block
    sd = jax.ShapeDtypeStruct
    return pl.pallas_call(
        leave_kernel, grid=(steps,),
        in_specs=[pl.BlockSpec((block // LANES, rows + POST, LANES), lambda c: (c, 0, 0)),
                  pl.BlockSpec((rows, block), lambda c: (0, c)), pl.BlockSpec((POST, block), lambda c: (0, c)),
                  pl.BlockSpec((3, PRE + rows, block), lambda c: (0, 0, c)), pl.BlockSpec((3, POST, block), lambda c: (0, 0, c)),
                  pl.BlockSpec((12, block), lambda c: (0, c))],
        out_specs=[pl.BlockSpec((3, 1, rows, block), lambda c: (0, c, 0, 0)), pl.BlockSpec((16, block), lambda c: (0, c))],
        out_shape=[sd((3, steps, rows, block), BF16), sd((16, width), F32)],
        scratch_shapes=[pltpu.VMEM((3, PRE + rows + POST, block), F32), pltpu.VMEM((3, rows + POST, block), F32)],
        cost_estimate=cost(60 * rows * width, 9 << 20),
        compiler_params=pltpu.CompilerParams(vmem_limit_bytes=GRANT), name="leave")(ginner, ggate, ggate_after, proj, proj_after, taps)

def tokens_kernel(gproj, weight, x, gres, gain, out, sums, acc):
    k = pl.program_id(0)
    rows, width = x.shape
    unit = gproj.shape[3]
    part = sum(mxu_nt(gproj[0, j], weight[:, j * unit : (j + 1) * unit]) for j in range(gproj.shape[1]))
    @pl.when(k == 0)
    def _():
        acc[...] = part
    @pl.when(k > 0)
    def _():
        acc[...] += part
    @pl.when(k == pl.num_programs(0) - 1)
    def _():
        def body(r, carry):
            a, b = carry
            v = x[r, :].astype(F32)
            v = v - jnp.mean(v, axis=-1, keepdims=True)
            s = lax.rsqrt(jnp.mean(v * v, axis=-1, keepdims=True) + EPSILON)
            n = v * s
            d = acc[r, :]
            a += fold8(d * n)
            b += fold8(d)
            e = d * gain[...]
            m1 = jnp.mean(e, axis=-1, keepdims=True)
            m2 = jnp.mean(e * n, axis=-1, keepdims=True)
            out[r, :] = gres[r, :].astype(F32) + (e - m1 - n * m2) * s
            return a, b
        zero = jnp.zeros((8, width), F32)
        a, b = rows_loop(rows, CHUNK, body)((zero, zero))
        sums[0:1, :] = jnp.sum(a, axis=0, keepdims=True)
        sums[1:2, :] = jnp.sum(b, axis=0, keepdims=True)

def tokens_back(gproj, weight, x, gres, gain):
    rows, width = x.shape
    whole = lambda *s: pl.BlockSpec(s, lambda k: (0,) * len(s))
    sd = jax.ShapeDtypeStruct
    return pl.pallas_call(
        tokens_kernel, grid=(3,),
        in_specs=[pl.BlockSpec((1,) + gproj.shape[1:], lambda k: (k, 0, 0, 0)), pl.BlockSpec((width, width), lambda k: (0, k)),
                  whole(rows, width), whole(rows, width), whole(1, width)],
        out_specs=[whole(rows, width), whole(2, width)],
        out_shape=[sd((rows, width), F32), sd((2, width), F32)],
        scratch_shapes=[pltpu.VMEM((rows, width), F32)],
        cost_estimate=cost(6 * rows * width * width, 14 << 20),
        compiler_params=pltpu.CompilerParams(vmem_limit_bytes=GRANT), name="tokens_back")(gproj, weight, x, gres, gain)


def wgrad_kernel(row_order, units, *refs, sides, lefts, rights, held, mode):
    acc = None
    for side in range(sides):
        refs_left, refs = refs[:lefts], refs[lefts:]
        left = jnp.concatenate([r[...] for r in refs_left], axis=1)
        refs_right, refs = refs[:rights], refs[rights:]
        right = jnp.concatenate([r[0] for r in refs_right], axis=1)
        part = mxu_tn(left, right)
        acc = part if acc is None else acc + part
    outs = refs[held:]
    count, height, _ = outs[0].shape
    width = acc.shape[1] // 2
    value = acc.reshape(count, height, acc.shape[1]).astype(BF16)
    if mode == "x":
        outs[0][...] = value[..., :width]
        outs[1][...] = value[..., width:]
    if mode == "y":
        early = pl.program_id(0) < pl.num_programs(0) // 2

        @pl.when(early)
        def _():
            place = 0
            for piece in outs[:-1]:
                piece[...] = value[..., place : place + piece.shape[2]]
                place += piece.shape[2]

        @pl.when(jnp.logical_not(early))
        def _():
            outs[-1][...] = value


def wgrad(left, right, row_order, units, unit, mode, each, held=(), tall=None, start=0, pieces=(1,)):
    rows, m = left[0].shape
    sides, blocks, count = len(left), row_order.shape[0], units[0].shape[0]
    height = m // blocks
    tall = tall or height
    at = start // height
    wide = count * unit
    half = wide // 2
    if height % LANES:
        left = [v.reshape(rows, blocks, height)[:, row_order].reshape(rows, m) for v in left]
        each = max(each, LANES // height)
        left_specs = [pl.BlockSpec((rows, each * height), lambda i, r, u: (0, i))]
    else:
        left_specs = [pl.BlockSpec((rows, height), lambda i, r, u, q=q: (0, r[i * each + q])) for q in range(each)]
    lefts, steps = len(left_specs), blocks // each
    in_specs, args = [], []
    for side in range(sides):
        per, base = right[side].shape[2] // unit, side * count
        in_specs += left_specs + [
            pl.BlockSpec((1, rows, unit), lambda i, r, u, j=base + j, per=per: (u[j] // per, 0, u[j] % per))
            for j in range(count)
        ]
        args += [left[side]] * lefts + [right[side]] * count
    aliases = {2 + len(args) + i: i for i in range(len(held))}
    in_specs += [pl.BlockSpec(memory_space=pl.ANY)] * len(held)
    args += list(held)
    full = lambda w: ((blocks, tall, w), pl.BlockSpec((each, height, w), lambda i, r, u: (i, at, 0)))
    first = ((blocks // 2, tall, wide), lambda i: jnp.minimum(i, steps // 2 - 1))
    second = ((blocks // 2, tall, wide), lambda i: jnp.maximum(i - steps // 2, 0))
    part = lambda s, w: ((s[0][0], tall, w), pl.BlockSpec((each, height, w), lambda i, r, u: (s[1](i), at, 0)))
    outs = {
        "x": [full(half)] * 2,
        "y": [part(first, wide * p // sum(pieces)) for p in pieces] + [part(second, wide)],
    }[mode]
    return pl.pallas_call(
        functools.partial(wgrad_kernel, sides=sides, lefts=lefts, rights=count, held=len(held), mode=mode),
        grid_spec=pltpu.PrefetchScalarGridSpec(
            num_scalar_prefetch=2, grid=(steps,), in_specs=in_specs, out_specs=[o[1] for o in outs]
        ),
        out_shape=[jax.ShapeDtypeStruct(o[0], BF16) for o in outs],
        input_output_aliases=aliases,
        cost_estimate=cost(2 * sides * rows * m * wide, 2 * sides * (rows * m + rows * wide) + 4 * m * wide),
        compiler_params=pltpu.CompilerParams(vmem_limit_bytes=GRANT),
        name="wgrad",
    )(row_order, jnp.concatenate(units), *args)


def on_device(
    tokens,
    cotangent,
    norm1_gain,
    norm1_bias,
    in_weight,
    in_bias,
    short_weight,
    short_bias,
    filter_in,
    filter_in_bias,
    sine_freq,
    filter_out,
    decay_rates,
    filter_bias,
    out_weight,
    out_bias,
    norm2_gain,
    norm2_bias,
    up_weight,
    up_bias,
    down_weight,
    down_bias,
):
    width = in_weight.shape[0]
    ff = up_weight.shape[1]
    rows = tokens.shape[1]
    seq = lax.axis_size("seq")
    me = lax.axis_index("seq")
    length = rows * seq
    chans = width // seq
    down_shift = [(i + 1, i) for i in range(seq - 1)]

    x, dy = tokens[0], cotangent[0]
    mine = jnp.concatenate([short_weight.reshape(9 * chans), short_bias.reshape(3 * chans), x[rows - 2 :].reshape(-1).astype(F32)])
    used = mine.size
    mine = jnp.pad(mine, (0, -used % (8 * LANES)))
    got = lax.all_to_all(
        jnp.broadcast_to(mine.reshape(1, -1, LANES), (seq, mine.size // LANES, LANES)),
        "seq", split_axis=0, concat_axis=0, tiled=True,
    ).reshape(seq, -1)
    all_taps = got[:, : 12 * chans].reshape(seq, 12, chans).transpose(1, 0, 2).reshape(12, width)
    before = pick(got, jnp.maximum(me - 1, 0), 0)[12 * chans : used].reshape(2, width)
    before = jnp.concatenate([jnp.zeros((PRE - 2, width), BF16), before.astype(BF16)], axis=0)

    row = lambda v: v[None, :]
    first = me.reshape(1).astype(jnp.int32)
    fast = length // BLOCK <= 64
    tables = make_tables(length) if fast else None
    before, all_taps, tables = lax.optimization_barrier((before, all_taps, tables))
    inner, gate, proj, normed = enter(
        first, x, before, row(norm1_gain), row(norm1_bias), in_weight, row(in_bias), all_taps
    )
    proj_after = lax.ppermute(proj[:, PRE : PRE + POST], "seq", down_shift)

    def to_channels(value):
        if chans != LANES:
            value = value.transpose(1, 0, 2).reshape(rows, seq, chans).transpose(1, 0, 2)
        got = lax.all_to_all(value, "seq", split_axis=0, concat_axis=0, tiled=True)
        return got.reshape(length, chans)

    def to_tokens(value):
        got = lax.all_to_all(value, "seq", split_axis=0, concat_axis=0, tiled=True)
        if chans != LANES:
            got = got.transpose(1, 0, 2).reshape(got.shape[1], width // LANES, LANES).transpose(1, 0, 2)
        return got

    inner_chan = to_channels(inner)

    mixer = (FastMixer if fast else PlainMixer)(length, chans, seq, tables)
    features = position_features(length)
    hidden_pre = jnp.dot(filter_in.T, features, precision=HIGH) + filter_in_bias[:, None]
    phase = sine_freq[:, None] * hidden_pre
    hidden = jnp.sin(phase)
    window = jnp.exp(-features[0][:, None] * decay_rates[None, :])
    kernel = jnp.einsum("hn,hc->nc", hidden, filter_out, precision=HIGH) * window
    kernel_spec = mixer.spectrum(kernel)

    conv_chan, inner_spec = mixer.convolve(inner_chan, kernel_spec, filter_bias, False, 0)
    normed_x = swap(normed, "dp", 2)
    conv_chan, proj_after, normed_x = tie(conv_chan, proj_after, normed_x)
    normed_all = [normed, swap(normed, "dp", 1), normed_x, swap(normed_x, "dp", 1)]
    conv = to_tokens(conv_chan)
    dy_other = swap(dy, "dp", 1)
    grad_act, dy_sum = back_act(dy, down_weight)
    conv, dy_other, normed_all = tie(conv, dy_other, normed_all)
    act, gup, gup_sum, resid, normed2, mixed, grad_attn, grad_conv, grad_gate, mid_sums = middle(
        conv, gate, x, dy, grad_act, out_weight, row(out_bias), row(norm2_gain), row(norm2_bias), up_weight, row(up_bias)
    )
    grad_chan = to_channels(grad_conv)
    gate_after = lax.ppermute(grad_gate[:POST], "seq", down_shift)

    bits = seq_bits()
    order = block_order(bits)
    up_bits = [bits[1], bits[0]] + bits[2:]
    up_order = block_order(up_bits)
    unit = width // 4
    tall = (ff + width) // seq
    wide = ff // seq

    pair = lambda value: (value, swap(value, "dp", 1))
    near_units, near_up = chip_units(dy[None], unit, (2, 0)), chip_units(gup[None], ff // 4, (2, 0))
    dy_pair, act_pair = (dy[None], dy_other[None]), pair(act)
    mixed_pair, attn_pair = pair(mixed), pair(grad_attn[None])
    gup_pair, normed2_pair = pair(gup[None]), pair(normed2)
    parts = wgrad(act_pair, dy_pair, order, [near_units] * 2, unit, "x", 2, tall=tall)
    each = 8 if seq == 8 else 4
    tall_send, tall_kept = wgrad(
        mixed_pair, attn_pair, order, [near_units] * 2, unit, "x", each, held=parts, tall=tall, start=wide
    )
    tall_got = swap(tall_send, "dp", 2)
    grad_chan, tall_kept = tie(grad_chan, tall_kept)
    grad_inner_chan, grad_spec = mixer.convolve(grad_chan, kernel_spec, filter_bias, True, POST)
    gup_pair, normed2_pair, grad_inner_chan, gate_after = tie(gup_pair, normed2_pair, grad_inner_chan, gate_after)
    grad_inner = to_tokens(grad_inner_chan)
    *up_sends, up_kept = wgrad(normed2_pair, gup_pair, up_order, [near_up] * 2, ff // 4, "y", 4, pieces=(1, 2, 1))

    grad_filter_out, grad_filter_in, filter_sums, grad_filter_bias = mixer.filter_grad(
        grad_spec, inner_spec, grad_chan, inner_chan, (features, hidden_pre, phase, hidden, window, filter_out)
    )
    grad_freq = filter_sums[0]
    grad_filter_in_bias = filter_sums[1] * sine_freq
    grad_filter_in = grad_filter_in * sine_freq[None, :]

    grad_inner, grad_filter_out, up_sends = tie(grad_inner, grad_filter_out, up_sends)
    up_gots = [swap(up_sends[0], "seq", up_bits[0])]
    grad_proj, leave_sums = leave(grad_inner, grad_gate, gate_after, proj, proj_after, all_taps)
    grad_proj, tall_got, up_gots[0] = tie(grad_proj, tall_got, up_gots[0])
    tall_send, tall_kept = halve(tall_kept, tall_got)
    tall_got = swap(tall_send, "seq", bits[0])
    proj_units = grad_proj.reshape((-1,) + grad_proj.shape[2:])
    proj_all = lax.all_to_all(proj_units, "dp", split_axis=0, concat_axis=0, tiled=True)
    up_gots.append(swap(up_sends[1], "seq", up_bits[0]))
    grad_tokens, token_sums = tokens_back(grad_proj, in_weight, x, grad_attn, row(norm1_gain))

    shared = (token_sums, leave_sums, mid_sums, gup_sum, dy_sum, grad_filter_in, grad_filter_in_bias, grad_freq)
    channel = (grad_filter_out, grad_filter_bias)
    packed, extra = pack(shared), pack(channel)
    rows_shared = packed.shape[0]
    packed = jnp.concatenate([packed, extra], axis=0)
    packed = packed + swap(packed, "dp", 1)
    packed, up_gots[1], proj_all = tie(packed, up_gots[1], proj_all)
    packed, extra = packed[:rows_shared], packed[rows_shared:]
    up_gots.append(swap(up_sends[2], "seq", up_bits[0]))
    small = swap(packed, "seq", bits[0])
    dp_me = lax.axis_index("dp")
    share = proj_units.shape[0] // 4
    ahead = jnp.arange(share, dtype=jnp.int32)
    in_units = [jnp.bitwise_xor(dp_me, w) * share + ahead for w in range(4)]
    in_send, in_kept = wgrad(normed_all, [proj_all] * 4, order, in_units, proj_units.shape[2], "y", 4)

    in_send, small, tall_got, up_gots, act = tie(in_send, small, tall_got, up_gots, act)
    in_got = swap(in_send, "seq", bits[0])
    cut = ff // 4
    part = up_gots[1].shape[2] // 2
    up_send = add(up_kept[..., :cut], jnp.concatenate([up_gots[0], up_gots[1][..., :part]], axis=2))
    up_got = swap(up_send, "dp", 2)
    tall_send, tall_kept = halve(tall_kept, tall_got)
    tall_got = swap(tall_send, "seq", bits[1])
    both = jnp.concatenate([packed + small, extra], axis=0)
    small = swap(both, "dp", 2)
    block_output = block_out(act, down_weight, resid, row(down_bias))
    up_kept = add(up_kept[..., cut:], jnp.concatenate([up_gots[1][..., part:], up_gots[2]], axis=2))

    in_got, tall_got, block_output, up_kept = tie(in_got, tall_got, block_output, up_kept)
    in_send, in_kept = halve(in_kept, in_got)
    in_got = swap(in_send, "seq", bits[1])
    tall_send, tall_kept = halve(tall_kept, tall_got)
    tall_got = swap(tall_send, "seq", bits[2])

    in_got, up_got, small = tie(in_got, up_got, small)
    in_send, in_kept = halve(in_kept, in_got)
    in_got = swap(in_send, "seq", bits[2])
    up_send, up_kept = halve(up_kept, up_got)
    up_got = swap(up_send, "seq", up_bits[1])
    both = both + small
    packed, extra = both[:rows_shared], both[rows_shared:]
    small = swap(packed, "seq", bits[1])

    for i in range(2, len(bits)):
        up_got, small = tie(up_got, small)
        if i > 2:
            in_got, tall_got = tie(in_got, tall_got)
            in_send, in_kept = halve(in_kept, in_got)
            in_got = swap(in_send, "seq", bits[i])
            tall_send, tall_kept = halve(tall_kept, tall_got)
            tall_got = swap(tall_send, "seq", bits[i])
        up_send, up_kept = halve(up_kept, up_got)
        up_got = swap(up_send, "seq", up_bits[i])
        packed = packed + small
        small = swap(packed, "seq", bits[i])
    grad_up, packed = last(up_kept, up_got), packed + small
    grad_in, both = last(in_kept, in_got), last(tall_kept, tall_got)
    grad_down, grad_out_weight = both[:wide], both[wide:]
    channel = unpack(extra, channel)
    shared = unpack(packed, shared)
    token_sums, leave_sums, mid_sums, gup_sum, dy_sum = shared[:5]
    own = lax.dynamic_slice_in_dim(leave_sums[:12], me * chans, chans, 1)
    return (
        block_output[None],
        grad_tokens[None],
        token_sums[0],
        token_sums[1],
        grad_in,
        leave_sums[12:15].reshape(-1),
        own[:9].reshape(3, 3, chans),
        own[9:],
        shared[5],
        shared[6],
        shared[7],
        channel[0],
        channel[1],
        grad_out_weight,
        mid_sums[2],
        mid_sums[0],
        mid_sums[1],
        grad_up,
        gup_sum[0],
        grad_down,
        dy_sum[0],
    )


def solution(mesh):
    everywhere, by_token, by_rows = P(), P("dp", "seq", None), P("seq", "dp")
    taps, shift, chan = P(None, None, "seq"), P(None, "seq"), P("seq")
    in_specs = (by_token,) * 2 + (everywhere,) * 4 + (taps, shift) + (everywhere,) * 3
    in_specs += (shift, chan, chan) + (everywhere,) * 8
    out_specs = (by_token, by_token, everywhere, everywhere, by_rows, everywhere, taps, shift)
    out_specs += (everywhere,) * 3 + (shift, chan, by_rows) + (everywhere,) * 3
    out_specs += (by_rows, everywhere, by_rows, everywhere)
    return jax.shard_map(
        on_device, mesh=mesh, in_specs=in_specs, out_specs=out_specs, check_vma=False
    )
```

```python
import functools
import math

import jax
import jax.numpy as jnp
import numpy as np
from jax import lax
from jax.experimental import pallas as pl
from jax.experimental.pallas import tpu as pltpu
from jax.sharding import PartitionSpec as P

EMB = 33
HIGH = lax.Precision.HIGHEST
EPSILON = 1e-05
BLOCK = 128
LANES = 128
ROWS = 16
CHUNK = 128
GRANT = 60 << 20
COST = 8
F32 = jnp.float32
BF16 = jnp.bfloat16


def times_root(re, im, num, den):
    num = num % den
    if num == 0:
        return re, im
    if 4 * num == den:
        return -im, re
    if 2 * num == den:
        return -re, -im
    if 4 * num == 3 * den:
        return im, -re
    angle = 2.0 * math.pi * num / den
    cos, sin = math.cos(angle), math.sin(angle)
    if abs(abs(cos) - abs(sin)) < 1e-12:
        sc, ss = (1.0 if cos > 0 else -1.0), (1.0 if sin > 0 else -1.0)
        root = abs(cos)
        return root * (sc * re - ss * im), root * (sc * im + ss * re)
    return re * cos - im * sin, im * cos + re * sin


def small_fft(re, im, sign):
    count = len(re)
    if count == 1:
        return re, im
    if count == 2:
        return [re[0] + re[1], re[0] - re[1]], [im[0] + im[1], im[0] - im[1]]
    even_re, even_im = small_fft(re[0::2], im[0::2], sign)
    odd_re, odd_im = small_fft(re[1::2], im[1::2], sign)
    low_re, low_im, top_re, top_im = [], [], [], []
    for k in range(count // 2):
        tr, ti = times_root(odd_re[k], odd_im[k], sign * k, count)
        low_re.append(even_re[k] + tr)
        low_im.append(even_im[k] + ti)
        top_re.append(even_re[k] - tr)
        top_im.append(even_im[k] - ti)
    return low_re + top_re, low_im + top_im


def blocks_forward(source, target, count):
    def body(step, carry):
        row = pl.multiple_of(step * ROWS, ROWS)
        re, im = [], []
        for a in range(count):
            value = source[a, pl.ds(row, ROWS), :].astype(F32)
            angle = 2.0 * math.pi * a / (4 * count)
            re.append(value * math.cos(angle))
            im.append(value * math.sin(angle))
        re, im = small_fft(re, im, -1)
        for k in range(count):
            target[k, pl.ds(row, ROWS), :] = re[k].astype(BF16)
            target[k, pl.ds(BLOCK + row, ROWS), :] = im[k].astype(BF16)
        return carry

    lax.fori_loop(0, BLOCK // ROWS, body, 0)


def blocks_inverse(source, emit, count):
    def body(step, carry):
        row = pl.multiple_of(step * ROWS, ROWS)
        re = [source[k, pl.ds(row, ROWS), :] for k in range(count)]
        im = [source[k, pl.ds(BLOCK + row, ROWS), :] for k in range(count)]
        re, im = small_fft(re, im, 1)
        for a in range(count):
            angle = 2.0 * math.pi * a / (4 * count)
            emit(a, row, re[a] * math.cos(angle) + im[a] * math.sin(angle))
        return carry

    lax.fori_loop(0, BLOCK // ROWS, body, 0)


def cost(flops, bytes_accessed):
    return pl.CostEstimate(flops=flops // COST, bytes_accessed=bytes_accessed // COST, transcendentals=0)


def mxu(left, right):
    return jnp.dot(left, right, preferred_element_type=F32)

def mxu_nt(left, right):
    return lax.dot_general(left, right, (((1,), (1,)), ((), ())), preferred_element_type=F32)

def mxu_tn(left, right):
    return lax.dot_general(left, right, (((0,), (0,)), ((), ())), preferred_element_type=F32)

def rows_loop(total, chunk, body, unroll=1):
    def step(i, carry):
        return body(pl.ds(pl.multiple_of(i * chunk, chunk), chunk), carry)
    return lambda init: lax.fori_loop(0, total // chunk, step, init, unroll=unroll)

def fold8(v):
    return jnp.sum(v.reshape(v.shape[0] // 8, 8, v.shape[1]), axis=0)


def table_kernel(alpha_cos, alpha_sin, beta_cos, beta_sin, forward, inverse, *, scale):
    cb, sb = beta_cos[...], beta_sin[...]
    for i in range(forward.shape[0]):
        ca, sa = alpha_cos[i], alpha_sin[i]
        cos = ca * cb - sa * sb
        sin = sa * cb + ca * sb
        low_cos, low_sin = cos.astype(BF16), sin.astype(BF16)
        forward[i, :BLOCK, :BLOCK] = low_cos
        forward[i, :BLOCK, BLOCK:] = low_sin
        forward[i, BLOCK:, :BLOCK] = -low_sin
        forward[i, BLOCK:, BLOCK:] = low_cos
        low_cos, low_sin = (cos.T * scale).astype(BF16), (sin.T * scale).astype(BF16)
        inverse[i, :BLOCK, :BLOCK] = low_cos
        inverse[i, :BLOCK, BLOCK:] = -low_sin
        inverse[i, BLOCK:, :BLOCK] = low_sin
        inverse[i, BLOCK:, BLOCK:] = low_cos


def make_tables(length):
    count = length // BLOCK
    alpha = 2.0 * np.pi * np.arange(BLOCK)[None, :] * (np.arange(count)[:, None] - 0.25) / length
    beta = 2.0 * np.pi * ((np.arange(BLOCK)[:, None] * np.arange(BLOCK)[None, :]) % BLOCK) / BLOCK
    alpha = alpha[:, None, :]
    consts = [jnp.asarray(f(v), F32) for v in (alpha, beta) for f in (np.cos, np.sin)]
    each = math.gcd(count, 4)
    row = pl.BlockSpec((each, 1, BLOCK), lambda i: (i, 0, 0))
    flat = pl.BlockSpec((BLOCK, BLOCK), lambda i: (0, 0))
    out = pl.BlockSpec((each, 2 * BLOCK, 2 * BLOCK), lambda i: (i, 0, 0))
    shape = jax.ShapeDtypeStruct((count, 2 * BLOCK, 2 * BLOCK), BF16)
    return pl.pallas_call(
        functools.partial(table_kernel, scale=1.0 / length),
        grid=(count // each,),
        in_specs=[row, row, flat, flat],
        out_specs=[out, out],
        out_shape=[shape, shape],
        cost_estimate=cost(16 * count * BLOCK * BLOCK, 8 << 20),
        name="tables",
    )(*consts)


def split_spec(value):
    return value[:BLOCK], value[BLOCK:]


def turn_back(prod, inverse, back):
    def body(k, carry):
        back[k] = mxu(inverse[k], prod[k])
        return carry

    lax.fori_loop(0, prod.shape[0], body, 0, unroll=8)


def spectrum_kernel(signal, forward, spectrum, mid):
    (signal, have_signal), (forward, have_forward) = signal, forward
    count = signal.shape[0]
    have_signal()
    blocks_forward(signal, mid, count)
    have_forward()

    def body(k, carry):
        spectrum[k] = mxu(forward[k], mid[k]).astype(BF16)
        return carry

    lax.fori_loop(0, count, body, 0, unroll=8)


def conv_kernel(signal, kernel_spec, bias, forward, inverse, result, spectrum, mid, prod, back, *, conjugate):
    (signal, have_signal), (kernel_spec, have_spec), (bias, have_bias) = signal, kernel_spec, bias
    (forward, have_forward), (inverse, have_inverse) = forward, inverse
    count = signal.shape[0]
    have_signal()
    blocks_forward(signal, mid, count)
    have_spec()
    have_bias()
    have_forward()

    def body(k, carry):
        spec = mxu(forward[k], mid[k])
        spectrum[k] = spec.astype(BF16)
        a_re, a_im = split_spec(spec)
        b_re, b_im = split_spec(kernel_spec[k].astype(F32))
        if conjugate:
            b_im = -b_im
        prod[k, :BLOCK, :] = (a_re * b_re - a_im * b_im).astype(BF16)
        prod[k, BLOCK:, :] = (a_re * b_im + a_im * b_re).astype(BF16)
        return carry

    lax.fori_loop(0, count, body, 0, unroll=8)
    have_inverse()
    turn_back(prod, inverse, back)
    gain = bias[...]
    devices, rows, _ = result.shape
    per = count // devices
    size = per * BLOCK

    def emit(a, row, value):
        direct = signal[a, pl.ds(row, ROWS), :].astype(F32) * gain
        result[a // per, pl.ds((a % per) * BLOCK + row, ROWS), :] = (value + direct).astype(result.dtype)

    blocks_inverse(back, emit, count)
    if rows > size:
        for j in range(devices - 1):
            result[j, size:, :] = result[j + 1, : rows - size, :]
        result[devices - 1, size:, :] = jnp.zeros((rows - size, result.shape[2]), result.dtype)


def filter_grad_kernel(
    grad_spec, signal_spec, grad, signal, inverse, window, hidden, slope, hidden_pre, features, filter_out,
    out_grad, in_grad, sums, bias_grad, prod, back, raw,
):
    (grad_spec, have_grad_spec), (signal_spec, have_signal_spec) = grad_spec, signal_spec
    count = grad_spec.shape[0]
    have_grad_spec()
    have_signal_spec()

    def body(k, carry):
        a_re, a_im = split_spec(grad_spec[k].astype(F32))
        b_re, b_im = split_spec(signal_spec[k].astype(F32))
        prod[k, :BLOCK, :] = (a_re * b_re + a_im * b_im).astype(BF16)
        prod[k, BLOCK:, :] = (a_im * b_re - a_re * b_im).astype(BF16)
        return carry

    lax.fori_loop(0, count, body, 0, unroll=2)
    for _, wait in (grad, signal, inverse, window, hidden, slope, hidden_pre, features, filter_out):
        wait()
    grad, signal, inverse, window, hidden, slope, hidden_pre, features, filter_out = (
        v[0] for v in (grad, signal, inverse, window, hidden, slope, hidden_pre, features, filter_out)
    )
    turn_back(prod, inverse, back)

    def emit(a, row, value):
        at = pl.ds(a * BLOCK + row, ROWS)
        raw[at, :] = (value * window[at, :]).astype(BF16)

    blocks_inverse(back, emit, count)

    def total(a, acc):
        return acc + fold8(grad[a].astype(F32) * signal[a].astype(F32))

    acc = lax.fori_loop(0, count, total, jnp.zeros((8, grad.shape[-1]), F32))
    bias_grad[...] = jnp.sum(acc, axis=0, keepdims=True)
    out_grad[...] = mxu(hidden[...], raw[...])
    turned = mxu_nt(filter_out[...], raw[...]) * slope[...]
    sums[...] = jnp.concatenate(
        [jnp.sum(turned * hidden_pre[...], axis=1, keepdims=True), jnp.sum(turned, axis=1, keepdims=True)], axis=1
    )
    in_grad[...] = mxu_nt(features[...], turned.astype(BF16))


def vmem_call(kernel, outs, scratch, args, name):
    count = len(args)

    def body(*refs):
        ins, rest = refs[:count], refs[count:]
        results, local = rest[: len(outs)], rest[len(outs) : len(outs) + len(scratch)]
        bufs, sems = rest[len(outs) + len(scratch) : -1], rest[-1]
        copies = [pltpu.make_async_copy(src, dst, sems.at[i]) for i, (src, dst) in enumerate(zip(ins, bufs))]
        for copy in copies:
            copy.start()
        kernel(*[(buf, copy.wait) for buf, copy in zip(bufs, copies)], *results, *local)

    scratch = list(scratch)
    held = [pltpu.VMEM(a.shape, a.dtype) for a in args]
    return pl.pallas_call(
        body,
        in_specs=[pl.BlockSpec(memory_space=pl.ANY)] * count,
        out_specs=[pl.BlockSpec(o.shape, lambda n=len(o.shape): (0,) * n) for o in outs],
        out_shape=outs,
        scratch_shapes=scratch + held + [pltpu.SemaphoreType.DMA((count,))],
        cost_estimate=cost(4 << 30, 16 << 20),
        compiler_params=pltpu.CompilerParams(vmem_limit_bytes=GRANT),
        name=name,
    )(*args)


class FastMixer:
    def __init__(self, length, channels, devices, tables):
        self.count = length // BLOCK
        self.channels = channels
        self.devices = devices
        self.forward, self.inverse = tables
        self.mid = pltpu.VMEM((self.count, 2 * BLOCK, channels), BF16)
        self.back = pltpu.VMEM((self.count, 2 * BLOCK, channels), F32)
        self.spec = jax.ShapeDtypeStruct((self.count, 2 * BLOCK, channels), BF16)

    def blocked(self, value):
        return value.reshape(self.count, BLOCK, self.channels)

    def spectrum(self, signal):
        args = (self.blocked(signal), self.forward)
        return vmem_call(spectrum_kernel, [self.spec], [self.mid], args, "spectrum")[0]

    def convolve(self, signal, kernel_spec, bias, conjugate, extra):
        rows = self.count * BLOCK // self.devices + extra
        out = jax.ShapeDtypeStruct((self.devices, rows, self.channels), BF16)
        return vmem_call(
            functools.partial(conv_kernel, conjugate=conjugate),
            [out, self.spec],
            [self.mid, self.mid, self.back],
            (self.blocked(signal), kernel_spec, bias[None, :], self.forward, self.inverse),
            "correlate" if conjugate else "convolve",
        )

    def filter_grad(self, grad_spec, signal_spec, grad, signal, filt):
        features, hidden_pre, phase, hidden, window, filter_out = filt
        units = hidden.shape[0]
        outs = [
            jax.ShapeDtypeStruct((units, self.channels), F32),
            jax.ShapeDtypeStruct((48, units), F32),
            jax.ShapeDtypeStruct((units, 2), F32),
            jax.ShapeDtypeStruct((1, self.channels), F32),
        ]
        padded = jnp.pad(features.astype(BF16), ((0, 48 - EMB), (0, 0)))
        raw = pltpu.VMEM((self.count * BLOCK, self.channels), BF16)
        out_grad, in_grad, sums, bias_grad = vmem_call(
            filter_grad_kernel,
            outs,
            [self.mid, self.back, raw],
            (grad_spec, signal_spec, self.blocked(grad), self.blocked(signal), self.inverse, window)
            + (hidden.astype(BF16), jnp.cos(phase), hidden_pre, padded, filter_out.astype(BF16)),
            "filter_grad",
        )
        return out_grad, in_grad[:EMB], sums.T, bias_grad[0]


class PlainMixer:
    def __init__(self, length, channels, devices, tables):
        self.length = length
        self.devices = devices
        self.channels = channels
        full = 2 * length
        p = 2
        while p * p * 2 <= full and full % (p * 2) == 0:
            p = p * 2
        q = full // p
        self.p, self.q = p, q
        ip, iq = jnp.arange(p, dtype=jnp.int32), jnp.arange(q, dtype=jnp.int32)
        tp = 2.0 * math.pi * (ip[:, None] * ip[None, :] % p).astype(F32) / p
        tq = 2.0 * math.pi * (iq[:, None] * iq[None, :] % q).astype(F32) / q
        tt = 2.0 * math.pi * (ip[:, None] * iq[None, :] % full).astype(F32) / full
        self.cp, self.sp, self.cq, self.sq = jnp.cos(tp), jnp.sin(tp), jnp.cos(tq), jnp.sin(tq)
        self.ct, self.st = jnp.cos(tt), jnp.sin(tt)

    def spectrum(self, signal):
        half = self.p // 2
        x = signal.astype(F32).T.reshape(self.channels, half, self.q)
        ein = functools.partial(jnp.einsum, precision=HIGH)
        re = ein("kn,cnq->ckq", self.cp[:, :half], x)
        im = -ein("kn,cnq->ckq", self.sp[:, :half], x)
        re, im = re * self.ct + im * self.st, im * self.ct - re * self.st
        return (
            ein("ckn,nm->ckm", re, self.cq) + ein("ckn,nm->ckm", im, self.sq),
            ein("ckn,nm->ckm", im, self.cq) - ein("ckn,nm->ckm", re, self.sq),
        )

    def back(self, re, im):
        half = self.p // 2
        ein = functools.partial(jnp.einsum, precision=HIGH)
        br = ein("ckm,nm->ckn", re, self.cq) - ein("ckm,nm->ckn", im, self.sq)
        bi = ein("ckm,nm->ckn", im, self.cq) + ein("ckm,nm->ckn", re, self.sq)
        br, bi = br * self.ct - bi * self.st, bi * self.ct + br * self.st
        out = ein("nk,ckq->cnq", self.cp[:half], br) - ein("nk,ckq->cnq", self.sp[:half], bi)
        return (out.reshape(self.channels, self.length) / (2 * self.length)).T

    def convolve(self, signal, kernel_spec, bias, conjugate, extra):
        a_re, a_im = self.spectrum(signal)
        b_re, b_im = kernel_spec
        if conjugate:
            b_im = -b_im
        out = self.back(a_re * b_re - a_im * b_im, a_re * b_im + a_im * b_re)
        out = out + signal.astype(F32) * bias[None, :]
        out = jnp.pad(out.astype(BF16), ((0, extra), (0, 0)))
        rows = self.length // self.devices
        parts = [out[j * rows : (j + 1) * rows + extra] for j in range(self.devices)]
        return jnp.stack(parts), (a_re, a_im)

    def filter_grad(self, grad_spec, signal_spec, grad, signal, filt):
        features, hidden_pre, phase, hidden, window, filter_out = filt
        a_re, a_im = grad_spec
        b_re, b_im = signal_spec
        raw = self.back(a_re * b_re + a_im * b_im, a_im * b_re - a_re * b_im) * window
        out_grad = jnp.einsum("hn,nc->hc", hidden, raw, precision=HIGH)
        turned = jnp.einsum("nc,hc->hn", raw, filter_out, precision=HIGH) * jnp.cos(phase)
        in_grad = jnp.einsum("en,hn->eh", features, turned, precision=HIGH)
        sums = jnp.stack([jnp.sum(turned * hidden_pre, axis=1), jnp.sum(turned, axis=1)])
        return out_grad, in_grad, sums, jnp.sum(grad.astype(F32) * signal.astype(F32), axis=0)


def position_features(length):
    steps = jnp.arange(length, dtype=F32)
    scaled = steps / (length - 1)
    angles = 2.0 * math.pi * steps / length
    bands = (EMB - 1) // 2
    freqs = 0.0001 + jnp.arange(bands, dtype=F32) * (bands - 1 - 0.0001) / (bands - 1)
    phase = freqs[:, None] * angles[None, :]
    return jnp.concatenate([scaled[None, :], jnp.cos(phase), -jnp.sin(phase)], axis=0)


def swap(value, axis, bit):
    size = lax.axis_size(axis)
    return lax.ppermute(value, axis, [(i, i ^ bit) for i in range(size)])


def pick(value, index, axis):
    return lax.dynamic_index_in_dim(value, index, axis, keepdims=False)


def add(left, right):
    return (left.astype(F32) + right.astype(F32)).astype(BF16)


def seq_bits():
    bit, bits = 1, []
    while bit < lax.axis_size("seq"):
        bits.append(bit)
        bit *= 2
    return bits


def block_order(bits):
    order = [0]
    for bit in reversed(bits):
        order = [r ^ bit for r in order] + order
    return jnp.bitwise_xor(lax.axis_index("seq"), jnp.array(order, jnp.int32))


def chip_units(right, unit, which):
    per = right.shape[0] * right.shape[2] // (4 * unit)
    me = lax.axis_index("dp")
    return jnp.concatenate([jnp.bitwise_xor(me, w) * per + jnp.arange(per, dtype=jnp.int32) for w in which])


def halve(kept, got):
    half = kept.shape[0] // 2
    return add(kept[:half], got[:half]), add(kept[half:], got[half:])


def last(kept, got):
    return (kept.astype(F32) + got.astype(F32))[0]


def tie(*values):
    return lax.optimization_barrier(values)


def pack(parts):
    flat = jnp.concatenate([p.reshape(-1) for p in parts])
    short = -flat.shape[0] % 1024
    return jnp.pad(flat, (0, short)).reshape(-1, 128)


def unpack(packed, like):
    flat = packed.reshape(-1)
    out, place = [], 0
    for p in like:
        out.append(flat[place : place + p.size].reshape(p.shape))
        place += p.size
    return out


def back_act_kernel(dy, down, out, dy_sum):
    out[...] = mxu_nt(dy[...], down[...]).astype(BF16)
    @pl.when(pl.program_id(0) == 0)
    def _():
        acc = rows_loop(dy.shape[0], 16, lambda r, c: c + fold8(dy[r, :].astype(F32)))(jnp.zeros((8, dy.shape[1]), F32))
        dy_sum[...] = jnp.sum(acc, axis=0, keepdims=True)

def back_act(dy, down, block=512):
    rows, width = dy.shape
    ff = down.shape[0]
    return pl.pallas_call(
        back_act_kernel, grid=(ff // block,),
        in_specs=[pl.BlockSpec((rows, width), lambda f: (0, 0)), pl.BlockSpec((block, width), lambda f: (f, 0))],
        out_specs=[pl.BlockSpec((rows, block), lambda f: (0, f)), pl.BlockSpec((1, width), lambda f: (0, 0))],
        out_shape=[jax.ShapeDtypeStruct((rows, ff), BF16), jax.ShapeDtypeStruct((1, width), F32)],
        cost_estimate=cost(2 * rows * width * ff, 13 << 20),
        compiler_params=pltpu.CompilerParams(vmem_limit_bytes=GRANT), name="back_act")(dy, down)

def block_out_kernel(act, down, resid, bias, out, acc):
    f = pl.program_id(0)
    part = mxu(act[...], down[...])
    @pl.when(f == 0)
    def _():
        acc[...] = part + bias[...]
    @pl.when((f > 0) & (f < pl.num_programs(0) - 1))
    def _():
        acc[...] += part
    @pl.when(f == pl.num_programs(0) - 1)
    def _():
        out[...] = (acc[...] + part + resid[...].astype(F32)).astype(BF16)

def block_out(act, down, resid, bias, block=1024):
    rows, ff = act.shape
    width = down.shape[1]
    return pl.pallas_call(
        block_out_kernel, grid=(ff // block,),
        in_specs=[pl.BlockSpec((rows, block), lambda f: (0, f)), pl.BlockSpec((block, width), lambda f: (f, 0)),
                  pl.BlockSpec((rows, width), lambda f: (0, 0)), pl.BlockSpec((1, width), lambda f: (0, 0))],
        out_specs=pl.BlockSpec((rows, width), lambda f: (0, 0)),
        out_shape=jax.ShapeDtypeStruct((rows, width), BF16),
        scratch_shapes=[pltpu.VMEM((rows, width), F32)],
        cost_estimate=cost(2 * rows * width * ff, 15 << 20),
        compiler_params=pltpu.CompilerParams(vmem_limit_bytes=GRANT), name="block_out")(act, down, resid, bias)

C0 = math.sqrt(2.0 / math.pi)
C1 = C0 * 0.044715

def middle_kernel(conv, gate, x, dy, ga, wout, bout, gain, bias, up, up_bias,
                  act, gup, gup_sum, resid, normed, mixed, gattn, gconv, ggate, sums,
                  d2, normal, scale):
    f = pl.program_id(0)
    last = pl.num_programs(0) - 1
    rows, width = x.shape
    nb = width // LANES

    @pl.when((f == 0))
    def _():
        def mix(r, c):
            for j in range(nb):
                lanes = slice(j * LANES, (j + 1) * LANES)
                mixed[r, lanes] = (conv[j, r, :].astype(F32) * gate[r, lanes].astype(F32)).astype(BF16)
            return c
        rows_loop(rows, CHUNK, mix)(0)
        for h in range(2):
            half = slice(h * rows // 2, (h + 1) * rows // 2)
            d2[half, :] = mxu(mixed[half, :], wout[...])

        def norm(r, c):
            v = x[r, :].astype(F32) + d2[r, :] + bout[...]
            resid[r, :] = v.astype(BF16)
            mean = jnp.mean(v, axis=-1, keepdims=True)
            v = v - mean
            s = lax.rsqrt(jnp.mean(v * v, axis=-1, keepdims=True) + EPSILON)
            n = v * s
            scale[r, :] = s
            normal[r, :] = n
            normed[r, :] = (n * gain[...] + bias[...]).astype(BF16)
            return c
        rows_loop(rows, CHUNK, norm)(0)

    total = jnp.zeros((8, up.shape[1]), F32)
    pieces = 1
    for h in range(pieces):
        part = slice(h * rows // pieces, (h + 1) * rows // pieces)
        v = mxu(normed[part, :], up[...]) + up_bias[...]
        v2 = v * v
        t = jnp.tanh(v * (C0 + C1 * v2))
        half = 0.5 + 0.5 * t
        act[part, :] = (v * half).astype(BF16)
        slope = half + (0.5 * v) * (1.0 - t * t) * (C0 + (3.0 * C1) * v2)
        g = (ga[part, :].astype(F32) * slope).astype(BF16)
        gup[part, :] = g
        total += fold8(g.astype(F32))
        back = mxu_nt(g, up[...])
        @pl.when(f == 0)
        def _():
            d2[part, :] = back
        @pl.when(f > 0)
        def _():
            d2[part, :] += back
    gup_sum[...] = jnp.sum(total, axis=0, keepdims=True)

    @pl.when((f == last))
    def _():
        def norm_back(r, carry):
            a, b, o = carry
            d, n = d2[r, :], normal[r, :]
            a += fold8(d * n)
            b += fold8(d)
            e = d * gain[...]
            m1 = jnp.mean(e, axis=-1, keepdims=True)
            m2 = jnp.mean(e * n, axis=-1, keepdims=True)
            g = dy[r, :].astype(F32) + (e - m1 - n * m2) * scale[r, :]
            low = g.astype(BF16)
            gattn[r, :] = low
            o += fold8(low.astype(F32))
            return a, b, o
        zero = jnp.zeros((8, width), F32)
        a, b, o = rows_loop(rows, CHUNK, norm_back)((zero, zero, zero))
        sums[0:1, :] = jnp.sum(a, axis=0, keepdims=True)
        sums[1:2, :] = jnp.sum(b, axis=0, keepdims=True)
        sums[2:3, :] = jnp.sum(o, axis=0, keepdims=True)
        for h in range(2):
            half = slice(h * rows // 2, (h + 1) * rows // 2)
            d2[half, :] = mxu_nt(gattn[half, :], wout[...])
        def out(r, c):
            for j in range(nb):
                lanes = slice(j * LANES, (j + 1) * LANES)
                g = d2[r, lanes]
                gconv[j, r, :] = (g * gate[r, lanes].astype(F32)).astype(BF16)
                ggate[r, lanes] = (g * conv[j, r, :].astype(F32)).astype(BF16)
            return c
        rows_loop(rows, CHUNK, out)(0)

def middle(conv, gate, x, dy, ga, wout, bout, gain, bias, up, up_bias, block=512):
    rows, width = x.shape
    ff = up.shape[1]
    nb = width // LANES
    whole = lambda *s: pl.BlockSpec(s, lambda f: (0,) * len(s))
    flat = whole(rows, width)
    row = whole(1, width)
    cols = pl.BlockSpec((rows, block), lambda f: (0, f))
    bar = pl.BlockSpec((1, block), lambda f: (0, f))
    sd = jax.ShapeDtypeStruct
    return pl.pallas_call(
        middle_kernel, grid=(ff // block,),
        in_specs=[whole(nb, rows, LANES), flat, flat, flat, cols, whole(width, width), row, row, row,
                  pl.BlockSpec((width, block), lambda f: (0, f)), bar],
        out_specs=[cols, cols, bar, flat, flat, flat, flat, whole(nb, rows, LANES), flat, whole(3, width)],
        out_shape=[sd((rows, ff), BF16), sd((rows, ff), BF16), sd((1, ff), F32), sd((rows, width), BF16),
                   sd((rows, width), BF16), sd((rows, width), BF16), sd((rows, width), BF16),
                   sd((nb, rows, LANES), BF16), sd((rows, width), BF16), sd((3, width), F32)],
        scratch_shapes=[pltpu.VMEM((rows, width), F32), pltpu.VMEM((rows, width), F32), pltpu.VMEM((rows, 1), F32)],
        cost_estimate=cost(4 * rows * width * (ff + width), 34 << 20),
        compiler_params=pltpu.CompilerParams(vmem_limit_bytes=GRANT), name="middle")(
            conv, gate, x, dy, ga, wout, bout, gain, bias, up, up_bias)

PRE = 16

def enter_kernel(first, x, before, gain, bias, w0, w1, w2, b0, b1, b2, taps, inner, gate, proj, normed_out, normed, shifted):
    rows, width = x.shape
    def norm(src, base):
        def body(r, c):
            v = src[r, :].astype(F32)
            v = v - jnp.mean(v, axis=-1, keepdims=True)
            s = lax.rsqrt(jnp.mean(v * v, axis=-1, keepdims=True) + EPSILON)
            normed[pl.ds(r.start + base, r.size), :] = (v * s * gain[...] + bias[...]).astype(BF16)
            return c
        return body
    @pl.when(pl.program_id(0) == 0)
    def _():
        rows_loop(PRE, 16, norm(before, 0))(0)
        rows_loop(rows, CHUNK, norm(x, PRE))(0)
        normed_out[...] = normed[PRE:, :]
    cb = w0.shape[1]
    short = []
    keep = jnp.where(first[0] == 0, 0.0, 1.0)
    for k, (w, b) in enumerate(((w0, b0), (w1, b1), (w2, b2))):
        p = (mxu(normed[...], w[...]) + b[...]).astype(BF16)
        proj[k, PRE:, :] = p[PRE:]
        proj[k, :PRE, :] = (p[:PRE].astype(F32) * keep).astype(BF16)
        shifted[k, PRE:, :] = p[PRE:].astype(F32)
        shifted[k, :PRE, :] = p[:PRE].astype(F32) * keep
    def gates(r, c):
        s = []
        for k in range(3):
            p = shifted[k, pl.ds(r.start + (PRE - 8), r.size + 8), :]
            v = taps[9 + k : 10 + k, :] + sum(
                taps[3 * j + k : 3 * j + k + 1, :] * p[6 + j : 6 + j + r.size] for j in range(3))
            s.append(v)
        gate[r, :] = s[0].astype(BF16)
        v = (s[1] * s[2]).astype(BF16)
        for j in range(cb // LANES):
            inner[j, r, :] = v[:, j * LANES : (j + 1) * LANES]
        return c
    rows_loop(rows, CHUNK, gates)(0)

def enter(first, x, before, gain, bias, weight, in_bias, taps, block=256):
    rows, width = x.shape
    nb = width // LANES
    steps = width // block
    whole = lambda *s: pl.BlockSpec(s, lambda c: (0,) * len(s))
    wspec = lambda k: pl.BlockSpec((width, block), lambda c, k=k: (0, k * steps + c))
    bspec = lambda k: pl.BlockSpec((1, block), lambda c, k=k: (0, k * steps + c))
    sd = jax.ShapeDtypeStruct
    return pl.pallas_call(
        enter_kernel, grid=(steps,),
        in_specs=[pl.BlockSpec(memory_space=pltpu.SMEM), whole(rows, width), whole(PRE, width), whole(1, width), whole(1, width),
                  wspec(0), wspec(1), wspec(2), bspec(0), bspec(1), bspec(2), pl.BlockSpec((12, block), lambda c: (0, c))],
        out_specs=[pl.BlockSpec((block // LANES, rows, LANES), lambda c: (c, 0, 0)), pl.BlockSpec((rows, block), lambda c: (0, c)),
                   pl.BlockSpec((3, PRE + rows, block), lambda c: (0, 0, c)), whole(rows, width)],
        out_shape=[sd((nb, rows, LANES), BF16), sd((rows, width), BF16), sd((3, PRE + rows, width), BF16), sd((rows, width), BF16)],
        scratch_shapes=[pltpu.VMEM((PRE + rows, width), BF16), pltpu.VMEM((3, PRE + rows, block), F32)],
        cost_estimate=cost(6 * rows * width * width, 14 << 20),
        compiler_params=pltpu.CompilerParams(vmem_limit_bytes=GRANT), name="enter")(
            first, x, before, gain, bias, weight, weight, weight, in_bias, in_bias, in_bias, taps)

POST = 16

def leave_kernel(ginner, ggate, ggate_after, proj, proj_after, taps, gproj, sums, pbuf, gbuf):
    rows = ggate.shape[0]
    cb = ggate.shape[1]
    for k in range(3):
        pbuf[k, : PRE + rows, :] = proj[k].astype(F32)
        pbuf[k, PRE + rows :, :] = proj_after[k].astype(F32)
    tap = lambda j, k: taps[3 * j + k : 3 * j + k + 1, :]

    def lags(k, start, size):
        p = pbuf[k, pl.ds(start + (PRE - 8), size + 8), :]
        return [p[6 + j : 6 + j + size] for j in range(3)]

    def grads(start, size, g0):
        gi = jnp.concatenate([ginner[j, pl.ds(start, size), :] for j in range(cb // LANES)], axis=1).astype(F32)
        p1 = lags(1, start, size)
        p2 = lags(2, start, size)
        s1 = taps[10:11, :] + sum(tap(j, 1) * p1[j] for j in range(3))
        s2 = taps[11:12, :] + sum(tap(j, 2) * p2[j] for j in range(3))
        return (g0, gi * s2, gi * s1), p1, p2

    def first(r, carry):
        g, p1, p2 = grads(r.start, r.size, ggate[r, :].astype(F32))
        p0 = lags(0, r.start, r.size)
        out = []
        for k in range(3):
            gbuf[k, r, :] = g[k]
        for j in range(3):
            for k, p in enumerate((p0, p1, p2)):
                out.append(carry[3 * j + k] + fold8(g[k] * p[j]))
        for k in range(3):
            out.append(carry[9 + k] + fold8(g[k]))
        return tuple(out)

    acc = rows_loop(rows, CHUNK, first)(tuple(jnp.zeros((8, cb), F32) for _ in range(12)))
    for i in range(12):
        sums[i : i + 1, :] = jnp.sum(acc[i], axis=0, keepdims=True)
    g, _, _ = grads(rows, POST, ggate_after[...].astype(F32))
    for k in range(3):
        gbuf[k, rows:, :] = g[k]

    def second(r, carry):
        out = []
        for k in range(3):
            g = gbuf[k, pl.ds(r.start, r.size + 8), :]
            v = sum(tap(j, k) * g[2 - j : 2 - j + r.size] for j in range(3)).astype(BF16)
            gproj[k, 0, r, :] = v
            out.append(carry[k] + fold8(v.astype(F32)))
        return tuple(out)

    acc = rows_loop(rows, CHUNK, second)(tuple(jnp.zeros((8, cb), F32) for _ in range(3)))
    for i in range(3):
        sums[12 + i : 13 + i, :] = jnp.sum(acc[i], axis=0, keepdims=True)
    sums[15:16, :] = jnp.zeros((1, cb), F32)

def leave(ginner, ggate, ggate_after, proj, proj_after, taps, block=256):
    rows, width = ggate.shape
    steps = width // block
    sd = jax.ShapeDtypeStruct
    return pl.pallas_call(
        leave_kernel, grid=(steps,),
        in_specs=[pl.BlockSpec((block // LANES, rows + POST, LANES), lambda c: (c, 0, 0)),
                  pl.BlockSpec((rows, block), lambda c: (0, c)), pl.BlockSpec((POST, block), lambda c: (0, c)),
                  pl.BlockSpec((3, PRE + rows, block), lambda c: (0, 0, c)), pl.BlockSpec((3, POST, block), lambda c: (0, 0, c)),
                  pl.BlockSpec((12, block), lambda c: (0, c))],
        out_specs=[pl.BlockSpec((3, 1, rows, block), lambda c: (0, c, 0, 0)), pl.BlockSpec((16, block), lambda c: (0, c))],
        out_shape=[sd((3, steps, rows, block), BF16), sd((16, width), F32)],
        scratch_shapes=[pltpu.VMEM((3, PRE + rows + POST, block), F32), pltpu.VMEM((3, rows + POST, block), F32)],
        cost_estimate=cost(60 * rows * width, 9 << 20),
        compiler_params=pltpu.CompilerParams(vmem_limit_bytes=GRANT), name="leave")(ginner, ggate, ggate_after, proj, proj_after, taps)

def tokens_kernel(gproj, weight, x, gres, gain, out, sums, acc):
    k = pl.program_id(0)
    rows, width = x.shape
    unit = gproj.shape[3]
    part = sum(mxu_nt(gproj[0, j], weight[:, j * unit : (j + 1) * unit]) for j in range(gproj.shape[1]))
    @pl.when(k == 0)
    def _():
        acc[...] = part
    @pl.when(k > 0)
    def _():
        acc[...] += part
    @pl.when(k == pl.num_programs(0) - 1)
    def _():
        def body(r, carry):
            a, b = carry
            v = x[r, :].astype(F32)
            v = v - jnp.mean(v, axis=-1, keepdims=True)
            s = lax.rsqrt(jnp.mean(v * v, axis=-1, keepdims=True) + EPSILON)
            n = v * s
            d = acc[r, :]
            a += fold8(d * n)
            b += fold8(d)
            e = d * gain[...]
            m1 = jnp.mean(e, axis=-1, keepdims=True)
            m2 = jnp.mean(e * n, axis=-1, keepdims=True)
            out[r, :] = gres[r, :].astype(F32) + (e - m1 - n * m2) * s
            return a, b
        zero = jnp.zeros((8, width), F32)
        a, b = rows_loop(rows, CHUNK, body)((zero, zero))
        sums[0:1, :] = jnp.sum(a, axis=0, keepdims=True)
        sums[1:2, :] = jnp.sum(b, axis=0, keepdims=True)

def tokens_back(gproj, weight, x, gres, gain):
    rows, width = x.shape
    whole = lambda *s: pl.BlockSpec(s, lambda k: (0,) * len(s))
    sd = jax.ShapeDtypeStruct
    return pl.pallas_call(
        tokens_kernel, grid=(3,),
        in_specs=[pl.BlockSpec((1,) + gproj.shape[1:], lambda k: (k, 0, 0, 0)), pl.BlockSpec((width, width), lambda k: (0, k)),
                  whole(rows, width), whole(rows, width), whole(1, width)],
        out_specs=[whole(rows, width), whole(2, width)],
        out_shape=[sd((rows, width), F32), sd((2, width), F32)],
        scratch_shapes=[pltpu.VMEM((rows, width), F32)],
        cost_estimate=cost(6 * rows * width * width, 14 << 20),
        compiler_params=pltpu.CompilerParams(vmem_limit_bytes=GRANT), name="tokens_back")(gproj, weight, x, gres, gain)


def wgrad_kernel(row_order, units, *refs, sides, lefts, rights, held, mode):
    acc = None
    for side in range(sides):
        refs_left, refs = refs[:lefts], refs[lefts:]
        left = jnp.concatenate([r[...] for r in refs_left], axis=1)
        refs_right, refs = refs[:rights], refs[rights:]
        right = jnp.concatenate([r[0] for r in refs_right], axis=1)
        part = mxu_tn(left, right)
        acc = part if acc is None else acc + part
    outs = refs[held:]
    count, height, _ = outs[0].shape
    width = acc.shape[1] // 2
    value = acc.reshape(count, height, acc.shape[1]).astype(BF16)
    if mode == "x":
        outs[0][...] = value[..., :width]
        outs[1][...] = value[..., width:]
    if mode == "y":
        early = pl.program_id(0) < pl.num_programs(0) // 2

        @pl.when(early)
        def _():
            place = 0
            for piece in outs[:-1]:
                piece[...] = value[..., place : place + piece.shape[2]]
                place += piece.shape[2]

        @pl.when(jnp.logical_not(early))
        def _():
            outs[-1][...] = value


def wgrad(left, right, row_order, units, unit, mode, each, held=(), tall=None, start=0, pieces=(1,)):
    rows, m = left[0].shape
    sides, blocks, count = len(left), row_order.shape[0], units[0].shape[0]
    height = m // blocks
    tall = tall or height
    at = start // height
    wide = count * unit
    half = wide // 2
    if height % LANES:
        left = [v.reshape(rows, blocks, height)[:, row_order].reshape(rows, m) for v in left]
        each = max(each, LANES // height)
        left_specs = [pl.BlockSpec((rows, each * height), lambda i, r, u: (0, i))]
    else:
        left_specs = [pl.BlockSpec((rows, height), lambda i, r, u, q=q: (0, r[i * each + q])) for q in range(each)]
    lefts, steps = len(left_specs), blocks // each
    in_specs, args = [], []
    for side in range(sides):
        per, base = right[side].shape[2] // unit, side * count
        in_specs += left_specs + [
            pl.BlockSpec((1, rows, unit), lambda i, r, u, j=base + j, per=per: (u[j] // per, 0, u[j] % per))
            for j in range(count)
        ]
        args += [left[side]] * lefts + [right[side]] * count
    aliases = {2 + len(args) + i: i for i in range(len(held))}
    in_specs += [pl.BlockSpec(memory_space=pl.ANY)] * len(held)
    args += list(held)
    full = lambda w: ((blocks, tall, w), pl.BlockSpec((each, height, w), lambda i, r, u: (i, at, 0)))
    first = ((blocks // 2, tall, wide), lambda i: jnp.minimum(i, steps // 2 - 1))
    second = ((blocks // 2, tall, wide), lambda i: jnp.maximum(i - steps // 2, 0))
    part = lambda s, w: ((s[0][0], tall, w), pl.BlockSpec((each, height, w), lambda i, r, u: (s[1](i), at, 0)))
    outs = {
        "x": [full(half)] * 2,
        "y": [part(first, wide * p // sum(pieces)) for p in pieces] + [part(second, wide)],
    }[mode]
    return pl.pallas_call(
        functools.partial(wgrad_kernel, sides=sides, lefts=lefts, rights=count, held=len(held), mode=mode),
        grid_spec=pltpu.PrefetchScalarGridSpec(
            num_scalar_prefetch=2, grid=(steps,), in_specs=in_specs, out_specs=[o[1] for o in outs]
        ),
        out_shape=[jax.ShapeDtypeStruct(o[0], BF16) for o in outs],
        input_output_aliases=aliases,
        cost_estimate=cost(2 * sides * rows * m * wide, 2 * sides * (rows * m + rows * wide) + 4 * m * wide),
        compiler_params=pltpu.CompilerParams(vmem_limit_bytes=GRANT),
        name="wgrad",
    )(row_order, jnp.concatenate(units), *args)


def on_device(
    tokens,
    cotangent,
    norm1_gain,
    norm1_bias,
    in_weight,
    in_bias,
    short_weight,
    short_bias,
    filter_in,
    filter_in_bias,
    sine_freq,
    filter_out,
    decay_rates,
    filter_bias,
    out_weight,
    out_bias,
    norm2_gain,
    norm2_bias,
    up_weight,
    up_bias,
    down_weight,
    down_bias,
):
    width = in_weight.shape[0]
    ff = up_weight.shape[1]
    rows = tokens.shape[1]
    seq = lax.axis_size("seq")
    me = lax.axis_index("seq")
    length = rows * seq
    chans = width // seq
    down_shift = [(i + 1, i) for i in range(seq - 1)]

    x, dy = tokens[0], cotangent[0]
    edge = 2 * width // chans
    mine = jnp.concatenate(
        [short_weight.reshape(9, chans), short_bias, x[rows - 2 :].astype(F32).reshape(edge, chans)], axis=0
    )
    got = lax.all_to_all(
        jnp.broadcast_to(mine[None], (seq, 12 + edge, chans)), "seq", split_axis=0, concat_axis=0, tiled=True
    ).reshape(seq, 12 + edge, chans)
    all_taps = got[:, :12].transpose(1, 0, 2).reshape(12, width)
    before = pick(got, jnp.maximum(me - 1, 0), 0)[12:].reshape(2, width)
    before = jnp.concatenate([jnp.zeros((PRE - 2, width), BF16), before.astype(BF16)], axis=0)

    row = lambda v: v[None, :]
    first = me.reshape(1).astype(jnp.int32)
    fast = length // BLOCK <= 64
    tables = make_tables(length) if fast else None
    before, all_taps, tables = lax.optimization_barrier((before, all_taps, tables))
    inner, gate, proj, normed = enter(
        first, x, before, row(norm1_gain), row(norm1_bias), in_weight, row(in_bias), all_taps
    )
    proj_after = lax.ppermute(proj[:, PRE : PRE + POST], "seq", down_shift)

    def to_channels(value):
        if chans != LANES:
            value = value.transpose(1, 0, 2).reshape(rows, seq, chans).transpose(1, 0, 2)
        got = lax.all_to_all(value, "seq", split_axis=0, concat_axis=0, tiled=True)
        return got.reshape(length, chans)

    def to_tokens(value):
        got = lax.all_to_all(value, "seq", split_axis=0, concat_axis=0, tiled=True)
        if chans != LANES:
            got = got.transpose(1, 0, 2).reshape(got.shape[1], width // LANES, LANES).transpose(1, 0, 2)
        return got

    inner_chan = to_channels(inner)

    mixer = (FastMixer if fast else PlainMixer)(length, chans, seq, tables)
    features = position_features(length)
    hidden_pre = jnp.dot(filter_in.T, features, precision=HIGH) + filter_in_bias[:, None]
    phase = sine_freq[:, None] * hidden_pre
    hidden = jnp.sin(phase)
    window = jnp.exp(-features[0][:, None] * decay_rates[None, :])
    kernel = jnp.einsum("hn,hc->nc", hidden, filter_out, precision=HIGH) * window
    kernel_spec = mixer.spectrum(kernel)

    conv_chan, inner_spec = mixer.convolve(inner_chan, kernel_spec, filter_bias, False, 0)
    normed_x = swap(normed, "dp", 2)
    conv_chan, proj_after, normed_x = tie(conv_chan, proj_after, normed_x)
    normed_all = [normed, swap(normed, "dp", 1), normed_x, swap(normed_x, "dp", 1)]
    conv = to_tokens(conv_chan)
    dy_other = swap(dy, "dp", 1)
    grad_act, dy_sum = back_act(dy, down_weight)
    conv, dy_other, normed_all = tie(conv, dy_other, normed_all)
    act, gup, gup_sum, resid, normed2, mixed, grad_attn, grad_conv, grad_gate, mid_sums = middle(
        conv, gate, x, dy, grad_act, out_weight, row(out_bias), row(norm2_gain), row(norm2_bias), up_weight, row(up_bias)
    )
    grad_chan = to_channels(grad_conv)
    gate_after = lax.ppermute(grad_gate[:POST], "seq", down_shift)

    bits = seq_bits()
    order = block_order(bits)
    up_bits = [bits[1], bits[0]] + bits[2:]
    up_order = block_order(up_bits)
    unit = width // 4
    tall = (ff + width) // seq
    wide = ff // seq

    pair = lambda value: (value, swap(value, "dp", 1))
    near_units, near_up = chip_units(dy[None], unit, (2, 0)), chip_units(gup[None], ff // 4, (2, 0))
    dy_pair, act_pair = (dy[None], dy_other[None]), pair(act)
    mixed_pair, attn_pair = pair(mixed), pair(grad_attn[None])
    gup_pair, normed2_pair = pair(gup[None]), pair(normed2)
    parts = wgrad(act_pair, dy_pair, order, [near_units] * 2, unit, "x", 2, tall=tall)
    each = 8 if seq == 8 else 4
    tall_send, tall_kept = wgrad(
        mixed_pair, attn_pair, order, [near_units] * 2, unit, "x", each, held=parts, tall=tall, start=wide
    )
    tall_got = swap(tall_send, "dp", 2)
    grad_chan, tall_kept = tie(grad_chan, tall_kept)
    grad_inner_chan, grad_spec = mixer.convolve(grad_chan, kernel_spec, filter_bias, True, POST)
    gup_pair, normed2_pair, grad_inner_chan, gate_after = tie(gup_pair, normed2_pair, grad_inner_chan, gate_after)
    grad_inner = to_tokens(grad_inner_chan)
    *up_sends, up_kept = wgrad(normed2_pair, gup_pair, up_order, [near_up] * 2, ff // 4, "y", 4, pieces=(1, 2, 1))

    grad_filter_out, grad_filter_in, filter_sums, grad_filter_bias = mixer.filter_grad(
        grad_spec, inner_spec, grad_chan, inner_chan, (features, hidden_pre, phase, hidden, window, filter_out)
    )
    grad_freq = filter_sums[0]
    grad_filter_in_bias = filter_sums[1] * sine_freq
    grad_filter_in = grad_filter_in * sine_freq[None, :]

    grad_inner, grad_filter_out, up_sends = tie(grad_inner, grad_filter_out, up_sends)
    up_gots = [swap(up_sends[0], "seq", up_bits[0])]
    grad_proj, leave_sums = leave(grad_inner, grad_gate, gate_after, proj, proj_after, all_taps)
    grad_proj, tall_got, up_gots[0] = tie(grad_proj, tall_got, up_gots[0])
    tall_send, tall_kept = halve(tall_kept, tall_got)
    proj_units = grad_proj.reshape((-1,) + grad_proj.shape[2:])
    proj_all = lax.all_to_all(proj_units, "dp", split_axis=0, concat_axis=0, tiled=True)
    up_gots.append(swap(up_sends[1], "seq", up_bits[0]))
    grad_proj, tall_send = tie(grad_proj, tall_send)
    tall_got = swap(tall_send, "seq", bits[0])
    grad_tokens, token_sums = tokens_back(grad_proj, in_weight, x, grad_attn, row(norm1_gain))

    shared = (token_sums, leave_sums, mid_sums, gup_sum, dy_sum, grad_filter_in, grad_filter_in_bias, grad_freq)
    channel = (grad_filter_out, grad_filter_bias)
    packed, extra = pack(shared), pack(channel)
    rows_shared = packed.shape[0]
    packed = jnp.concatenate([packed, extra], axis=0)
    packed = packed + swap(packed, "dp", 1)
    packed, up_gots[1] = tie(packed, up_gots[1])
    small = swap(packed, "dp", 2)
    up_gots.append(swap(up_sends[2], "seq", up_bits[0]))
    cut = ff // 4
    part = up_gots[1].shape[2] // 2
    up_send = add(up_kept[..., :cut], jnp.concatenate([up_gots[0], up_gots[1][..., :part]], axis=2))
    up_send, act = tie(up_send, act)
    up_got = swap(up_send, "dp", 2)
    block_output = block_out(act, down_weight, resid, row(down_bias))
    block_output, proj_all = tie(block_output, proj_all)
    dp_me = lax.axis_index("dp")
    share = proj_units.shape[0] // 4
    ahead = jnp.arange(share, dtype=jnp.int32)
    in_units = [jnp.bitwise_xor(dp_me, w) * share + ahead for w in range(4)]
    in_send, in_kept = wgrad(normed_all, [proj_all] * 4, order, in_units, proj_units.shape[2], "y", 4)

    in_send, tall_got, up_gots = tie(in_send, tall_got, up_gots)
    in_got = swap(in_send, "seq", bits[0])
    tall_send, tall_kept = halve(tall_kept, tall_got)
    tall_got = swap(tall_send, "seq", bits[1])
    up_kept = add(up_kept[..., cut:], jnp.concatenate([up_gots[1][..., part:], up_gots[2]], axis=2))
    up_got, up_kept, tall_send, small = tie(up_got, up_kept, tall_send, small)
    up_send, up_kept = halve(up_kept, up_got)
    up_got = swap(up_send, "seq", up_bits[1])
    packed = packed + small
    packed, extra = packed[:rows_shared], packed[rows_shared:]
    small = swap(packed, "seq", bits[0])

    in_got, tall_got, up_send, small = tie(in_got, tall_got, up_send, small)
    in_send, in_kept = halve(in_kept, in_got)
    in_got = swap(in_send, "seq", bits[1])
    tall_send, tall_kept = halve(tall_kept, tall_got)
    tall_got = swap(tall_send, "seq", bits[2])
    packed = packed + small
    small = swap(packed, "seq", bits[1])

    for i in range(2, len(bits)):
        in_send, up_got = tie(in_send, up_got)
        up_send, up_kept = halve(up_kept, up_got)
        up_got = swap(up_send, "seq", up_bits[i])
        in_got, tall_got, up_send, small = tie(in_got, tall_got, up_send, small)
        if i > 2:
            tall_send, tall_kept = halve(tall_kept, tall_got)
            tall_got = swap(tall_send, "seq", bits[i])
        in_send, in_kept = halve(in_kept, in_got)
        in_got = swap(in_send, "seq", bits[i])
        packed = packed + small
        small = swap(packed, "seq", bits[i])
    up_got, in_got, small = tie(up_got, in_got, small)
    grad_up, packed = last(up_kept, up_got), packed + small
    grad_in, both = last(in_kept, in_got), last(tall_kept, tall_got)
    grad_down, grad_out_weight = both[:wide], both[wide:]
    channel = unpack(extra, channel)
    shared = unpack(packed, shared)
    token_sums, leave_sums, mid_sums, gup_sum, dy_sum = shared[:5]
    own = lax.dynamic_slice_in_dim(leave_sums[:12], me * chans, chans, 1)
    return (
        block_output[None],
        grad_tokens[None],
        token_sums[0],
        token_sums[1],
        grad_in,
        leave_sums[12:15].reshape(-1),
        own[:9].reshape(3, 3, chans),
        own[9:],
        shared[5],
        shared[6],
        shared[7],
        channel[0],
        channel[1],
        grad_out_weight,
        mid_sums[2],
        mid_sums[0],
        mid_sums[1],
        grad_up,
        gup_sum[0],
        grad_down,
        dy_sum[0],
    )


def solution(mesh):
    everywhere, by_token, by_rows = P(), P("dp", "seq", None), P("seq", "dp")
    taps, shift, chan = P(None, None, "seq"), P(None, "seq"), P("seq")
    in_specs = (by_token,) * 2 + (everywhere,) * 4 + (taps, shift) + (everywhere,) * 3
    in_specs += (shift, chan, chan) + (everywhere,) * 8
    out_specs = (by_token, by_token, everywhere, everywhere, by_rows, everywhere, taps, shift)
    out_specs += (everywhere,) * 3 + (shift, chan, by_rows) + (everywhere,) * 3
    out_specs += (by_rows, everywhere, by_rows, everywhere)
    return jax.shard_map(
        on_device, mesh=mesh, in_specs=in_specs, out_specs=out_specs, check_vma=False
    )
```

```python
import functools
import math

import jax
import jax.numpy as jnp
import numpy as np
from jax import lax
from jax.experimental import pallas as pl
from jax.experimental.pallas import tpu as pltpu
from jax.sharding import PartitionSpec as P

EMB = 33
HIGH = lax.Precision.HIGHEST
EPSILON = 1e-05
BLOCK = 128
LANES = 128
ROWS = 16
CHUNK = 256
GRANT = 60 << 20
COST = 8
F32 = jnp.float32
BF16 = jnp.bfloat16


def times_root(re, im, num, den):
    num = num % den
    if num == 0:
        return re, im
    if 4 * num == den:
        return -im, re
    if 2 * num == den:
        return -re, -im
    if 4 * num == 3 * den:
        return im, -re
    angle = 2.0 * math.pi * num / den
    cos, sin = math.cos(angle), math.sin(angle)
    if abs(abs(cos) - abs(sin)) < 1e-12:
        sc, ss = (1.0 if cos > 0 else -1.0), (1.0 if sin > 0 else -1.0)
        root = abs(cos)
        return root * (sc * re - ss * im), root * (sc * im + ss * re)
    return re * cos - im * sin, im * cos + re * sin


def small_fft(re, im, sign):
    count = len(re)
    if count == 1:
        return re, im
    if count == 2:
        return [re[0] + re[1], re[0] - re[1]], [im[0] + im[1], im[0] - im[1]]
    even_re, even_im = small_fft(re[0::2], im[0::2], sign)
    odd_re, odd_im = small_fft(re[1::2], im[1::2], sign)
    low_re, low_im, top_re, top_im = [], [], [], []
    for k in range(count // 2):
        tr, ti = times_root(odd_re[k], odd_im[k], sign * k, count)
        low_re.append(even_re[k] + tr)
        low_im.append(even_im[k] + ti)
        top_re.append(even_re[k] - tr)
        top_im.append(even_im[k] - ti)
    return low_re + top_re, low_im + top_im


def blocks_forward(source, target, count):
    def body(step, carry):
        row = pl.multiple_of(step * ROWS, ROWS)
        re, im = [], []
        for a in range(count):
            value = source[a, pl.ds(row, ROWS), :].astype(F32)
            angle = 2.0 * math.pi * a / (4 * count)
            re.append(value * math.cos(angle))
            im.append(value * math.sin(angle))
        re, im = small_fft(re, im, -1)
        for k in range(count):
            target[k, pl.ds(row, ROWS), :] = re[k].astype(BF16)
            target[k, pl.ds(BLOCK + row, ROWS), :] = im[k].astype(BF16)
        return carry

    lax.fori_loop(0, BLOCK // ROWS, body, 0)


def blocks_inverse(source, emit, count):
    def body(step, carry):
        row = pl.multiple_of(step * ROWS, ROWS)
        re = [source[k, pl.ds(row, ROWS), :] for k in range(count)]
        im = [source[k, pl.ds(BLOCK + row, ROWS), :] for k in range(count)]
        re, im = small_fft(re, im, 1)
        for a in range(count):
            angle = 2.0 * math.pi * a / (4 * count)
            emit(a, row, re[a] * math.cos(angle) + im[a] * math.sin(angle))
        return carry

    lax.fori_loop(0, BLOCK // ROWS, body, 0)


def cost(flops, bytes_accessed):
    return pl.CostEstimate(flops=flops // COST, bytes_accessed=bytes_accessed // COST, transcendentals=0)


def mxu(left, right):
    return jnp.dot(left, right, preferred_element_type=F32)

def mxu_nt(left, right):
    return lax.dot_general(left, right, (((1,), (1,)), ((), ())), preferred_element_type=F32)

def mxu_tn(left, right):
    return lax.dot_general(left, right, (((0,), (0,)), ((), ())), preferred_element_type=F32)

def rows_loop(total, chunk, body, unroll=1):
    def step(i, carry):
        return body(pl.ds(pl.multiple_of(i * chunk, chunk), chunk), carry)
    return lambda init: lax.fori_loop(0, total // chunk, step, init, unroll=unroll)

def fold8(v):
    return jnp.sum(v.reshape(v.shape[0] // 8, 8, v.shape[1]), axis=0)


def table_kernel(alpha_cos, alpha_sin, beta_cos, beta_sin, forward, inverse, *, scale):
    cb, sb = beta_cos[...], beta_sin[...]
    for i in range(forward.shape[0]):
        ca, sa = alpha_cos[i], alpha_sin[i]
        cos = ca * cb - sa * sb
        sin = sa * cb + ca * sb
        low_cos, low_sin = cos.astype(BF16), sin.astype(BF16)
        forward[i, :BLOCK, :BLOCK] = low_cos
        forward[i, :BLOCK, BLOCK:] = low_sin
        forward[i, BLOCK:, :BLOCK] = -low_sin
        forward[i, BLOCK:, BLOCK:] = low_cos
        low_cos, low_sin = (cos.T * scale).astype(BF16), (sin.T * scale).astype(BF16)
        inverse[i, :BLOCK, :BLOCK] = low_cos
        inverse[i, :BLOCK, BLOCK:] = -low_sin
        inverse[i, BLOCK:, :BLOCK] = low_sin
        inverse[i, BLOCK:, BLOCK:] = low_cos


def make_tables(length):
    count = length // BLOCK
    alpha = 2.0 * np.pi * np.arange(BLOCK)[None, :] * (np.arange(count)[:, None] - 0.25) / length
    beta = 2.0 * np.pi * ((np.arange(BLOCK)[:, None] * np.arange(BLOCK)[None, :]) % BLOCK) / BLOCK
    alpha = alpha[:, None, :]
    consts = [jnp.asarray(f(v), F32) for v in (alpha, beta) for f in (np.cos, np.sin)]
    each = math.gcd(count, 4)
    row = pl.BlockSpec((each, 1, BLOCK), lambda i: (i, 0, 0))
    flat = pl.BlockSpec((BLOCK, BLOCK), lambda i: (0, 0))
    out = pl.BlockSpec((each, 2 * BLOCK, 2 * BLOCK), lambda i: (i, 0, 0))
    shape = jax.ShapeDtypeStruct((count, 2 * BLOCK, 2 * BLOCK), BF16)
    return pl.pallas_call(
        functools.partial(table_kernel, scale=1.0 / length),
        grid=(count // each,),
        in_specs=[row, row, flat, flat],
        out_specs=[out, out],
        out_shape=[shape, shape],
        cost_estimate=cost(16 * count * BLOCK * BLOCK, 8 << 20),
        name="tables",
    )(*consts)


def split_spec(value):
    return value[:BLOCK], value[BLOCK:]


def turn_back(prod, inverse, back):
    def body(k, carry):
        back[k] = mxu(inverse[k], prod[k])
        return carry

    lax.fori_loop(0, prod.shape[0], body, 0, unroll=16)


def spectrum_kernel(signal, forward, spectrum, mid):
    (signal, have_signal), (forward, have_forward) = signal, forward
    count = signal.shape[0]
    have_signal()
    blocks_forward(signal, mid, count)
    have_forward()

    def body(k, carry):
        spectrum[k] = mxu(forward[k], mid[k]).astype(BF16)
        return carry

    lax.fori_loop(0, count, body, 0, unroll=16)


def conv_kernel(signal, kernel_spec, bias, forward, inverse, result, spectrum, mid, prod, back, *, conjugate):
    (signal, have_signal), (kernel_spec, have_spec), (bias, have_bias) = signal, kernel_spec, bias
    (forward, have_forward), (inverse, have_inverse) = forward, inverse
    count = signal.shape[0]
    have_signal()
    blocks_forward(signal, mid, count)
    have_spec()
    have_bias()
    have_forward()

    def body(k, carry):
        spec = mxu(forward[k], mid[k])
        spectrum[k] = spec.astype(BF16)
        a_re, a_im = split_spec(spec)
        b_re, b_im = split_spec(kernel_spec[k].astype(F32))
        if conjugate:
            b_im = -b_im
        prod[k, :BLOCK, :] = (a_re * b_re - a_im * b_im).astype(BF16)
        prod[k, BLOCK:, :] = (a_re * b_im + a_im * b_re).astype(BF16)
        return carry

    lax.fori_loop(0, count, body, 0, unroll=16)
    have_inverse()
    turn_back(prod, inverse, back)
    gain = bias[...]
    devices, rows, _ = result.shape
    per = count // devices
    size = per * BLOCK

    def emit(a, row, value):
        direct = signal[a, pl.ds(row, ROWS), :].astype(F32) * gain
        result[a // per, pl.ds((a % per) * BLOCK + row, ROWS), :] = (value + direct).astype(result.dtype)

    blocks_inverse(back, emit, count)
    if rows > size:
        for j in range(devices - 1):
            result[j, size:, :] = result[j + 1, : rows - size, :]
        result[devices - 1, size:, :] = jnp.zeros((rows - size, result.shape[2]), result.dtype)


def filter_grad_kernel(
    grad_spec, signal_spec, grad, signal, inverse, window, hidden, slope, hidden_pre, features, filter_out,
    out_grad, in_grad, sums, bias_grad, prod, back, raw,
):
    (grad_spec, have_grad_spec), (signal_spec, have_signal_spec) = grad_spec, signal_spec
    count = grad_spec.shape[0]
    have_grad_spec()
    have_signal_spec()

    def body(k, carry):
        a_re, a_im = split_spec(grad_spec[k].astype(F32))
        b_re, b_im = split_spec(signal_spec[k].astype(F32))
        prod[k, :BLOCK, :] = (a_re * b_re + a_im * b_im).astype(BF16)
        prod[k, BLOCK:, :] = (a_im * b_re - a_re * b_im).astype(BF16)
        return carry

    lax.fori_loop(0, count, body, 0, unroll=2)
    for _, wait in (grad, signal, inverse, window, hidden, slope, hidden_pre, features, filter_out):
        wait()
    grad, signal, inverse, window, hidden, slope, hidden_pre, features, filter_out = (
        v[0] for v in (grad, signal, inverse, window, hidden, slope, hidden_pre, features, filter_out)
    )
    turn_back(prod, inverse, back)

    def emit(a, row, value):
        at = pl.ds(a * BLOCK + row, ROWS)
        raw[at, :] = (value * window[at, :]).astype(BF16)

    blocks_inverse(back, emit, count)

    def total(a, acc):
        return acc + fold8(grad[a].astype(F32) * signal[a].astype(F32))

    acc = lax.fori_loop(0, count, total, jnp.zeros((8, grad.shape[-1]), F32))
    bias_grad[...] = jnp.sum(acc, axis=0, keepdims=True)
    out_grad[...] = mxu(hidden[...], raw[...])
    turned = mxu_nt(filter_out[...], raw[...]) * slope[...]
    sums[...] = jnp.concatenate(
        [jnp.sum(turned * hidden_pre[...], axis=1, keepdims=True), jnp.sum(turned, axis=1, keepdims=True)], axis=1
    )
    in_grad[...] = mxu_nt(features[...], turned.astype(BF16))


def vmem_call(kernel, outs, scratch, args, name):
    count = len(args)

    def body(*refs):
        ins, rest = refs[:count], refs[count:]
        results, local = rest[: len(outs)], rest[len(outs) : len(outs) + len(scratch)]
        bufs, sems = rest[len(outs) + len(scratch) : -1], rest[-1]
        copies = [pltpu.make_async_copy(src, dst, sems.at[i]) for i, (src, dst) in enumerate(zip(ins, bufs))]
        for copy in copies:
            copy.start()
        kernel(*[(buf, copy.wait) for buf, copy in zip(bufs, copies)], *results, *local)

    scratch = list(scratch)
    held = [pltpu.VMEM(a.shape, a.dtype) for a in args]
    return pl.pallas_call(
        body,
        in_specs=[pl.BlockSpec(memory_space=pl.ANY)] * count,
        out_specs=[pl.BlockSpec(o.shape, lambda n=len(o.shape): (0,) * n) for o in outs],
        out_shape=outs,
        scratch_shapes=scratch + held + [pltpu.SemaphoreType.DMA((count,))],
        cost_estimate=cost(4 << 30, 16 << 20),
        compiler_params=pltpu.CompilerParams(vmem_limit_bytes=GRANT),
        name=name,
    )(*args)


class FastMixer:
    def __init__(self, length, channels, devices, tables):
        self.count = length // BLOCK
        self.channels = channels
        self.devices = devices
        self.forward, self.inverse = tables
        self.mid = pltpu.VMEM((self.count, 2 * BLOCK, channels), BF16)
        self.back = pltpu.VMEM((self.count, 2 * BLOCK, channels), F32)
        self.spec = jax.ShapeDtypeStruct((self.count, 2 * BLOCK, channels), BF16)

    def blocked(self, value):
        return value.reshape(self.count, BLOCK, self.channels)

    def spectrum(self, signal):
        args = (self.blocked(signal), self.forward)
        return vmem_call(spectrum_kernel, [self.spec], [self.mid], args, "spectrum")[0]

    def convolve(self, signal, kernel_spec, bias, conjugate, extra):
        rows = self.count * BLOCK // self.devices + extra
        out = jax.ShapeDtypeStruct((self.devices, rows, self.channels), BF16)
        return vmem_call(
            functools.partial(conv_kernel, conjugate=conjugate),
            [out, self.spec],
            [self.mid, self.mid, self.back],
            (self.blocked(signal), kernel_spec, bias[None, :], self.forward, self.inverse),
            "correlate" if conjugate else "convolve",
        )

    def filter_grad(self, grad_spec, signal_spec, grad, signal, filt):
        features, hidden_pre, phase, hidden, window, filter_out = filt
        units = hidden.shape[0]
        outs = [
            jax.ShapeDtypeStruct((units, self.channels), F32),
            jax.ShapeDtypeStruct((48, units), F32),
            jax.ShapeDtypeStruct((units, 2), F32),
            jax.ShapeDtypeStruct((1, self.channels), F32),
        ]
        padded = jnp.pad(features.astype(BF16), ((0, 48 - EMB), (0, 0)))
        raw = pltpu.VMEM((self.count * BLOCK, self.channels), BF16)
        out_grad, in_grad, sums, bias_grad = vmem_call(
            filter_grad_kernel,
            outs,
            [self.mid, self.back, raw],
            (grad_spec, signal_spec, self.blocked(grad), self.blocked(signal), self.inverse, window)
            + (hidden.astype(BF16), jnp.cos(phase), hidden_pre, padded, filter_out.astype(BF16)),
            "filter_grad",
        )
        return out_grad, in_grad[:EMB], sums.T, bias_grad[0]


class PlainMixer:
    def __init__(self, length, channels, devices, tables):
        self.length = length
        self.devices = devices
        self.channels = channels
        full = 2 * length
        p = 2
        while p * p * 2 <= full and full % (p * 2) == 0:
            p = p * 2
        q = full // p
        self.p, self.q = p, q
        ip, iq = jnp.arange(p, dtype=jnp.int32), jnp.arange(q, dtype=jnp.int32)
        tp = 2.0 * math.pi * (ip[:, None] * ip[None, :] % p).astype(F32) / p
        tq = 2.0 * math.pi * (iq[:, None] * iq[None, :] % q).astype(F32) / q
        tt = 2.0 * math.pi * (ip[:, None] * iq[None, :] % full).astype(F32) / full
        self.cp, self.sp, self.cq, self.sq = jnp.cos(tp), jnp.sin(tp), jnp.cos(tq), jnp.sin(tq)
        self.ct, self.st = jnp.cos(tt), jnp.sin(tt)

    def spectrum(self, signal):
        half = self.p // 2
        x = signal.astype(F32).T.reshape(self.channels, half, self.q)
        ein = functools.partial(jnp.einsum, precision=HIGH)
        re = ein("kn,cnq->ckq", self.cp[:, :half], x)
        im = -ein("kn,cnq->ckq", self.sp[:, :half], x)
        re, im = re * self.ct + im * self.st, im * self.ct - re * self.st
        return (
            ein("ckn,nm->ckm", re, self.cq) + ein("ckn,nm->ckm", im, self.sq),
            ein("ckn,nm->ckm", im, self.cq) - ein("ckn,nm->ckm", re, self.sq),
        )

    def back(self, re, im):
        half = self.p // 2
        ein = functools.partial(jnp.einsum, precision=HIGH)
        br = ein("ckm,nm->ckn", re, self.cq) - ein("ckm,nm->ckn", im, self.sq)
        bi = ein("ckm,nm->ckn", im, self.cq) + ein("ckm,nm->ckn", re, self.sq)
        br, bi = br * self.ct - bi * self.st, bi * self.ct + br * self.st
        out = ein("nk,ckq->cnq", self.cp[:half], br) - ein("nk,ckq->cnq", self.sp[:half], bi)
        return (out.reshape(self.channels, self.length) / (2 * self.length)).T

    def convolve(self, signal, kernel_spec, bias, conjugate, extra):
        a_re, a_im = self.spectrum(signal)
        b_re, b_im = kernel_spec
        if conjugate:
            b_im = -b_im
        out = self.back(a_re * b_re - a_im * b_im, a_re * b_im + a_im * b_re)
        out = out + signal.astype(F32) * bias[None, :]
        out = jnp.pad(out.astype(BF16), ((0, extra), (0, 0)))
        rows = self.length // self.devices
        parts = [out[j * rows : (j + 1) * rows + extra] for j in range(self.devices)]
        return jnp.stack(parts), (a_re, a_im)

    def filter_grad(self, grad_spec, signal_spec, grad, signal, filt):
        features, hidden_pre, phase, hidden, window, filter_out = filt
        a_re, a_im = grad_spec
        b_re, b_im = signal_spec
        raw = self.back(a_re * b_re + a_im * b_im, a_im * b_re - a_re * b_im) * window
        out_grad = jnp.einsum("hn,nc->hc", hidden, raw, precision=HIGH)
        turned = jnp.einsum("nc,hc->hn", raw, filter_out, precision=HIGH) * jnp.cos(phase)
        in_grad = jnp.einsum("en,hn->eh", features, turned, precision=HIGH)
        sums = jnp.stack([jnp.sum(turned * hidden_pre, axis=1), jnp.sum(turned, axis=1)])
        return out_grad, in_grad, sums, jnp.sum(grad.astype(F32) * signal.astype(F32), axis=0)


def position_features(length):
    steps = jnp.arange(length, dtype=F32)
    scaled = steps / (length - 1)
    angles = 2.0 * math.pi * steps / length
    bands = (EMB - 1) // 2
    freqs = 0.0001 + jnp.arange(bands, dtype=F32) * (bands - 1 - 0.0001) / (bands - 1)
    phase = freqs[:, None] * angles[None, :]
    return jnp.concatenate([scaled[None, :], jnp.cos(phase), -jnp.sin(phase)], axis=0)


def swap(value, axis, bit):
    size = lax.axis_size(axis)
    return lax.ppermute(value, axis, [(i, i ^ bit) for i in range(size)])


def pick(value, index, axis):
    return lax.dynamic_index_in_dim(value, index, axis, keepdims=False)


def add(left, right):
    return (left.astype(F32) + right.astype(F32)).astype(BF16)


def seq_bits():
    bit, bits = 1, []
    while bit < lax.axis_size("seq"):
        bits.append(bit)
        bit *= 2
    return bits


def block_order(bits):
    order = [0]
    for bit in reversed(bits):
        order = [r ^ bit for r in order] + order
    return jnp.bitwise_xor(lax.axis_index("seq"), jnp.array(order, jnp.int32))


def chip_units(right, unit, which):
    per = right.shape[0] * right.shape[2] // (4 * unit)
    me = lax.axis_index("dp")
    return jnp.concatenate([jnp.bitwise_xor(me, w) * per + jnp.arange(per, dtype=jnp.int32) for w in which])


def halve(kept, got):
    half = kept.shape[0] // 2
    return add(kept[:half], got[:half]), add(kept[half:], got[half:])


def last(kept, got):
    return (kept.astype(F32) + got.astype(F32))[0]


def tie(*values):
    return lax.optimization_barrier(values)


def pack(parts):
    flat = jnp.concatenate([p.reshape(-1) for p in parts])
    short = -flat.shape[0] % 1024
    return jnp.pad(flat, (0, short)).reshape(-1, 128)


def unpack(packed, like):
    flat = packed.reshape(-1)
    out, place = [], 0
    for p in like:
        out.append(flat[place : place + p.size].reshape(p.shape))
        place += p.size
    return out


def back_act_kernel(dy, down, out, dy_sum):
    out[...] = mxu_nt(dy[...], down[...]).astype(BF16)
    @pl.when(pl.program_id(0) == 0)
    def _():
        acc = rows_loop(dy.shape[0], 16, lambda r, c: c + fold8(dy[r, :].astype(F32)))(jnp.zeros((8, dy.shape[1]), F32))
        dy_sum[...] = jnp.sum(acc, axis=0, keepdims=True)

def back_act(dy, down, block=512):
    rows, width = dy.shape
    ff = down.shape[0]
    return pl.pallas_call(
        back_act_kernel, grid=(ff // block,),
        in_specs=[pl.BlockSpec((rows, width), lambda f: (0, 0)), pl.BlockSpec((block, width), lambda f: (f, 0))],
        out_specs=[pl.BlockSpec((rows, block), lambda f: (0, f)), pl.BlockSpec((1, width), lambda f: (0, 0))],
        out_shape=[jax.ShapeDtypeStruct((rows, ff), BF16), jax.ShapeDtypeStruct((1, width), F32)],
        cost_estimate=cost(2 * rows * width * ff, 13 << 20),
        compiler_params=pltpu.CompilerParams(vmem_limit_bytes=GRANT), name="back_act")(dy, down)

def block_out_kernel(act, down, resid, bias, out, acc):
    f = pl.program_id(0)
    part = mxu(act[...], down[...])
    @pl.when(f == 0)
    def _():
        acc[...] = part + bias[...]
    @pl.when((f > 0) & (f < pl.num_programs(0) - 1))
    def _():
        acc[...] += part
    @pl.when(f == pl.num_programs(0) - 1)
    def _():
        out[...] = (acc[...] + part + resid[...].astype(F32)).astype(BF16)

def block_out(act, down, resid, bias, block=1024):
    rows, ff = act.shape
    width = down.shape[1]
    return pl.pallas_call(
        block_out_kernel, grid=(ff // block,),
        in_specs=[pl.BlockSpec((rows, block), lambda f: (0, f)), pl.BlockSpec((block, width), lambda f: (f, 0)),
                  pl.BlockSpec((rows, width), lambda f: (0, 0)), pl.BlockSpec((1, width), lambda f: (0, 0))],
        out_specs=pl.BlockSpec((rows, width), lambda f: (0, 0)),
        out_shape=jax.ShapeDtypeStruct((rows, width), BF16),
        scratch_shapes=[pltpu.VMEM((rows, width), F32)],
        cost_estimate=cost(2 * rows * width * ff, 15 << 20),
        compiler_params=pltpu.CompilerParams(vmem_limit_bytes=GRANT), name="block_out")(act, down, resid, bias)

C0 = math.sqrt(2.0 / math.pi)
C1 = C0 * 0.044715

def middle_kernel(conv, gate, x, dy, ga, wout, bout, gain, bias, up, up_bias,
                  act, gup, gup_sum, resid, normed, mixed, gattn, gconv, ggate, sums,
                  d2, normal, scale):
    f = pl.program_id(0)
    last = pl.num_programs(0) - 1
    rows, width = x.shape
    nb = width // LANES

    @pl.when((f == 0))
    def _():
        def mix(r, c):
            for j in range(nb):
                lanes = slice(j * LANES, (j + 1) * LANES)
                mixed[r, lanes] = (conv[j, r, :].astype(F32) * gate[r, lanes].astype(F32)).astype(BF16)
            return c
        rows_loop(rows, CHUNK, mix)(0)
        for h in range(2):
            half = slice(h * rows // 2, (h + 1) * rows // 2)
            d2[half, :] = mxu(mixed[half, :], wout[...])

        def norm(r, c):
            v = x[r, :].astype(F32) + d2[r, :] + bout[...]
            resid[r, :] = v.astype(BF16)
            mean = jnp.mean(v, axis=-1, keepdims=True)
            v = v - mean
            s = lax.rsqrt(jnp.mean(v * v, axis=-1, keepdims=True) + EPSILON)
            n = v * s
            scale[r, :] = s
            normal[r, :] = n
            normed[r, :] = (n * gain[...] + bias[...]).astype(BF16)
            return c
        rows_loop(rows, CHUNK, norm)(0)

    total = jnp.zeros((8, up.shape[1]), F32)
    pieces = 1
    for h in range(pieces):
        part = slice(h * rows // pieces, (h + 1) * rows // pieces)
        v = mxu(normed[part, :], up[...]) + up_bias[...]
        v2 = v * v
        t = jnp.tanh(v * (C0 + C1 * v2))
        half = 0.5 + 0.5 * t
        act[part, :] = (v * half).astype(BF16)
        slope = half + (0.5 * v) * (1.0 - t * t) * (C0 + (3.0 * C1) * v2)
        g = (ga[part, :].astype(F32) * slope).astype(BF16)
        gup[part, :] = g
        total += fold8(g.astype(F32))
        back = mxu_nt(g, up[...])
        @pl.when(f == 0)
        def _():
            d2[part, :] = back
        @pl.when(f > 0)
        def _():
            d2[part, :] += back
    gup_sum[...] = jnp.sum(total, axis=0, keepdims=True)

    @pl.when((f == last))
    def _():
        def norm_back(r, carry):
            a, b, o = carry
            d, n = d2[r, :], normal[r, :]
            a += fold8(d * n)
            b += fold8(d)
            e = d * gain[...]
            m1 = jnp.mean(e, axis=-1, keepdims=True)
            m2 = jnp.mean(e * n, axis=-1, keepdims=True)
            g = dy[r, :].astype(F32) + (e - m1 - n * m2) * scale[r, :]
            low = g.astype(BF16)
            gattn[r, :] = low
            o += fold8(low.astype(F32))
            return a, b, o
        zero = jnp.zeros((8, width), F32)
        a, b, o = rows_loop(rows, CHUNK, norm_back)((zero, zero, zero))
        sums[0:1, :] = jnp.sum(a, axis=0, keepdims=True)
        sums[1:2, :] = jnp.sum(b, axis=0, keepdims=True)
        sums[2:3, :] = jnp.sum(o, axis=0, keepdims=True)
        for h in range(2):
            half = slice(h * rows // 2, (h + 1) * rows // 2)
            d2[half, :] = mxu_nt(gattn[half, :], wout[...])
        def out(r, c):
            for j in range(nb):
                lanes = slice(j * LANES, (j + 1) * LANES)
                g = d2[r, lanes]
                gconv[j, r, :] = (g * gate[r, lanes].astype(F32)).astype(BF16)
                ggate[r, lanes] = (g * conv[j, r, :].astype(F32)).astype(BF16)
            return c
        rows_loop(rows, CHUNK, out)(0)

def middle(conv, gate, x, dy, ga, wout, bout, gain, bias, up, up_bias, block=512):
    rows, width = x.shape
    ff = up.shape[1]
    nb = width // LANES
    whole = lambda *s: pl.BlockSpec(s, lambda f: (0,) * len(s))
    flat = whole(rows, width)
    row = whole(1, width)
    cols = pl.BlockSpec((rows, block), lambda f: (0, f))
    bar = pl.BlockSpec((1, block), lambda f: (0, f))
    sd = jax.ShapeDtypeStruct
    return pl.pallas_call(
        middle_kernel, grid=(ff // block,),
        in_specs=[whole(nb, rows, LANES), flat, flat, flat, cols, whole(width, width), row, row, row,
                  pl.BlockSpec((width, block), lambda f: (0, f)), bar],
        out_specs=[cols, cols, bar, flat, flat, flat, flat, whole(nb, rows, LANES), flat, whole(3, width)],
        out_shape=[sd((rows, ff), BF16), sd((rows, ff), BF16), sd((1, ff), F32), sd((rows, width), BF16),
                   sd((rows, width), BF16), sd((rows, width), BF16), sd((rows, width), BF16),
                   sd((nb, rows, LANES), BF16), sd((rows, width), BF16), sd((3, width), F32)],
        scratch_shapes=[pltpu.VMEM((rows, width), F32), pltpu.VMEM((rows, width), F32), pltpu.VMEM((rows, 1), F32)],
        cost_estimate=cost(4 * rows * width * (ff + width), 34 << 20),
        compiler_params=pltpu.CompilerParams(vmem_limit_bytes=GRANT), name="middle")(
            conv, gate, x, dy, ga, wout, bout, gain, bias, up, up_bias)

PRE = 16

def enter_kernel(first, x, before, gain, bias, w0, w1, w2, b0, b1, b2, taps, inner, gate, proj, normed_out, normed, shifted):
    rows, width = x.shape
    def norm(src, base):
        def body(r, c):
            v = src[r, :].astype(F32)
            v = v - jnp.mean(v, axis=-1, keepdims=True)
            s = lax.rsqrt(jnp.mean(v * v, axis=-1, keepdims=True) + EPSILON)
            normed[pl.ds(r.start + base, r.size), :] = (v * s * gain[...] + bias[...]).astype(BF16)
            return c
        return body
    @pl.when(pl.program_id(0) == 0)
    def _():
        rows_loop(PRE, 16, norm(before, 0))(0)
        rows_loop(rows, CHUNK, norm(x, PRE))(0)
        normed_out[...] = normed[PRE:, :]
    cb = w0.shape[1]
    short = []
    keep = jnp.where(first[0] == 0, 0.0, 1.0)
    for k, (w, b) in enumerate(((w0, b0), (w1, b1), (w2, b2))):
        p = (mxu(normed[...], w[...]) + b[...]).astype(BF16)
        proj[k, PRE:, :] = p[PRE:]
        proj[k, :PRE, :] = (p[:PRE].astype(F32) * keep).astype(BF16)
        shifted[k, PRE:, :] = p[PRE:].astype(F32)
        shifted[k, :PRE, :] = p[:PRE].astype(F32) * keep
    def gates(r, c):
        s = []
        for k in range(3):
            p = shifted[k, pl.ds(r.start + (PRE - 8), r.size + 8), :]
            v = taps[9 + k : 10 + k, :] + sum(
                taps[3 * j + k : 3 * j + k + 1, :] * p[6 + j : 6 + j + r.size] for j in range(3))
            s.append(v)
        gate[r, :] = s[0].astype(BF16)
        v = (s[1] * s[2]).astype(BF16)
        for j in range(cb // LANES):
            inner[j, r, :] = v[:, j * LANES : (j + 1) * LANES]
        return c
    rows_loop(rows, CHUNK, gates)(0)

def enter(first, x, before, gain, bias, weight, in_bias, taps, block=256):
    rows, width = x.shape
    nb = width // LANES
    steps = width // block
    whole = lambda *s: pl.BlockSpec(s, lambda c: (0,) * len(s))
    wspec = lambda k: pl.BlockSpec((width, block), lambda c, k=k: (0, k * steps + c))
    bspec = lambda k: pl.BlockSpec((1, block), lambda c, k=k: (0, k * steps + c))
    sd = jax.ShapeDtypeStruct
    return pl.pallas_call(
        enter_kernel, grid=(steps,),
        in_specs=[pl.BlockSpec(memory_space=pltpu.SMEM), whole(rows, width), whole(PRE, width), whole(1, width), whole(1, width),
                  wspec(0), wspec(1), wspec(2), bspec(0), bspec(1), bspec(2), pl.BlockSpec((12, block), lambda c: (0, c))],
        out_specs=[pl.BlockSpec((block // LANES, rows, LANES), lambda c: (c, 0, 0)), pl.BlockSpec((rows, block), lambda c: (0, c)),
                   pl.BlockSpec((3, PRE + rows, block), lambda c: (0, 0, c)), whole(rows, width)],
        out_shape=[sd((nb, rows, LANES), BF16), sd((rows, width), BF16), sd((3, PRE + rows, width), BF16), sd((rows, width), BF16)],
        scratch_shapes=[pltpu.VMEM((PRE + rows, width), BF16), pltpu.VMEM((3, PRE + rows, block), F32)],
        cost_estimate=cost(6 * rows * width * width, 14 << 20),
        compiler_params=pltpu.CompilerParams(vmem_limit_bytes=GRANT), name="enter")(
            first, x, before, gain, bias, weight, weight, weight, in_bias, in_bias, in_bias, taps)

POST = 16

def leave_kernel(ginner, ggate, ggate_after, proj, proj_after, taps, gproj, sums, pbuf, gbuf):
    rows = ggate.shape[0]
    cb = ggate.shape[1]
    for k in range(3):
        pbuf[k, : PRE + rows, :] = proj[k].astype(F32)
        pbuf[k, PRE + rows :, :] = proj_after[k].astype(F32)
    tap = lambda j, k: taps[3 * j + k : 3 * j + k + 1, :]

    def lags(k, start, size):
        p = pbuf[k, pl.ds(start + (PRE - 8), size + 8), :]
        return [p[6 + j : 6 + j + size] for j in range(3)]

    def grads(start, size, g0):
        gi = jnp.concatenate([ginner[j, pl.ds(start, size), :] for j in range(cb // LANES)], axis=1).astype(F32)
        p1 = lags(1, start, size)
        p2 = lags(2, start, size)
        s1 = taps[10:11, :] + sum(tap(j, 1) * p1[j] for j in range(3))
        s2 = taps[11:12, :] + sum(tap(j, 2) * p2[j] for j in range(3))
        return (g0, gi * s2, gi * s1), p1, p2

    def first(r, carry):
        g, p1, p2 = grads(r.start, r.size, ggate[r, :].astype(F32))
        p0 = lags(0, r.start, r.size)
        out = []
        for k in range(3):
            gbuf[k, r, :] = g[k]
        for j in range(3):
            for k, p in enumerate((p0, p1, p2)):
                out.append(carry[3 * j + k] + fold8(g[k] * p[j]))
        for k in range(3):
            out.append(carry[9 + k] + fold8(g[k]))
        return tuple(out)

    acc = rows_loop(rows, CHUNK, first)(tuple(jnp.zeros((8, cb), F32) for _ in range(12)))
    for i in range(12):
        sums[i : i + 1, :] = jnp.sum(acc[i], axis=0, keepdims=True)
    g, _, _ = grads(rows, POST, ggate_after[...].astype(F32))
    for k in range(3):
        gbuf[k, rows:, :] = g[k]

    def second(r, carry):
        out = []
        for k in range(3):
            g = gbuf[k, pl.ds(r.start, r.size + 8), :]
            v = sum(tap(j, k) * g[2 - j : 2 - j + r.size] for j in range(3)).astype(BF16)
            gproj[k, 0, r, :] = v
            out.append(carry[k] + fold8(v.astype(F32)))
        return tuple(out)

    acc = rows_loop(rows, CHUNK, second)(tuple(jnp.zeros((8, cb), F32) for _ in range(3)))
    for i in range(3):
        sums[12 + i : 13 + i, :] = jnp.sum(acc[i], axis=0, keepdims=True)
    sums[15:16, :] = jnp.zeros((1, cb), F32)

def leave(ginner, ggate, ggate_after, proj, proj_after, taps, block=256):
    rows, width = ggate.shape
    steps = width // block
    sd = jax.ShapeDtypeStruct
    return pl.pallas_call(
        leave_kernel, grid=(steps,),
        in_specs=[pl.BlockSpec((block // LANES, rows + POST, LANES), lambda c: (c, 0, 0)),
                  pl.BlockSpec((rows, block), lambda c: (0, c)), pl.BlockSpec((POST, block), lambda c: (0, c)),
                  pl.BlockSpec((3, PRE + rows, block), lambda c: (0, 0, c)), pl.BlockSpec((3, POST, block), lambda c: (0, 0, c)),
                  pl.BlockSpec((12, block), lambda c: (0, c))],
        out_specs=[pl.BlockSpec((3, 1, rows, block), lambda c: (0, c, 0, 0)), pl.BlockSpec((16, block), lambda c: (0, c))],
        out_shape=[sd((3, steps, rows, block), BF16), sd((16, width), F32)],
        scratch_shapes=[pltpu.VMEM((3, PRE + rows + POST, block), F32), pltpu.VMEM((3, rows + POST, block), F32)],
        cost_estimate=cost(60 * rows * width, 9 << 20),
        compiler_params=pltpu.CompilerParams(vmem_limit_bytes=GRANT), name="leave")(ginner, ggate, ggate_after, proj, proj_after, taps)

def tokens_kernel(gproj, weight, x, gres, gain, out, sums, acc):
    k = pl.program_id(0)
    rows, width = x.shape
    unit = gproj.shape[3]
    part = sum(mxu_nt(gproj[0, j], weight[:, j * unit : (j + 1) * unit]) for j in range(gproj.shape[1]))
    @pl.when(k == 0)
    def _():
        acc[...] = part
    @pl.when(k > 0)
    def _():
        acc[...] += part
    @pl.when(k == pl.num_programs(0) - 1)
    def _():
        def body(r, carry):
            a, b = carry
            v = x[r, :].astype(F32)
            v = v - jnp.mean(v, axis=-1, keepdims=True)
            s = lax.rsqrt(jnp.mean(v * v, axis=-1, keepdims=True) + EPSILON)
            n = v * s
            d = acc[r, :]
            a += fold8(d * n)
            b += fold8(d)
            e = d * gain[...]
            m1 = jnp.mean(e, axis=-1, keepdims=True)
            m2 = jnp.mean(e * n, axis=-1, keepdims=True)
            out[r, :] = gres[r, :].astype(F32) + (e - m1 - n * m2) * s
            return a, b
        zero = jnp.zeros((8, width), F32)
        a, b = rows_loop(rows, CHUNK, body)((zero, zero))
        sums[0:1, :] = jnp.sum(a, axis=0, keepdims=True)
        sums[1:2, :] = jnp.sum(b, axis=0, keepdims=True)

def tokens_back(gproj, weight, x, gres, gain):
    rows, width = x.shape
    whole = lambda *s: pl.BlockSpec(s, lambda k: (0,) * len(s))
    sd = jax.ShapeDtypeStruct
    return pl.pallas_call(
        tokens_kernel, grid=(3,),
        in_specs=[pl.BlockSpec((1,) + gproj.shape[1:], lambda k: (k, 0, 0, 0)), pl.BlockSpec((width, width), lambda k: (0, k)),
                  whole(rows, width), whole(rows, width), whole(1, width)],
        out_specs=[whole(rows, width), whole(2, width)],
        out_shape=[sd((rows, width), F32), sd((2, width), F32)],
        scratch_shapes=[pltpu.VMEM((rows, width), F32)],
        cost_estimate=cost(6 * rows * width * width, 14 << 20),
        compiler_params=pltpu.CompilerParams(vmem_limit_bytes=GRANT), name="tokens_back")(gproj, weight, x, gres, gain)


def wgrad_kernel(row_order, units, *refs, sides, lefts, rights, held, mode):
    acc = None
    for side in range(sides):
        refs_left, refs = refs[:lefts], refs[lefts:]
        left = jnp.concatenate([r[...] for r in refs_left], axis=1)
        refs_right, refs = refs[:rights], refs[rights:]
        right = jnp.concatenate([r[0] for r in refs_right], axis=1)
        part = mxu_tn(left, right)
        acc = part if acc is None else acc + part
    outs = refs[held:]
    count, height, _ = outs[0].shape
    width = acc.shape[1] // 2
    value = acc.reshape(count, height, acc.shape[1]).astype(BF16)
    if mode == "x":
        outs[0][...] = value[..., :width]
        outs[1][...] = value[..., width:]
    if mode == "y":
        early = pl.program_id(0) < pl.num_programs(0) // 2

        @pl.when(early)
        def _():
            place = 0
            for piece in outs[:-1]:
                piece[...] = value[..., place : place + piece.shape[2]]
                place += piece.shape[2]

        @pl.when(jnp.logical_not(early))
        def _():
            outs[-1][...] = value


def wgrad(left, right, row_order, units, unit, mode, each, held=(), tall=None, start=0, pieces=(1,)):
    rows, m = left[0].shape
    sides, blocks, count = len(left), row_order.shape[0], units[0].shape[0]
    height = m // blocks
    tall = tall or height
    at = start // height
    wide = count * unit
    half = wide // 2
    if height % LANES:
        left = [v.reshape(rows, blocks, height)[:, row_order].reshape(rows, m) for v in left]
        each = max(each, LANES // height)
        left_specs = [pl.BlockSpec((rows, each * height), lambda i, r, u: (0, i))]
    else:
        left_specs = [pl.BlockSpec((rows, height), lambda i, r, u, q=q: (0, r[i * each + q])) for q in range(each)]
    lefts, steps = len(left_specs), blocks // each
    in_specs, args = [], []
    for side in range(sides):
        per, base = right[side].shape[2] // unit, side * count
        in_specs += left_specs + [
            pl.BlockSpec((1, rows, unit), lambda i, r, u, j=base + j, per=per: (u[j] // per, 0, u[j] % per))
            for j in range(count)
        ]
        args += [left[side]] * lefts + [right[side]] * count
    aliases = {2 + len(args) + i: i for i in range(len(held))}
    in_specs += [pl.BlockSpec(memory_space=pl.ANY)] * len(held)
    args += list(held)
    full = lambda w: ((blocks, tall, w), pl.BlockSpec((each, height, w), lambda i, r, u: (i, at, 0)))
    first = ((blocks // 2, tall, wide), lambda i: jnp.minimum(i, steps // 2 - 1))
    second = ((blocks // 2, tall, wide), lambda i: jnp.maximum(i - steps // 2, 0))
    part = lambda s, w: ((s[0][0], tall, w), pl.BlockSpec((each, height, w), lambda i, r, u: (s[1](i), at, 0)))
    outs = {
        "x": [full(half)] * 2,
        "y": [part(first, wide * p // sum(pieces)) for p in pieces] + [part(second, wide)],
    }[mode]
    return pl.pallas_call(
        functools.partial(wgrad_kernel, sides=sides, lefts=lefts, rights=count, held=len(held), mode=mode),
        grid_spec=pltpu.PrefetchScalarGridSpec(
            num_scalar_prefetch=2, grid=(steps,), in_specs=in_specs, out_specs=[o[1] for o in outs]
        ),
        out_shape=[jax.ShapeDtypeStruct(o[0], BF16) for o in outs],
        input_output_aliases=aliases,
        cost_estimate=cost(2 * sides * rows * m * wide, 2 * sides * (rows * m + rows * wide) + 4 * m * wide),
        compiler_params=pltpu.CompilerParams(vmem_limit_bytes=GRANT),
        name="wgrad",
    )(row_order, jnp.concatenate(units), *args)


def on_device(
    tokens,
    cotangent,
    norm1_gain,
    norm1_bias,
    in_weight,
    in_bias,
    short_weight,
    short_bias,
    filter_in,
    filter_in_bias,
    sine_freq,
    filter_out,
    decay_rates,
    filter_bias,
    out_weight,
    out_bias,
    norm2_gain,
    norm2_bias,
    up_weight,
    up_bias,
    down_weight,
    down_bias,
):
    width = in_weight.shape[0]
    ff = up_weight.shape[1]
    rows = tokens.shape[1]
    seq = lax.axis_size("seq")
    me = lax.axis_index("seq")
    length = rows * seq
    chans = width // seq
    down_shift = [(i + 1, i) for i in range(seq - 1)]

    x, dy = tokens[0], cotangent[0]
    edge = 2 * width // chans
    mine = jnp.concatenate(
        [short_weight.reshape(9, chans), short_bias, x[rows - 2 :].astype(F32).reshape(edge, chans)], axis=0
    )
    got = lax.all_to_all(
        jnp.broadcast_to(mine[None], (seq, 12 + edge, chans)), "seq", split_axis=0, concat_axis=0, tiled=True
    ).reshape(seq, 12 + edge, chans)
    all_taps = got[:, :12].transpose(1, 0, 2).reshape(12, width)
    before = pick(got, jnp.maximum(me - 1, 0), 0)[12:].reshape(2, width)
    before = jnp.concatenate([jnp.zeros((PRE - 2, width), BF16), before.astype(BF16)], axis=0)

    row = lambda v: v[None, :]
    first = me.reshape(1).astype(jnp.int32)
    fast = length // BLOCK <= 64
    tables = make_tables(length) if fast else None
    before, all_taps, tables = lax.optimization_barrier((before, all_taps, tables))
    inner, gate, proj, normed = enter(
        first, x, before, row(norm1_gain), row(norm1_bias), in_weight, row(in_bias), all_taps
    )
    proj_after = lax.ppermute(proj[:, PRE : PRE + POST], "seq", down_shift)

    def to_channels(value):
        if chans != LANES:
            value = value.transpose(1, 0, 2).reshape(rows, seq, chans).transpose(1, 0, 2)
        got = lax.all_to_all(value, "seq", split_axis=0, concat_axis=0, tiled=True)
        return got.reshape(length, chans)

    def to_tokens(value):
        got = lax.all_to_all(value, "seq", split_axis=0, concat_axis=0, tiled=True)
        if chans != LANES:
            got = got.transpose(1, 0, 2).reshape(got.shape[1], width // LANES, LANES).transpose(1, 0, 2)
        return got

    inner_chan = to_channels(inner)

    mixer = (FastMixer if fast else PlainMixer)(length, chans, seq, tables)
    features = position_features(length)
    hidden_pre = jnp.dot(filter_in.T, features, precision=HIGH) + filter_in_bias[:, None]
    phase = sine_freq[:, None] * hidden_pre
    hidden = jnp.sin(phase)
    window = jnp.exp(-features[0][:, None] * decay_rates[None, :])
    kernel = jnp.einsum("hn,hc->nc", hidden, filter_out, precision=HIGH) * window
    kernel_spec = mixer.spectrum(kernel)

    conv_chan, inner_spec = mixer.convolve(inner_chan, kernel_spec, filter_bias, False, 0)
    normed_x = swap(normed, "dp", 2)
    conv_chan, proj_after, normed_x = tie(conv_chan, proj_after, normed_x)
    normed_all = [normed, swap(normed, "dp", 1), normed_x, swap(normed_x, "dp", 1)]
    conv = to_tokens(conv_chan)
    dy_other = swap(dy, "dp", 1)
    grad_act, dy_sum = back_act(dy, down_weight)
    conv, dy_other, normed_all = tie(conv, dy_other, normed_all)
    act, gup, gup_sum, resid, normed2, mixed, grad_attn, grad_conv, grad_gate, mid_sums = middle(
        conv, gate, x, dy, grad_act, out_weight, row(out_bias), row(norm2_gain), row(norm2_bias), up_weight, row(up_bias)
    )
    grad_chan = to_channels(grad_conv)
    gate_after = lax.ppermute(grad_gate[:POST], "seq", down_shift)

    bits = seq_bits()
    order = block_order(bits)
    up_bits = [bits[1], bits[0]] + bits[2:]
    up_order = block_order(up_bits)
    unit = width // 4
    tall = (ff + width) // seq
    wide = ff // seq

    pair = lambda value: (value, swap(value, "dp", 1))
    near_units, near_up = chip_units(dy[None], unit, (2, 0)), chip_units(gup[None], ff // 4, (2, 0))
    dy_pair, act_pair = (dy[None], dy_other[None]), pair(act)
    mixed_pair, attn_pair = pair(mixed), pair(grad_attn[None])
    gup_pair, normed2_pair = pair(gup[None]), pair(normed2)
    parts = wgrad(act_pair, dy_pair, order, [near_units] * 2, unit, "x", 2, tall=tall)
    each = 8 if seq == 8 else 4
    tall_send, tall_kept = wgrad(
        mixed_pair, attn_pair, order, [near_units] * 2, unit, "x", each, held=parts, tall=tall, start=wide
    )
    tall_got = swap(tall_send, "dp", 2)
    grad_chan, tall_kept = tie(grad_chan, tall_kept)
    grad_inner_chan, grad_spec = mixer.convolve(grad_chan, kernel_spec, filter_bias, True, POST)
    gup_pair, normed2_pair, grad_inner_chan, gate_after = tie(gup_pair, normed2_pair, grad_inner_chan, gate_after)
    grad_inner = to_tokens(grad_inner_chan)
    *up_sends, up_kept = wgrad(normed2_pair, gup_pair, up_order, [near_up] * 2, ff // 4, "y", 4, pieces=(1, 2, 1))

    grad_filter_out, grad_filter_in, filter_sums, grad_filter_bias = mixer.filter_grad(
        grad_spec, inner_spec, grad_chan, inner_chan, (features, hidden_pre, phase, hidden, window, filter_out)
    )
    grad_freq = filter_sums[0]
    grad_filter_in_bias = filter_sums[1] * sine_freq
    grad_filter_in = grad_filter_in * sine_freq[None, :]

    grad_inner, grad_filter_out, up_sends = tie(grad_inner, grad_filter_out, up_sends)
    up_gots = [swap(up_sends[0], "seq", up_bits[0])]
    grad_proj, leave_sums = leave(grad_inner, grad_gate, gate_after, proj, proj_after, all_taps)
    grad_proj, tall_got, up_gots[0] = tie(grad_proj, tall_got, up_gots[0])
    tall_send, tall_kept = halve(tall_kept, tall_got)
    proj_units = grad_proj.reshape((-1,) + grad_proj.shape[2:])
    proj_all = lax.all_to_all(proj_units, "dp", split_axis=0, concat_axis=0, tiled=True)
    up_gots.append(swap(up_sends[1], "seq", up_bits[0]))
    grad_proj, tall_send = tie(grad_proj, tall_send)
    tall_got = swap(tall_send, "seq", bits[0])
    grad_tokens, token_sums = tokens_back(grad_proj, in_weight, x, grad_attn, row(norm1_gain))

    shared = (token_sums, leave_sums, mid_sums, gup_sum, dy_sum, grad_filter_in, grad_filter_in_bias, grad_freq)
    channel = (grad_filter_out, grad_filter_bias)
    packed, extra = pack(shared), pack(channel)
    rows_shared = packed.shape[0]
    packed = jnp.concatenate([packed, extra], axis=0)
    packed = packed + swap(packed, "dp", 1)
    packed, up_gots[1] = tie(packed, up_gots[1])
    small = swap(packed, "dp", 2)
    up_gots.append(swap(up_sends[2], "seq", up_bits[0]))
    cut = ff // 4
    part = up_gots[1].shape[2] // 2
    up_send = add(up_kept[..., :cut], jnp.concatenate([up_gots[0], up_gots[1][..., :part]], axis=2))
    up_send, act = tie(up_send, act)
    up_got = swap(up_send, "dp", 2)
    block_output = block_out(act, down_weight, resid, row(down_bias))
    block_output, proj_all = tie(block_output, proj_all)
    dp_me = lax.axis_index("dp")
    share = proj_units.shape[0] // 4
    ahead = jnp.arange(share, dtype=jnp.int32)
    in_units = [jnp.bitwise_xor(dp_me, w) * share + ahead for w in range(4)]
    in_send, in_kept = wgrad(normed_all, [proj_all] * 4, order, in_units, proj_units.shape[2], "y", 4)

    in_send, tall_got, up_gots = tie(in_send, tall_got, up_gots)
    in_got = swap(in_send, "seq", bits[0])
    tall_send, tall_kept = halve(tall_kept, tall_got)
    tall_got = swap(tall_send, "seq", bits[1])
    up_kept = add(up_kept[..., cut:], jnp.concatenate([up_gots[1][..., part:], up_gots[2]], axis=2))
    up_got, up_kept, tall_send, small = tie(up_got, up_kept, tall_send, small)
    up_send, up_kept = halve(up_kept, up_got)
    up_got = swap(up_send, "seq", up_bits[1])
    packed = packed + small
    packed, extra = packed[:rows_shared], packed[rows_shared:]
    small = swap(packed, "seq", bits[0])

    in_got, tall_got, up_send, small = tie(in_got, tall_got, up_send, small)
    in_send, in_kept = halve(in_kept, in_got)
    in_got = swap(in_send, "seq", bits[1])
    tall_send, tall_kept = halve(tall_kept, tall_got)
    tall_got = swap(tall_send, "seq", bits[2])
    packed = packed + small
    small = swap(packed, "seq", bits[1])

    for i in range(2, len(bits)):
        in_send, up_got = tie(in_send, up_got)
        up_send, up_kept = halve(up_kept, up_got)
        up_got = swap(up_send, "seq", up_bits[i])
        in_got, tall_got, up_send, small = tie(in_got, tall_got, up_send, small)
        if i > 2:
            tall_send, tall_kept = halve(tall_kept, tall_got)
            tall_got = swap(tall_send, "seq", bits[i])
        in_send, in_kept = halve(in_kept, in_got)
        in_got = swap(in_send, "seq", bits[i])
        packed = packed + small
        small = swap(packed, "seq", bits[i])
    up_got, in_got = tie(up_got, in_got)
    grad_in, grad_up, both = last(in_kept, in_got), last(up_kept, up_got), last(tall_kept, tall_got)
    small, grad_in, grad_up = tie(small, grad_in, grad_up)
    packed = packed + small
    grad_down, grad_out_weight = both[:wide], both[wide:]
    channel = unpack(extra, channel)
    shared = unpack(packed, shared)
    token_sums, leave_sums, mid_sums, gup_sum, dy_sum = shared[:5]
    own = lax.dynamic_slice_in_dim(leave_sums[:12], me * chans, chans, 1)
    return (
        block_output[None],
        grad_tokens[None],
        token_sums[0],
        token_sums[1],
        grad_in,
        leave_sums[12:15].reshape(-1),
        own[:9].reshape(3, 3, chans),
        own[9:],
        shared[5],
        shared[6],
        shared[7],
        channel[0],
        channel[1],
        grad_out_weight,
        mid_sums[2],
        mid_sums[0],
        mid_sums[1],
        grad_up,
        gup_sum[0],
        grad_down,
        dy_sum[0],
    )


def solution(mesh):
    everywhere, by_token, by_rows = P(), P("dp", "seq", None), P("seq", "dp")
    taps, shift, chan = P(None, None, "seq"), P(None, "seq"), P("seq")
    in_specs = (by_token,) * 2 + (everywhere,) * 4 + (taps, shift) + (everywhere,) * 3
    in_specs += (shift, chan, chan) + (everywhere,) * 8
    out_specs = (by_token, by_token, everywhere, everywhere, by_rows, everywhere, taps, shift)
    out_specs += (everywhere,) * 3 + (shift, chan, by_rows) + (everywhere,) * 3
    out_specs += (by_rows, everywhere, by_rows, everywhere)
    return jax.shard_map(
        on_device, mesh=mesh, in_specs=in_specs, out_specs=out_specs, check_vma=False
    )
```
